32 devices in a mesh: rep: 16 (over z, x, core), shard: 2 (over y).
Axes of the slice: x: 2, y: 2, z: 4, core: 2. Of those that a mesh axis runs over, the one named last changes fastest.
Arguments:
- clips: bfloat16 [64, 1568, 1536], P(('rep', 'shard')), may hold values from -6 to 6
- visible_idx: int32 [64, 157], P(('rep', 'shard')), may hold values from 0 to 1567, as said below
- masked_idx: int32 [64, 1411], P(('rep', 'shard')), may hold values from 0 to 1567
- loss_counts: int32 [64], P(('rep', 'shard')), may hold values from 705 to 1411, as said below
- enc_rows: float32 [768, 6528], P('shard'), may hold values from -0.21875 to 0.21875
- enc_cols: float32 [4608, 768], P('shard'), may hold values from -0.109375 to 0.109375
- dec_rows: float32 [384, 4608], P('shard'), may hold values from -0.3125 to 0.3125
- dec_fc2: float32 [1536, 384], P('shard'), may hold values from -0.15625 to 0.15625
- vectors: float32 [14592], P('shard'), may hold values from 0.25 to 1.75
- m_enc_rows: float32 [768, 6528], P('shard'), may hold values from -1.9073486e-06 to 1.9073486e-06
- m_enc_cols: float32 [4608, 768], P('shard'), may hold values from -1.9073486e-06 to 1.9073486e-06
- m_dec_rows: float32 [384, 4608], P('shard'), may hold values from -1.9073486e-06 to 1.9073486e-06
- m_dec_fc2: float32 [1536, 384], P('shard'), may hold values from -1.9073486e-06 to 1.9073486e-06
- m_vectors: float32 [14592], P('shard'), may hold values from -1.9073486e-06 to 1.9073486e-06
- v_enc_rows: float32 [768, 6528], P('shard'), may hold values from 2.0269753e-14 to 2.0269753e-13
- v_enc_cols: float32 [4608, 768], P('shard'), may hold values from 2.0269753e-14 to 2.0269753e-13
- v_dec_rows: float32 [384, 4608], P('shard'), may hold values from 2.0269753e-14 to 2.0269753e-13
- v_dec_fc2: float32 [1536, 384], P('shard'), may hold values from 2.0269753e-14 to 2.0269753e-13
- v_vectors: float32 [14592], P('shard'), may hold values from 2.0269753e-14 to 2.0269753e-13
Outputs:
- loss: float32 [], replicated
- grad_norm: float32 [], replicated
- next_enc_rows: float32 [768, 6528], P('shard')
- next_enc_cols: float32 [4608, 768], P('shard')
- next_dec_rows: float32 [384, 4608], P('shard')
- next_dec_fc2: float32 [1536, 384], P('shard')
- next_vectors: float32 [14592], P('shard')
- next_m_enc_rows: float32 [768, 6528], P('shard')
- next_m_enc_cols: float32 [4608, 768], P('shard')
- next_m_dec_rows: float32 [384, 4608], P('shard')
- next_m_dec_fc2: float32 [1536, 384], P('shard')
- next_m_vectors: float32 [14592], P('shard')
- next_v_enc_rows: float32 [768, 6528], P('shard')
- next_v_enc_cols: float32 [4608, 768], P('shard')
- next_v_dec_rows: float32 [384, 4608], P('shard')
- next_v_dec_fc2: float32 [1536, 384], P('shard')
- next_v_vectors: float32 [14592], P('shard')
- low_enc_rows: bfloat16 [768, 6528], P('shard')
- low_enc_cols: bfloat16 [4608, 768], P('shard')
- low_dec_rows: bfloat16 [384, 4608], P('shard')
- low_dec_fc2: bfloat16 [1536, 384], P('shard')
- low_vectors: bfloat16 [14592], P('shard')
The draws below stay inside these ranges and needn't reach their ends.
Inputs may be any that keep to these rules, and one draw needn't show every extreme that they name: In each clip, visible_idx and masked_idx are disjoint and together name each of its 1568 tubes once. The loss counts the first loss_counts[c] entries of masked_idx[c].
All inputs are finite; a program needn't handle non-finite values.
Results may differ from the reference program's by a relative error of at most 0.0006.
The reference program's roundings to bfloat16 on the way count: a program that leaves them out, or rounds other values in their place, can miss the bound.
Values may be sent and summed in bfloat16 or wider, within the bound.
No kernel may reach another device: no remote copies, remote signals or barrier semaphores. Data moves between devices by JAX's collectives and lax.ppermute only.
A program may use at most 384 MiB of HBM per device.

```python
import math
import jax
import jax.numpy as jnp
from jax import lax

D = 768
HEADS = 12
FF = 3072
DD = 384
DHEADS = 6
DFF = 1536
PATCH = 1536
VIS = 157
MASKED = 1411
TUBES = 1568
CLIPS = 64
VEC = 14592
PARAMS = 10926336


def tube_order(key):
    base = jax.random.fold_in(key, 7)
    keys = jax.random.split(base, CLIPS)
    return jax.vmap(lambda single: jax.random.permutation(single, TUBES))(keys).astype(jnp.int32)


def draw_visible_idx(key, part):
    return tube_order(key)[:, :VIS]


def draw_masked_idx(key, part):
    return tube_order(key)[:, VIS:]


def draw_loss_counts(key, part):
    counts = jax.random.randint(jax.random.fold_in(key, 11), (CLIPS,), MASKED // 2, MASKED + 1)
    counts = counts.at[0].set(MASKED).at[1].set(MASKED // 2)
    return counts.astype(jnp.int32)


def steps_of(key, extent, shards, least, high):
    def one(axis_at, parts):
        steps = jax.random.uniform(jax.random.fold_in(jax.random.fold_in(key, 6), axis_at), (parts,), jnp.float32, least / len(shards), high / len(shards))
        return jnp.repeat(jnp.exp(steps), extent[axis_at] // parts).reshape((-1,) + (1,) * (len(extent) - axis_at - 1))

    gain = one(*shards[0])
    for cut in shards[1:]:
        gain = gain * one(*cut)
    return gain


def bell_draw(rng, shape, deviation, most, cuts=(), dtype=jnp.bfloat16):
    loudness = steps_of(rng, shape, cuts, -0.22, 0.18) if cuts else 1.0
    values = jax.random.normal(rng, shape, jnp.float32) * deviation * loudness
    return jnp.minimum(jnp.maximum(values, -most), most).astype(dtype)


def setup_inputs(seed: int = 0) -> dict:
    streams_of = jax.random.split(jax.random.key(seed), 20)
    return {
        "clips": bell_draw(streams_of[0], (CLIPS, TUBES, PATCH), 1.0, 6.0, ((0, 32),)),
        "visible_idx": draw_visible_idx(jax.random.fold_in(streams_of[19], 71), 0),
        "masked_idx": draw_masked_idx(jax.random.fold_in(streams_of[19], 71), 0),
        "loss_counts": draw_loss_counts(jax.random.fold_in(streams_of[19], 71), 0),
        "enc_rows": bell_draw(streams_of[4], (D, 4 * D + FF + DD), D ** -0.5, 0.21875, ((0, 2),), jnp.float32),
        "enc_cols": bell_draw(streams_of[5], (PATCH + FF, D), FF ** -0.5, 0.109375, ((0, 2),), jnp.float32),
        "dec_rows": bell_draw(streams_of[6], (DD, 4 * DD + DFF + PATCH), DD ** -0.5, 0.3125, ((0, 2),), jnp.float32),
        "dec_fc2": bell_draw(streams_of[7], (DFF, DD), DFF ** -0.5, 0.15625, ((0, 2),), jnp.float32),
        "vectors": jnp.clip(1.0 + 0.15 * jax.random.normal(streams_of[8], (VEC,), jnp.float32), 0.25, 1.75),
        "m_enc_rows": bell_draw(streams_of[9], (D, 4 * D + FF + DD), (0.13 * (CLIPS * MASKED * PARAMS) ** -0.5), 1.9073486328125e-06, ((0, 2),), jnp.float32),
        "m_enc_cols": bell_draw(streams_of[10], (PATCH + FF, D), (0.13 * (CLIPS * MASKED * PARAMS) ** -0.5), 1.9073486328125e-06, ((0, 2),), jnp.float32),
        "m_dec_rows": bell_draw(streams_of[11], (DD, 4 * DD + DFF + PATCH), (0.13 * (CLIPS * MASKED * PARAMS) ** -0.5), 1.9073486328125e-06, ((0, 2),), jnp.float32),
        "m_dec_fc2": bell_draw(streams_of[12], (DFF, DD), (0.13 * (CLIPS * MASKED * PARAMS) ** -0.5), 1.9073486328125e-06, ((0, 2),), jnp.float32),
        "m_vectors": bell_draw(streams_of[13], (VEC,), (0.13 * (CLIPS * MASKED * PARAMS) ** -0.5), 1.9073486328125e-06, ((0, 2),), jnp.float32),
        "v_enc_rows": jnp.clip(jnp.exp(math.log(2.026975321530594e-13) - 2.3025851 * jax.random.uniform(streams_of[14], (D, 4 * D + FF + DD), jnp.float32) ** steps_of(streams_of[14], (D, 4 * D + FF + DD), ((0, 2),), -0.2, 0.2)), 2.0269752537679583e-14, 2.026975321530594e-13),
        "v_enc_cols": jnp.clip(jnp.exp(math.log(2.026975321530594e-13) - 2.3025851 * jax.random.uniform(streams_of[15], (PATCH + FF, D), jnp.float32) ** steps_of(streams_of[15], (PATCH + FF, D), ((0, 2),), -0.2, 0.2)), 2.0269752537679583e-14, 2.026975321530594e-13),
        "v_dec_rows": jnp.clip(jnp.exp(math.log(2.026975321530594e-13) - 2.3025851 * jax.random.uniform(streams_of[16], (DD, 4 * DD + DFF + PATCH), jnp.float32) ** steps_of(streams_of[16], (DD, 4 * DD + DFF + PATCH), ((0, 2),), -0.2, 0.2)), 2.0269752537679583e-14, 2.026975321530594e-13),
        "v_dec_fc2": jnp.clip(jnp.exp(math.log(2.026975321530594e-13) - 2.3025851 * jax.random.uniform(streams_of[17], (DFF, DD), jnp.float32) ** steps_of(streams_of[17], (DFF, DD), ((0, 2),), -0.2, 0.2)), 2.0269752537679583e-14, 2.026975321530594e-13),
        "v_vectors": jnp.clip(jnp.exp(math.log(2.026975321530594e-13) - 2.3025851 * jax.random.uniform(streams_of[18], (VEC,), jnp.float32) ** steps_of(streams_of[18], (VEC,), ((0, 2),), -0.2, 0.2)), 2.0269752537679583e-14, 2.026975321530594e-13),
    }


@jax.custom_vjp
def low(v):
    return lax.optimization_barrier(v.astype(jnp.bfloat16)).astype(jnp.float32)

@jax.custom_vjp
def low_back(v):
    return v

def low_keep(v):
    return (low(v), None)

def low_pass(kept, grad):
    return (grad,)

def back_keep(v):
    return (v, None)

def back_low(kept, grad):
    return (low(grad),)
low.defvjp(low_keep, low_pass)
low_back.defvjp(back_keep, back_low)

def matmul(left, right):
    return jnp.dot(left, right, precision=lax.Precision.HIGHEST)

def sinusoid(positions, feat_width):
    places = jnp.arange(positions).astype(jnp.float32)[:, None]
    column = jnp.arange(feat_width)
    expo = (2 * (column // 2)).astype(jnp.float32) / feat_width
    angles = places / jnp.power(jnp.float32(10000.0), expo)[None, :]
    return jnp.where(column[None, :] % 2 == 0, jnp.sin(angles), jnp.cos(angles))

def unpack(vector):
    widths = [D] * 6 + [FF, D, DD] + [DD] * 6 + [DFF, DD, PATCH]
    pieces = []
    offset = 0
    for piece_width in widths:
        pieces.append(vector[offset:offset + piece_width])
        offset = offset + piece_width
    return pieces

def layer_norm(values, norm_gain, norm_bias):
    centred = values - lax.optimization_barrier(jnp.mean(values, axis=-1, keepdims=True))
    spread = lax.optimization_barrier(jnp.mean(centred * centred, axis=-1, keepdims=True))
    return centred * lax.rsqrt(spread + 1e-06) * norm_gain + norm_bias

def attention(qkv, head_count):
    length = qkv.shape[0]
    feat_width = qkv.shape[1] // 3
    head_dim = feat_width // head_count
    queries = qkv[:, :feat_width].reshape(length, head_count, head_dim)
    keys_all = qkv[:, feat_width:2 * feat_width].reshape(length, head_count, head_dim)
    values_all = qkv[:, 2 * feat_width:].reshape(length, head_count, head_dim)
    scores = low_back(jnp.einsum('qhd,khd->hqk', queries, keys_all, precision=lax.Precision.HIGHEST)) * head_dim ** (-0.5)
    weights = low(jax.nn.softmax(scores, axis=-1))
    mixed = jnp.einsum('hqk,khd->qhd', weights, values_all, precision=lax.Precision.HIGHEST)
    return mixed.reshape(length, feat_width)

def layer(hidden, mats, vecs, head_count):
    w_qkv, w_out, w_up, w_down = mats
    gain_one, bias_one, gain_two, bias_two, bias_up, bias_down = vecs
    normed = low(layer_norm(hidden, gain_one, bias_one))
    qkv = low(low_back(matmul(normed, w_qkv)))
    mixed = low(low_back(attention(qkv, head_count)))
    hidden = hidden + low_back(matmul(mixed, w_out))
    normed = low(layer_norm(hidden, gain_two, bias_two))
    inner = low_back(matmul(normed, w_up) + bias_up)
    activ = low(jax.nn.gelu(inner, approximate=False))
    return hidden + low_back(matmul(activ, w_down) + bias_down)

def clip_term(params, clip_pixels, visible, masked, loss_count):
    enc_rows, enc_cols, dec_rows, dec_fc2, pieces = params
    w_qkv = enc_rows[:, :3 * D]
    w_out = enc_rows[:, 3 * D:4 * D]
    w_up = enc_rows[:, 4 * D:4 * D + FF]
    w_proj = enc_rows[:, 4 * D + FF:]
    w_embed = enc_cols[:PATCH]
    w_down = enc_cols[PATCH:]
    u_qkv = dec_rows[:, :3 * DD]
    u_out = dec_rows[:, 3 * DD:4 * DD]
    u_up = dec_rows[:, 4 * DD:4 * DD + DFF]
    w_head = dec_rows[:, 4 * DD + DFF:]
    pos_enc = sinusoid(TUBES, D)
    pos_dec = sinusoid(TUBES, DD)
    embedded = low_back(matmul(clip_pixels[visible], w_embed)) + pos_enc[visible]
    enc_vecs = (pieces[0], pieces[1], pieces[2], pieces[3], pieces[6], pieces[7])
    encoded = layer(embedded, (w_qkv, w_out, w_up, w_down), enc_vecs, HEADS)
    latent = low(layer_norm(encoded, pieces[4], pieces[5]))
    projected = low_back(matmul(latent, w_proj))
    dec_input = jnp.concatenate([projected + pos_dec[visible], pieces[8][None, :] + pos_dec[masked]], axis=0)
    dec_vecs = (pieces[9], pieces[10], pieces[11], pieces[12], pieces[15], pieces[16])
    decoded = layer(dec_input, (u_qkv, u_out, u_up, dec_fc2), dec_vecs, DHEADS)
    final = low(layer_norm(decoded[VIS:], pieces[13], pieces[14]))
    pred = low_back(matmul(final, w_head) + pieces[17])
    target = clip_pixels[masked]
    centred = target - lax.optimization_barrier(jnp.mean(target, axis=-1, keepdims=True))
    target = centred * lax.rsqrt(lax.optimization_barrier(jnp.mean(centred * centred, axis=-1, keepdims=True)) + 1e-06)
    errors = lax.optimization_barrier(jnp.mean((pred - target) * (pred - target), axis=-1))
    live = (jnp.arange(MASKED) < loss_count).astype(jnp.float32)
    return jnp.sum(live * errors)

def adam_update(master, moment_one, moment_two, gradient):
    new_one = 0.9 * moment_one + 0.1 * gradient
    new_two = 0.95 * moment_two + 0.05 * gradient * gradient
    stepped = new_one / (1.0 - 0.9 ** 10) / (jnp.sqrt(new_two / (1.0 - 0.95 ** 10)) + 1e-12)
    return (master - 0.02 * (stepped + 0.05 * master), new_one, new_two)

def reference(clips, visible_idx, masked_idx, loss_counts, enc_rows, enc_cols, dec_rows, dec_fc2, vectors, m_enc_rows, m_enc_cols, m_dec_rows, m_dec_fc2, m_vectors, v_enc_rows, v_enc_cols, v_dec_rows, v_dec_fc2, v_vectors):
    pixels = clips.astype(jnp.float32)
    total = jnp.sum(loss_counts).astype(jnp.float32)
    term_fn = jax.checkpoint(clip_term)

    def loss_of(w_one, w_two, w_three, w_four, vec_all):
        low_params = (low(w_one), low(w_two), low(w_three), low(w_four), unpack(low(vec_all)))

        def scan_step(carry, items):
            return (carry + term_fn(low_params, items[0], items[1], items[2], items[3]), None)
        summed, ignored = lax.scan(scan_step, jnp.float32(0.0), (pixels, visible_idx, masked_idx, loss_counts))
        return summed / total
    masters = (enc_rows, enc_cols, dec_rows, dec_fc2, vectors)
    loss, pullback = jax.vjp(loss_of, *masters)
    grads = pullback(jnp.float32(1.0))
    squares = jnp.float32(0.0)
    for gradient in grads:
        squares = squares + jnp.sum(gradient * gradient)
    grad_norm = jnp.sqrt(squares)
    factor = jnp.minimum(jnp.float32(1.0), lax.rsqrt(total) / grad_norm)
    firsts = (m_enc_rows, m_enc_cols, m_dec_rows, m_dec_fc2, m_vectors)
    seconds = (v_enc_rows, v_enc_cols, v_dec_rows, v_dec_fc2, v_vectors)
    new_w, new_m, new_v = ([], [], [])
    for index in range(5):
        updated = adam_update(masters[index], firsts[index], seconds[index], grads[index] * factor)
        new_w.append(updated[0])
        new_m.append(updated[1])
        new_v.append(updated[2])
    return (loss, grad_norm, new_w[0], new_w[1], new_w[2], new_w[3], new_w[4], new_m[0], new_m[1], new_m[2], new_m[3], new_m[4], new_v[0], new_v[1], new_v[2], new_v[3], new_v[4], new_w[0].astype(jnp.bfloat16), new_w[1].astype(jnp.bfloat16), new_w[2].astype(jnp.bfloat16), new_w[3].astype(jnp.bfloat16), new_w[4].astype(jnp.bfloat16))
```

```python
import functools
import jax
import jax.numpy as jnp
from jax import lax
from jax.experimental import pallas as pl
from jax.experimental.pallas import tpu as pltpu
from jax.sharding import PartitionSpec as P

D = 768
HEADS = 12
FF = 3072
DD = 384
DHEADS = 6
DFF = 1536
PATCH = 1536


beta_one = 0.9
beta_two = 0.95
bias_fix_one = 1.0 - 0.9**10
bias_fix_two = 1.0 - 0.95**10
learn_rate = 0.02
decay_rate = 0.05
adam_eps = 1e-12
norm_eps = 1e-06


def product_of(left, right):
    return jnp.dot(left, right, preferred_element_type=jnp.float32)


def product_tn(left, right):
    return jnp.dot(left.T, right, preferred_element_type=jnp.float32)


f32, bf16 = jnp.float32, jnp.bfloat16
LOG2E = 1.4426950408889634
NT = (((1,), (1,)), ((), ()))
NN = (((1,), (0,)), ((), ()))
TN = (((0,), (0,)), ((), ()))
def dot(a, b, dims): return lax.dot_general(a, b, dims, preferred_element_type=f32)

def cost(micros, moved=0):
    return pl.CostEstimate(flops=int(micros * 1.1e9), transcendentals=0, bytes_accessed=moved)

def fwd_body(scale, q_ref, k_ref, v_ref, o_ref, lse_ref):
    q = q_ref[0]; k = k_ref[0]; v = v_ref[0]
    lane = lax.broadcasted_iota(jnp.int32, (1, 128), 1)
    outs = []
    for h in range(2):
        own = (lane < 64) if h == 0 else (lane >= 64)
        qh = jnp.where(own, q, jnp.zeros_like(q))
        s = dot(qh, k, NT)
        peak = jnp.max(s, axis=1, keepdims=True)
        e = jnp.exp2((s - peak) * (scale * LOG2E))
        tot = jnp.sum(e, axis=1, keepdims=True)
        p = (e * (1.0 / tot)).astype(bf16)
        outs.append(dot(p, v, NN))
        lse_ref[0, 0, h:h+1, :] = (peak * (scale * LOG2E) + jnp.log2(tot)).T
    o_ref[0] = jnp.where(lane < 64, outs[0], outs[1]).astype(bf16)

def attn_fwd(qkv, heads, rows, bq):
    clips, keys, w3 = qkv.shape
    pairs = heads // 2
    nb = rows // bq
    body = functools.partial(fwd_body, 64 ** -0.5)
    return pl.pallas_call(
        body, grid=(clips, pairs, nb),
        in_specs=[pl.BlockSpec((1, bq, 128), lambda c, p, i: (c, i, p)),
                  pl.BlockSpec((1, keys, 128), lambda c, p, i: (c, 0, pairs + p)),
                  pl.BlockSpec((1, keys, 128), lambda c, p, i: (c, 0, 2 * pairs + p))],
        out_specs=[pl.BlockSpec((1, bq, 128), lambda c, p, i: (c, i, p)),
                   pl.BlockSpec((1, 1, 2, bq), lambda c, p, i: (c * pairs + p, i, 0, 0))],
        out_shape=[jax.ShapeDtypeStruct((clips, rows, w3 // 3), bf16),
                   jax.ShapeDtypeStruct((clips * pairs, nb, 2, bq), f32)],
        compiler_params=pltpu.CompilerParams(vmem_limit_bytes=60 << 20), name="dec_attend_forward", cost_estimate=cost(70),
    )(qkv, qkv, qkv)

def bwd_body(scale, nb, mode, q_ref, k_ref, v_ref, do_ref, lse_ref, dq_ref, dk_ref, dv_ref, dk_acc, dv_acc, kt_ref):
    i = pl.program_id(2)
    q = q_ref[0]; k = k_ref[0]; v = v_ref[0]; do = do_ref[0]
    lane = lax.broadcasted_iota(jnp.int32, (1, 128), 1)
    if mode == 1:
        @pl.when(i == 0)
        def _(): kt_ref[...] = k.T
    dk = dv = None
    dqs = []
    for h in range(2):
        own = (lane < 64) if h == 0 else (lane >= 64)
        qh = jnp.where(own, q, jnp.zeros_like(q))
        doh = jnp.where(own, do, jnp.zeros_like(do))
        s = dot(k, qh, NT)
        dp = dot(v, doh, NT)
        p = jnp.exp2(s * (scale * LOG2E) - lse_ref[0, 0, h:h+1, :])
        pd = p * dp
        delta = jnp.sum(pd, axis=0, keepdims=True)
        ds = (p * (dp - delta)).astype(bf16)
        a = dot(p.astype(bf16), doh, NN)
        b = dot(ds, qh, NN)
        dv = a if dv is None else dv + a
        dk = b if dk is None else dk + b
        if mode == 0:
            dqs.append(dot(ds, k, TN))
        else:
            dqs.append(dot(kt_ref[h*64:(h+1)*64, :], ds, NN))
    if mode == 0:
        dq = jnp.where(lane < 64, dqs[0], dqs[1])
    else:
        dq = jnp.concatenate(dqs, axis=0).T
    bq = q.shape[0]
    dq_ref[0, pl.ds(pl.multiple_of(i * bq, bq), bq), :] = (dq * scale).astype(bf16)
    @pl.when(i == nb - 1)
    def _():
        keys = k.shape[0]
        if nb * bq < keys:
            dq_ref[0, nb * bq:keys, :] = jnp.zeros((keys - nb * bq, 128), bf16)
    @pl.when(i == 0)
    def _():
        dk_acc[...] = dk; dv_acc[...] = dv
    @pl.when(i > 0)
    def _():
        dk_acc[...] += dk; dv_acc[...] += dv
    @pl.when(i == nb - 1)
    def _():
        dk_ref[0] = (dk_acc[...] * scale).astype(bf16)
        dv_ref[0] = dv_acc[...].astype(bf16)

def attn_bwd(qkv, do, lse, heads, rows, bq, clip, pair):
    clips, keys, w3 = qkv.shape
    pairs = heads // 2
    nb = rows // bq
    return pl.pallas_call(
        functools.partial(bwd_body, 64 ** -0.5, nb, 0), grid=(1, 1, nb),
        in_specs=[pl.BlockSpec((1, bq, 128), lambda c, p, i: (clip, i, pair)),
                  pl.BlockSpec((1, keys, 128), lambda c, p, i: (clip, 0, pairs + pair)),
                  pl.BlockSpec((1, keys, 128), lambda c, p, i: (clip, 0, 2 * pairs + pair)),
                  pl.BlockSpec((1, bq, 128), lambda c, p, i: (clip, i, pair)),
                  pl.BlockSpec((1, 1, 2, bq), lambda c, p, i: (clip * pairs + pair, i, 0, 0))],
        out_specs=[pl.BlockSpec((1, keys, 128), lambda c, p, i: (0, 0, 0))] * 3,
        out_shape=[jax.ShapeDtypeStruct((1, keys, 128), bf16)] * 3,
        scratch_shapes=[pltpu.VMEM((keys, 128), f32), pltpu.VMEM((keys, 128), f32), pltpu.VMEM((128, keys), bf16)],
        compiler_params=pltpu.CompilerParams(vmem_limit_bytes=60 << 20), name=f"dec_attend_backward_{clip}_{pair}",
        cost_estimate=cost(17),
    )(qkv, qkv, qkv, do, lse)
DEC_VEC = 6 * D + FF + D + DD

def ln(x):
    c = x - jnp.mean(x, axis=1, keepdims=True)
    inv = lax.rsqrt(jnp.mean(c * c, axis=1, keepdims=True) + norm_eps)
    return c * inv, inv

def ln_back(up, scaled, inv, gain):
    w = up * gain
    return inv * (w - jnp.mean(w, axis=1, keepdims=True) - scaled * jnp.mean(w * scaled, axis=1, keepdims=True))

def col(x): return jnp.sum(x, axis=0, keepdims=True)

def gelu_parts(x):
    cdf = 0.5 * (1.0 + lax.erf(x * 0.7071067811865476))
    return x * cdf, cdf + x * jnp.exp(-0.5 * x * x) * 0.3989422804014327

def post_body(nb, rows, keys, cnt_ref, inv_ref, h_ref, o_ref, t_ref, wout_ref, wup_ref, wdown_ref, whead_ref,
              v_ref, dmid_ref, do_ref, grow_ref, gdown_ref, s384_ref, s1536_ref, loss_ref, gdown_acc):
    c = pl.program_id(0); i = pl.program_id(1)
    first = jnp.logical_and(c == 0, i == 0)
    @pl.when(first)
    def _():
        for r in (grow_ref, gdown_acc, s384_ref, s1536_ref, loss_ref):
            r[...] = jnp.zeros_like(r)
    R = rows
    h = h_ref[0]; o = o_ref[0]
    w, ff = h.shape[1], wup_ref.shape[1]
    gain2, bias2, gainf, biasf = (v_ref[:, DEC_VEC + j * DD:DEC_VEC + (j + 1) * DD] for j in range(2, 6))
    bup = v_ref[:, DEC_VEC + 6 * DD:DEC_VEC + 6 * DD + DFF]
    bdown = v_ref[:, DEC_VEC + 6 * DD + DFF:DEC_VEC + 7 * DD + DFF]
    bhead = v_ref[:, DEC_VEC + 7 * DD + DFF:]
    h1 = h + dot(o, wout_ref[...], NN)
    sc2, inv2 = ln(h1)
    m = (sc2 * gain2 + bias2).astype(bf16)
    inner = dot(m, wup_ref[...], NN) + bup
    act, slope = gelu_parts(inner)
    act = act.astype(bf16)
    out = h1 + (dot(act, wdown_ref[...], NN) + bdown)
    scf, invf = ln(out)
    fin = (scf * gainf + biasf).astype(bf16)
    pred = dot(fin, whead_ref[...], NN) + bhead
    t = t_ref[0].astype(f32)
    tc = t - jnp.mean(t, axis=1, keepdims=True)
    err = pred - tc * lax.rsqrt(jnp.mean(tc * tc, axis=1, keepdims=True) + norm_eps)
    row = lax.broadcasted_iota(jnp.int32, (R, 1), 0) + i * R
    live = (row < cnt_ref[c]).astype(f32)
    rl = jnp.mean(err * err, axis=1, keepdims=True) * live
    loss_ref[...] += jnp.sum(rl).reshape(1, 1)
    pg32 = err * (live * inv_ref[0])
    pg = pg32.astype(bf16)
    grow_ref[:, w + ff:] += dot(fin, pg, TN)
    dfin = dot(pg, whead_ref[...], NT)
    s1536_ref[1:2, :] += col(pg.astype(f32))
    s384_ref[2:3, :] += col(dfin * scf)
    s384_ref[3:4, :] += col(dfin)
    dout = ln_back(dfin, scf, invf, gainf)
    dl = dout.astype(bf16)
    gdown_acc[...] += dot(dl, act, TN)
    s384_ref[4:5, :] += col(dl.astype(f32))
    din = (dot(dl, wdown_ref[...], NT) * slope).astype(bf16)
    grow_ref[:, w:w + ff] += dot(m, din, TN)
    s1536_ref[0:1, :] += col(din.astype(f32))
    dm = dot(din, wup_ref[...], NT)
    s384_ref[0:1, :] += col(dm * sc2)
    s384_ref[1:2, :] += col(dm)
    dmid = dout + ln_back(dm, sc2, inv2, gain2)
    bl = dmid.astype(bf16)
    grow_ref[:, :w] += dot(o, bl, TN)
    do_ref[0] = dot(bl, wout_ref[...], NT).astype(bf16)
    dmid_ref[0, pl.ds(pl.multiple_of(i * R, R), R), :] = dmid
    @pl.when(i == nb - 1)
    def _():
        dmid_ref[0, nb * R:keys, :] = jnp.zeros((keys - nb * R, dmid.shape[1]), f32)
    @pl.when(jnp.logical_and(c == pl.num_programs(0) - 1, i == nb - 1))
    def _():
        gdown_ref[...] = gdown_acc[...].T

def dec_post(counts, inv, h, o, t, wout, wup, wdown, whead, vec, R):
    clips, keys, w = h.shape
    rows = o.shape[1]; nb = rows // R
    ff, px = wup.shape[1], whead.shape[1]
    full = lambda a: pl.BlockSpec(a.shape, lambda c, i: (0,) * len(a.shape))
    sm = pl.BlockSpec(memory_space=pltpu.SMEM)
    outs = [jax.ShapeDtypeStruct((clips, keys, w), f32), jax.ShapeDtypeStruct((clips, rows, w), bf16),
            jax.ShapeDtypeStruct((w, w + ff + px), f32), jax.ShapeDtypeStruct((ff, w), f32), jax.ShapeDtypeStruct((8, w), f32), jax.ShapeDtypeStruct((8, ff), f32),
            jax.ShapeDtypeStruct((1, 1), f32)]
    blk = lambda n: pl.BlockSpec((1, R, n), lambda c, i: (c, i, 0))
    return pl.pallas_call(
        functools.partial(post_body, nb, R, keys), grid=(clips, nb),
        in_specs=[sm, sm, blk(w), blk(w), blk(px), full(wout), full(wup), full(wdown), full(whead), full(vec)],
        out_specs=[pl.BlockSpec((1, keys, w), lambda c, i: (c, 0, 0)), blk(w)] + [full(x) for x in outs[2:]],
        out_shape=outs, compiler_params=pltpu.CompilerParams(vmem_limit_bytes=62 << 20), name="dec_post",
        scratch_shapes=[pltpu.VMEM((w, ff), f32)], cost_estimate=cost(67),
    )(counts, inv, h, o, t, wout, wup, wdown, whead, vec)

def qkv_body(h_ref, w_ref, v_ref, o_ref):
    s, _ = ln(h_ref[0])
    a = (s * v_ref[:, DEC_VEC:DEC_VEC + DD] + v_ref[:, DEC_VEC + DD:DEC_VEC + 2 * DD]).astype(bf16)
    o_ref[0] = dot(a, w_ref[...], NN).astype(bf16)

def dec_qkv(h, w, v, R):
    clips, keys, d = h.shape
    full = lambda a: pl.BlockSpec(a.shape, lambda c, i: (0,) * len(a.shape))
    return pl.pallas_call(qkv_body, grid=(clips, keys // R),
        in_specs=[pl.BlockSpec((1, R, d), lambda c, i: (c, i, 0)), full(w), full(v)],
        out_specs=pl.BlockSpec((1, R, w.shape[1]), lambda c, i: (c, i, 0)),
        out_shape=jax.ShapeDtypeStruct((clips, keys, w.shape[1]), bf16),
        compiler_params=pltpu.CompilerParams(vmem_limit_bytes=60 << 20), name="dec_qkv", cost_estimate=cost(9))(h, w, v)

def qkvb_body(R, masked, h_ref, dmid_ref, w_ref, v_ref, gi_ref, si_ref, *refs):
    parts, (dh_ref, g_ref, s_ref) = refs[:9], refs[9:]
    i = pl.program_id(0)
    @pl.when(i == 0)
    def _():
        g_ref[...] = gi_ref[...]; s_ref[...] = si_ref[...]
    d = h_ref.shape[2]
    s, inv = ln(h_ref[0])
    gain = v_ref[:, DEC_VEC:DEC_VEC + DD]
    a = (s * gain + v_ref[:, DEC_VEC + DD:DEC_VEC + 2 * DD]).astype(bf16)
    da = None
    for j in range(3):
        x = jnp.concatenate([parts[3 * p + j][0] for p in range(3)], axis=1)
        g_ref[:, j * d:(j + 1) * d] += dot(a, x, TN)
        y = dot(x, w_ref[:, j * d:(j + 1) * d], NT)
        da = y if da is None else da + y
    s_ref[0:1, :] += col(da * s)
    s_ref[1:2, :] += col(da)
    dh = dmid_ref[0] + ln_back(da, s, inv, gain)
    row = lax.broadcasted_iota(jnp.int32, (R, 1), 0) + i * R
    s_ref[2:3, :] += col(jnp.where(row < masked, dh, 0.0))
    dh_ref[0] = dh.astype(bf16)

def dec_qkv_back(h, parts, dmid, w, v, masked, R, clip, before):
    clips, keys, d = h.shape
    full = lambda a: pl.BlockSpec(a.shape, lambda i: (0,) * len(a.shape))
    blk = pl.BlockSpec((1, R, d), lambda i: (clip, i, 0))
    part = pl.BlockSpec((1, R, 128), lambda i: (0, i, 0))
    outs = [jax.ShapeDtypeStruct((1, keys, d), bf16), jax.ShapeDtypeStruct((d, 3 * d), f32), jax.ShapeDtypeStruct((8, d), f32)]
    return pl.pallas_call(functools.partial(qkvb_body, R, masked), grid=(keys // R,),
        in_specs=[blk, blk, full(w), full(v), full(outs[1]), full(outs[2])] + [part] * 9,
        out_specs=[pl.BlockSpec((1, R, d), lambda i: (0, i, 0)), full(outs[1]), full(outs[2])], out_shape=outs,
        compiler_params=pltpu.CompilerParams(vmem_limit_bytes=60 << 20), name=f"dec_qkv_back_{clip}",
        cost_estimate=cost(10))(h, dmid, w, v, *before, *parts)

def pick_body(idx_ref, x_ref, *refs):
    n = x_ref.shape[1]
    hot = (idx_ref[0] == lax.broadcasted_iota(jnp.int32, (1, n), 1)).astype(f32).astype(bf16)
    refs[-1][0] = dot(hot, x_ref[0], NN).astype(bf16)

def pick_rows(x, idx, R, clip, name, into=None):
    clips, n, w = x.shape
    m = idx.shape[1]
    more = [] if into is None else [into]
    return pl.pallas_call(pick_body, grid=(m // R,),
        in_specs=[pl.BlockSpec((1, R, 1), lambda i: (clip, i, 0)), pl.BlockSpec((1, n, w), lambda i: (clip, 0, 0))]
        + [pl.BlockSpec(memory_space=pl.ANY)] * len(more),
        out_specs=pl.BlockSpec((1, R, w), lambda i: (clip, i, 0)),
        out_shape=jax.ShapeDtypeStruct((clips, m, w), bf16), cost_estimate=cost(m / 140),
        input_output_aliases={2: 0} if more else {},
        compiler_params=pltpu.CompilerParams(vmem_limit_bytes=60 << 20), name=f"{name}_{clip}")(idx[:, :, None], x, *more)

QKV, OUT, UP, PROJ = slice(0, 3 * D), slice(3 * D, 4 * D), slice(4 * D, 4 * D + FF), slice(4 * D + FF, 4 * D + FF + DD)

def enc_vec(v_ref, at):
    starts = [0, D, 2 * D, 3 * D, 4 * D, 5 * D, 6 * D, 6 * D + FF]
    return v_ref[:, starts[at]:starts[at] + (FF if at == 6 else D)]

def most(x):
    x = x.astype(f32)
    return jnp.max(jnp.sum(x * x, axis=0, keepdims=True))

def enc_scores(qkv_ref, rows, p, h, seen):
    lane = lax.broadcasted_iota(jnp.int32, (1, 128), 1)
    own = (lane < 64) if h == 0 else (lane >= 64)
    q = qkv_ref[rows, p * 128:(p + 1) * 128]
    k = qkv_ref[rows, D + p * 128:D + (p + 1) * 128]
    v = qkv_ref[rows, 2 * D + p * 128:2 * D + (p + 1) * 128]
    qh = jnp.where(own, q, jnp.zeros_like(q))
    s = dot(qh, k, NT)
    s = jnp.where(lax.broadcasted_iota(jnp.int32, (1, s.shape[1]), 1) < seen, s, -3e38)
    peak = jnp.max(s, axis=1, keepdims=True)
    e = jnp.exp2((s - peak) * (0.125 * LOG2E))
    return q, k, v, qh, own, e * (1.0 / jnp.sum(e, axis=1, keepdims=True))

def enc_fwd_body(clips, seen, x_ref, pos_ref, wr_ref, wc_ref, v_ref,
                 h_ref, qkv_ref, h1_ref, inner_ref, enc_ref, proj_ref, tall_ref, pair_ref, m_ref, lat_ref, most_ref):
    x = x_ref[...]
    h = dot(x, wc_ref[:PATCH], NN) + pos_ref[...]
    h_ref[...] = h
    s1, _ = ln(h)
    a = (s1 * enc_vec(v_ref, 0) + enc_vec(v_ref, 1)).astype(bf16)
    pair_ref[0] = a
    qkv_ref[...] = dot(a, wr_ref[:, QKV], NN).astype(bf16)
    n = h.shape[0] // clips
    for c in range(clips):
        rows = slice(c * n, (c + 1) * n)
        for p in range(HEADS // 2):
            outs = []
            for hd in range(2):
                q, k, v, qh, own, prob = enc_scores(qkv_ref, rows, p, hd, seen)
                outs.append(dot(prob.astype(bf16), v, NN))
            lane = lax.broadcasted_iota(jnp.int32, (1, 128), 1)
            pair_ref[1, rows, p * 128:(p + 1) * 128] = jnp.where(lane < 64, outs[0], outs[1]).astype(bf16)
    o = pair_ref[1]
    h1 = h + dot(o, wr_ref[:, OUT], NN)
    h1_ref[...] = h1
    s2, _ = ln(h1)
    m = (s2 * enc_vec(v_ref, 2) + enc_vec(v_ref, 3)).astype(bf16)
    m_ref[...] = m
    inner = dot(m, wr_ref[:, UP], NN) + enc_vec(v_ref, 6)
    inner_ref[...] = inner
    act = gelu_parts(inner)[0].astype(bf16)
    out = h1 + (dot(act, wc_ref[PATCH:], NN) + enc_vec(v_ref, 7))
    enc_ref[...] = out
    sf, _ = ln(out)
    lat = (sf * enc_vec(v_ref, 4) + enc_vec(v_ref, 5)).astype(bf16)
    lat_ref[...] = lat
    proj_ref[...] = dot(lat, wr_ref[:, PROJ], NN)
    tall_ref[:, :PATCH] = x
    tall_ref[:, PATCH:] = act
    for at, y in enumerate((x, act, a, o, m)):
        most_ref[at:at + 1, :] = jnp.broadcast_to(most(y).reshape(1, 1), (1, 128))

def whole(shape): return pl.BlockSpec(shape, lambda: (0,) * len(shape))

def enc_fwd(x, pos, wr, wc, vec, clips, seen):
    n = x.shape[0]
    shapes = [((n, D), f32), ((n, 3 * D), bf16), ((n, D), f32), ((n, FF), f32), ((n, D), f32), ((n, DD), f32),
              ((n, PATCH + FF), bf16), ((2, n, D), bf16), ((n, D), bf16), ((n, D), bf16), ((8, 128), f32)]
    return pl.pallas_call(functools.partial(enc_fwd_body, clips, seen),
        in_specs=[whole(a.shape) for a in (x, pos, wr, wc, vec)],
        out_specs=[whole(s) for s, _ in shapes], out_shape=[jax.ShapeDtypeStruct(s, d) for s, d in shapes],
        compiler_params=pltpu.CompilerParams(vmem_limit_bytes=62 << 20), name="enc_forward",
        cost_estimate=pl.CostEstimate(flops=2 * n * 8552448, transcendentals=n * FF, bytes_accessed=26 << 20),
    )(x, pos, wr, wc, vec)

def enc_bwd_body(clips, seen, dp_ref, h_ref, qkv_ref, h1_ref, inner_ref, enc_ref, wr_ref, wc_ref, v_ref,
                 gdown_ref, gup_ref, gwide_ref, gin_ref, s_ref, sup_ref, most_ref):
    sf, invf = ln(enc_ref[...])
    up = dot(dp_ref[...], wr_ref[:, PROJ], NT)
    s_ref[4:5, :] = col(up * sf); s_ref[5:6, :] = col(up)
    dout = ln_back(up, sf, invf, enc_vec(v_ref, 4))
    dl = dout.astype(bf16)
    gdown_ref[...] = dl
    s_ref[6:7, :] = col(dl.astype(f32))
    din = (dot(dl, wc_ref[PATCH:], NT) * gelu_parts(inner_ref[...])[1]).astype(bf16)
    gup_ref[...] = din
    sup_ref[...] = col(din.astype(f32))
    dm = dot(din, wr_ref[:, UP], NT)
    s2, inv2 = ln(h1_ref[...])
    s_ref[2:3, :] = col(dm * s2); s_ref[3:4, :] = col(dm)
    dmid = dout + ln_back(dm, s2, inv2, enc_vec(v_ref, 2))
    bl = dmid.astype(bf16)
    gwide_ref[:, 3 * D:] = bl
    do = dot(bl, wr_ref[:, OUT], NT).astype(bf16)
    n = do.shape[0] // clips
    for c in range(clips):
        rows = slice(c * n, (c + 1) * n)
        for p in range(HEADS // 2):
            dop = do[rows, p * 128:(p + 1) * 128]
            dqs, dk, dv = [], None, None
            for hd in range(2):
                q, k, v, qh, own, prob = enc_scores(qkv_ref, rows, p, hd, seen)
                doh = jnp.where(own, dop, jnp.zeros_like(dop))
                dpr = dot(doh, v, NT)
                ds = (prob * (dpr - jnp.sum(dpr * prob, axis=1, keepdims=True))).astype(bf16)
                dqs.append(dot(ds, k, NN))
                x, y = dot(ds, qh, TN), dot(prob.astype(bf16), doh, TN)
                dk = x if dk is None else dk + x
                dv = y if dv is None else dv + y
            lane = lax.broadcasted_iota(jnp.int32, (1, 128), 1)
            dq = jnp.where(lane < 64, dqs[0], dqs[1])
            gwide_ref[rows, p * 128:(p + 1) * 128] = (dq * 0.125).astype(bf16)
            gwide_ref[rows, D + p * 128:D + (p + 1) * 128] = (dk * 0.125).astype(bf16)
            gwide_ref[rows, 2 * D + p * 128:2 * D + (p + 1) * 128] = dv.astype(bf16)
    da = dot(gwide_ref[:, :3 * D], wr_ref[:, QKV], NT)
    s1, inv1 = ln(h_ref[...])
    s_ref[0:1, :] = col(da * s1); s_ref[1:2, :] = col(da)
    s_ref[7:8, :] = jnp.zeros_like(s_ref[7:8, :])
    gin = (dmid + ln_back(da, s1, inv1, enc_vec(v_ref, 0))).astype(bf16)
    gin_ref[...] = gin
    for at, y in enumerate((gin, dl, gwide_ref[:, :3 * D], bl, din)):
        most_ref[at:at + 1, :] = jnp.broadcast_to(most(y).reshape(1, 1), (1, 128))

def enc_bwd(dp, h, qkv, h1, inner, enc, wr, wc, vec, clips, seen):
    n = h.shape[0]
    shapes = [((n, D), bf16), ((n, FF), bf16), ((n, 4 * D), bf16), ((n, D), bf16), ((8, D), f32), ((1, FF), f32), ((8, 128), f32)]
    ins = (dp, h, qkv, h1, inner, enc, wr, wc, vec)
    return pl.pallas_call(functools.partial(enc_bwd_body, clips, seen),
        in_specs=[whole(a.shape) for a in ins],
        out_specs=[whole(s) for s, _ in shapes], out_shape=[jax.ShapeDtypeStruct(s, d) for s, d in shapes],
        compiler_params=pltpu.CompilerParams(vmem_limit_bytes=62 << 20), name="enc_backward",
        cost_estimate=pl.CostEstimate(flops=2 * n * 8552448, transcendentals=n * FF, bytes_accessed=28 << 20),
    )(*ins)

def pair_body(al_ref, bl_ref, ar_ref, br_ref, o_ref):
    o_ref[...] = dot(al_ref[0], ar_ref[0], TN) + dot(bl_ref[0], br_ref[0], TN)

def pair_product(lefts, rights, rows, cols, bm, bn, left_at, right_at, name):
    n = lefts[0].shape[1]
    ls = pl.BlockSpec((1, n, bm), lambda i, j: left_at(i, j))
    rs = pl.BlockSpec((1, n, bn), lambda i, j: right_at(i, j))
    return pl.pallas_call(pair_body, grid=(rows // bm, cols // bn), in_specs=[ls, ls, rs, rs],
        out_specs=pl.BlockSpec((bm, bn), lambda i, j: (i, j)), out_shape=jax.ShapeDtypeStruct((rows, cols), f32),
        compiler_params=pltpu.CompilerParams(vmem_limit_bytes=60 << 20), name=name,
        cost_estimate=pl.CostEstimate(flops=4 * n * rows * cols, transcendentals=0, bytes_accessed=4 * rows * cols),
    )(lefts[0], lefts[1], rights[0], rights[1])
def dec_parts(dec_low_rows, dec_low_fc2):
    mats = (
        dec_low_rows[:, : 3 * DD],
        dec_low_rows[:, 3 * DD : 4 * DD],
        dec_low_rows[:, 4 * DD : 4 * DD + DFF],
        dec_low_fc2,
    )
    return (mats, dec_low_rows[:, 4 * DD + DFF :])


def adam_update(master, moment_one, moment_two, gradient):
    new_one = beta_one * moment_one + (1.0 - beta_one) * gradient
    new_two = beta_two * moment_two + (1.0 - beta_two) * gradient * gradient
    stepped = new_one / bias_fix_one / (jnp.sqrt(new_two / bias_fix_two) + adam_eps)
    return (master - learn_rate * (stepped + decay_rate * master), new_one, new_two)


BLOCK = 480


def sinusoid_at(places, feat_width):
    column = jnp.arange(feat_width)
    expo = (2 * (column // 2)).astype(jnp.float32) / feat_width
    angles = places.astype(jnp.float32)[..., None] / jnp.power(jnp.float32(10000.0), expo)
    return jnp.where(column % 2 == 0, jnp.sin(angles), jnp.cos(angles))


def bit_of(name, hop):
    return (lax.axis_index(name) // hop) % 2


def swap(value, name, size, hop):
    return lax.ppermute(value, name, [(i, i ^ hop) for i in range(size)])


def total_everywhere(value, sizes, combine=jnp.add):
    for name, size in sizes:
        hop = 1
        while hop < size:
            value = combine(value, swap(value, name, size, hop))
            hop *= 2
    return value


def keep_and_send(value, dim, bit):
    half = value.shape[dim] // 2
    kept = lax.dynamic_slice_in_dim(value, bit * half, half, dim)
    sent = lax.dynamic_slice_in_dim(value, (1 - bit) * half, half, dim)
    return kept, sent


def join(mine, other, dim, bit):
    return jnp.where(
        bit == 0, jnp.concatenate([mine, other], axis=dim), jnp.concatenate([other, mine], axis=dim)
    )


def split_view(value, shard, ways):
    rows = value.shape[0] // shard
    return value.reshape((shard,) + (2,) * ways + (rows >> ways, value.shape[1]))


class Links:
    def __init__(self, rep, shard):
        self.rep, self.shard = rep, shard
        self.ways = min(3, rep.bit_length() - 1)
        self.inner = [("rep", 1 << k) for k in range(self.ways)]
        self.outer = [("rep", 1 << k) for k in range(self.ways, rep.bit_length() - 1)]
        self.owners = [("shard", 1 << k) for k in reversed(range(shard.bit_length() - 1))]
        self.sizes = (("rep", rep), ("shard", shard))

    def size(self, name):
        return self.rep if name == "rep" else self.shard

    def swap(self, value, hop):
        return swap(value, hop[0], self.size(hop[0]), hop[1])

    def dim(self, hop, core):
        return 0 if hop[0] == "shard" else hop[1].bit_length() - (not core)

    def reduce(self, parts, scales, turns, core):
        parts = list(parts)
        first = self.inner[:1] if core else []
        rest = self.inner[1:] + self.owners[:1]
        orders = []
        for turn in turns:
            turn = turn % len(rest)
            orders.append(first + rest[turn:] + rest[:turn] + self.owners[1:])
        for step in range(len(orders[0])):
            held, moving = [], []
            for part, scale, order in zip(parts, scales, orders):
                hop = order[step]
                kept, sent = keep_and_send(part, self.dim(hop, core), bit_of(*hop))
                if scale is not None:
                    sent = (sent * scale).astype(jnp.float16)
                held.append(kept)
                moving.append(self.swap(sent, hop))
            moving = yield moving
            for at, (kept, came) in enumerate(zip(held, moving)):
                if scales[at] is not None:
                    came = came.astype(jnp.float32) * (1.0 / scales[at])
                parts[at] = kept + came
        for hop in self.outer:
            mine = [
                part if scale is None else lax.optimization_barrier((part * scale).astype(jnp.float16))
                for part, scale in zip(parts, scales)
            ]
            other = yield [self.swap(part, hop) for part in mine]
            for at, scale in enumerate(scales):
                if scale is None:
                    parts[at] = mine[at] + other[at]
                else:
                    both = mine[at].astype(jnp.float32) + other[at].astype(jnp.float32)
                    parts[at] = both * (1.0 / scale)
        return parts

    def spread(self, pieces, turns, core):
        pieces = list(pieces)
        rest = self.inner[1:]
        orders = []
        for turn in turns:
            turn = turn % len(rest) if rest else 0
            orders.append(rest[turn:] + rest[:turn] + (self.inner[:1] if core else []))
        for step in range(len(orders[0])):
            moving = yield [self.swap(piece, order[step]) for piece, order in zip(pieces, orders)]
            pieces = [
                join(piece, came, self.dim(order[step], core), bit_of(*order[step]))
                for piece, came, order in zip(pieces, moving, orders)
            ]
        return pieces

    def own_block(self, view):
        for hop in self.inner:
            view, _ = keep_and_send(view, self.dim(hop, True), bit_of(*hop))
        return view


class Steps:
    def __init__(self, generator):
        self.generator, self.flight, self.result = generator, None, None
        self.step()

    def step(self):
        if self.result is None:
            try:
                self.flight = self.generator.send(self.flight)
            except StopIteration as end:
                self.flight, self.result = None, end.value


def arrive(steps, value=()):
    steps = [each for each in steps if each.result is None]
    value, flights = lax.optimization_barrier((value, [each.flight for each in steps]))
    for each, flight in zip(steps, flights):
        each.flight = flight
        each.step()
    return value


def complete(*steps):
    while any(each.result is None for each in steps):
        arrive(steps)
    return [each.result for each in steps]


def one_hop(links, values, hop):
    return (yield [links.swap(value, hop) for value in values])


def over_all(links, value, combine, skip=()):
    for name, size in links.sizes:
        for k in range(size.bit_length() - 1):
            if (name, 1 << k) not in skip:
                other = yield links.swap(value, (name, 1 << k))
                value = combine(value, other)
    return value


def from_owners(links, owned, fars):
    size = links.shard
    return (
        yield [
            [lax.ppermute(own, "shard", [(i, (i + far) % size) for i in range(size)]) for own in owned] for far in fars
        ]
    )


def assembled(own, parts, me):
    parts = [part.reshape(own.shape) for part in parts]
    if len(parts) == 1:
        return join(own, parts[0], 0, me)
    whole = jnp.zeros((len(parts) + 1,) + own.shape, own.dtype)
    for far, part in enumerate([own] + parts):
        whole = lax.dynamic_update_slice_in_dim(whole, part[None], (me - far) % (len(parts) + 1), 0)
    return whole.reshape((-1,) + own.shape[1:])


def half_of(value, bit):
    size = value.shape[-1] // 2
    return lax.dynamic_slice_in_dim(value, bit * size, size, value.ndim - 1)


def local(mesh_shape, clips, visible_idx, masked_idx, loss_counts, *state):
    masters, firsts, seconds = state[:5], state[5:10], state[10:]
    seq_count, tube_count, _ = clips.shape
    seen_count = visible_idx.shape[1]
    hidden_count = masked_idx.shape[1]
    query_rows = -(-hidden_count // BLOCK) * BLOCK
    seen_rows = -(-seen_count // 16) * 16
    rep, shard = mesh_shape["rep"], mesh_shape["shard"]
    links = Links(rep, shard)
    me = lax.axis_index("shard")

    views = [split_view(master, 1, links.ways) for master in masters[:4]]
    blocks = [links.own_block(view).astype(jnp.bfloat16) for view in views]
    vec_own = masters[4].astype(jnp.bfloat16).reshape(1, -1)
    fars = range(1, shard)
    first = Steps(from_owners(links, blocks[:2] + [vec_own], fars))
    counts = Steps(over_all(links, jnp.sum(loss_counts).astype(jnp.float32).reshape(1), jnp.add))

    seen_idx = jnp.pad(visible_idx, ((0, 0), (0, seen_rows - seen_count)), constant_values=-1)
    hidden_idx = jnp.pad(masked_idx, ((0, 0), (0, query_rows - hidden_count)), constant_values=-1)
    seen_pixels = None
    for clip in range(seq_count):
        seen_pixels = pick_rows(clips, seen_idx, seen_rows, clip, "pick_seen", seen_pixels)
    lows = [master.astype(jnp.bfloat16) for master in masters[:4]]
    seen_pixels, lows, hidden_idx, dec_blocks = arrive([first, counts], (seen_pixels, lows, hidden_idx, blocks[2:]))
    enc_came = [came[:2] for came in first.result]
    vec_parts = [came[2] for came in first.result]
    share = Steps(links.spread([block for came in enc_came for block in came], (0, 1) * len(fars), True))
    second = Steps(from_owners(links, dec_blocks, fars))

    pixels = None
    for clip in range(seq_count):
        pixels = pick_rows(clips, hidden_idx, BLOCK, clip, "pick_hidden", pixels)
        if clip == 0:
            pixels, hidden_idx, visible_idx, masked_idx, vec_own, vec_parts = arrive(
                [share, counts, second], (pixels, hidden_idx, visible_idx, masked_idx, vec_own, vec_parts)
            )
    dec_share = Steps(links.spread([block for came in second.result for block in came], (0, 1) * len(fars), True))
    vec = assembled(vec_own, vec_parts, me).reshape(1, -1).astype(jnp.float32)
    token = vec[:, DEC_VEC - DD : DEC_VEC]
    place = (
        jnp.pad(sinusoid_at(visible_idx, D), ((0, 0), (0, seen_rows - seen_count), (0, 0))),
        jnp.concatenate([sinusoid_at(masked_idx, DD) + token, sinusoid_at(visible_idx, DD)], axis=1),
    )
    pixels, place = arrive([share, counts, dec_share], (pixels, place))
    place = arrive([share, counts, dec_share], place)
    flat = lambda whole: whole.reshape(-1, whole.shape[-1])
    enc_low_rows, enc_low_cols = [
        flat(assembled(lows[at], share.result[at :: 2], me)) for at in (0, 1)
    ]
    (enc_h, enc_qkv, enc_mid, enc_inner, encoded, projected, tall, pair, normed_two, latent, left_most) = enc_fwd(
        seen_pixels.reshape(-1, PATCH), place[0].reshape(-1, D), enc_low_rows, enc_low_cols, vec, seq_count, seen_count
    )
    core = links.inner[0]
    left_swap = Steps(one_hop(links, (tall, pair, normed_two), core))
    complete(dec_share)
    projected = arrive([counts], projected)
    count_sum = complete(counts)[0][0]
    dec_low_rows, u_down = [flat(assembled(lows[2 + at], dec_share.result[at::2], me)) for at in (0, 1)]
    (u_qkv, u_out, u_up, _), w_head = dec_parts(dec_low_rows, u_down)

    projected = projected.reshape(seq_count, seen_rows, DD)[:, :seen_count]
    hidden = place[1].at[:, hidden_count:].add(projected)
    qkv = dec_qkv(hidden, u_qkv, vec, tube_count // 2)
    mixed, log_sums = attn_fwd(qkv, DHEADS, query_rows, BLOCK)
    log_sums = arrive([left_swap], log_sums)
    far_lefts = left_swap.result
    (middle_grad, mixed_grad, grad_row_part, grad_dec_fc2, narrow_grads, wide_grads, loss_part) = dec_post(
        loss_counts, (2.0 / (PATCH * count_sum)).reshape(1), hidden, mixed, pixels,
        u_out, u_up, u_down, w_head, vec, BLOCK,
    )
    view = functools.partial(split_view, shard=shard, ways=links.ways)
    dec_flight = Steps(links.reduce([view(grad_row_part), view(grad_dec_fc2)], (None, None), (0, 1), True))
    input_grads, before = [], [jnp.zeros((DD, 3 * DD), jnp.float32), jnp.zeros((8, DD), jnp.float32)]
    parts = [[], []]
    for clip in range(seq_count):
        for pair_at in range(DHEADS // 2):
            parts[clip] += attn_bwd(qkv, mixed_grad, log_sums, DHEADS, query_rows, BLOCK, clip, pair_at)
            log_sums = arrive([dec_flight], log_sums)
        back = dec_qkv_back(
            hidden, parts[clip], middle_grad, u_qkv, vec, hidden_count, tube_count // 2, clip, before
        )
        input_grads.append(back[0])
        before = back[1:]
    grad_qkv, one_grads = before
    dec_sums = complete(dec_flight)[0]

    proj_grad = jnp.concatenate([grad[:, hidden_count:] for grad in input_grads], axis=0)
    proj_grad = jnp.pad(proj_grad, ((0, 0), (0, seen_rows - seen_count), (0, 0))).reshape(-1, DD)
    grad_proj = product_tn(latent, proj_grad)
    late = Steps(links.reduce([view(grad_qkv), view(grad_proj)], (None, None), (0, 1), True))
    proj_grad = arrive([late], proj_grad)
    dec_spread = Steps(links.spread(dec_sums, (0, 1), True))
    grad_down, grad_up, grad_wide, grad_in, enc_sums, up_sums, right_most = enc_bwd(
        proj_grad, enc_h, enc_qkv, enc_mid, enc_inner, encoded, enc_low_rows, enc_low_cols, vec, seq_count, seen_count
    )
    grad_vectors = jnp.concatenate(
        [enc_sums[at] for at in range(6)] + [up_sums[0], enc_sums[6], one_grads[2], one_grads[0], one_grads[1]]
        + [narrow_grads[0], narrow_grads[1], narrow_grads[2], narrow_grads[3], wide_grads[0], narrow_grads[4], wide_grads[1]]
    )

    bit = bit_of(*core)
    grad_up, grad_wide, grad_in, grad_down, right_most, grad_vectors = arrive(
        [late, dec_spread], (grad_up, grad_wide, grad_in, grad_down, right_most, grad_vectors)
    )
    shape_right = lambda b: (
        half_of(grad_up, b)[None],
        jnp.concatenate([half_of(grad_wide[:, : 3 * D], b), half_of(grad_wide[:, 3 * D :], b)], axis=1)[None],
        jnp.stack([half_of(grad_in, b), half_of(grad_down, b)]),
    )
    right_swap = Steps(one_hop(links, shape_right(1 - bit), core))
    rights = shape_right(bit)
    norms = jnp.sqrt(left_most[:5, 0] * right_most[:5, 0])
    bounds = jnp.stack([norms[4], jnp.maximum(norms[2], norms[3]), jnp.maximum(norms[0], norms[1])])
    size = grad_vectors.shape[0]
    is_sum = lax.broadcasted_iota(jnp.int32, (1, size + 128), 1) < size + 1
    message = jnp.concatenate([grad_vectors, loss_part[0], bounds, jnp.zeros(124, jnp.float32)]).reshape(1, -1)
    vector_flight = Steps(over_all(links, message, lambda x, y: jnp.where(is_sum, x + y, jnp.maximum(x, y))))
    rights = arrive([right_swap, vector_flight, late, dec_spread], rights)
    far_rights = right_swap.result
    wide_cols, tall_rows = 2 * D, PATCH + FF
    zero = lambda i, j: (0, 0, i)
    hops = [vector_flight, late, dec_spread]
    sum_up = pair_product(
        (normed_two[None], far_lefts[2][None]), (rights[0], far_rights[0]), D, wide_cols, D, D // 2,
        zero, lambda i, j: (0, 0, j), "grad_up",
    )
    sum_up, rights = arrive(hops, (sum_up, rights))
    sum_wide = pair_product(
        (pair, far_lefts[1]), (rights[1], far_rights[1]), D, wide_cols, D, D // 2,
        lambda i, j: (j // 3, 0, i), lambda i, j: (0, 0, j), "grad_wide",
    )
    sum_wide, rights = arrive(hops, (sum_wide, rights))
    sum_tall = pair_product(
        (tall[None], far_lefts[0][None]), (rights[2], far_rights[2]), tall_rows, D // 2, D, D // 2,
        zero, lambda i, j: (jnp.minimum(i // 2, 1), 0, j), "grad_tall",
    )
    sum_up, sum_wide, sum_tall = arrive(hops, (sum_up, sum_wide, sum_tall))
    totals = complete(*hops)[0]
    vector_sum, loss_sum = totals[0, :size], totals[0, size]
    bounds = totals[0, size + 1 : size + 4] * (2.0 * rep * shard)
    scales = list(jnp.exp2(jnp.floor(15.0 - jnp.log2(jnp.maximum(bounds, 1e-30)))))
    slim = functools.partial(split_view, shard=shard, ways=links.ways - 1)
    enc_flight = Steps(links.reduce([slim(sum_up), slim(sum_wide), slim(sum_tall)], scales, (0, 1, 2), False))
    late_sums = late.result
    late_spread = Steps(links.spread(late_sums, (0, 1), True))
    while enc_flight.result is None:
        arrive([enc_flight, late_spread])
    complete(late_spread)
    enc_parts_sum = enc_flight.result

    lowered = [(part * scale).astype(jnp.float16) for part, scale in zip(enc_parts_sum, scales)]
    enc_spread = Steps(links.spread(lowered, (0, 0, 1), False))
    squares = jnp.float32(0.0)
    for part in enc_parts_sum + dec_sums + late_sums:
        squares = squares + jnp.sum(part * part)
    norm = Steps(over_all(links, squares.reshape(1), jnp.add, links.outer))
    while enc_spread.result is None:
        arrive([norm])
        arrive([norm, enc_spread])
    everyone = complete(norm)[0]
    loss = loss_sum / count_sum
    grad_norm = jnp.sqrt(everyone[0] + jnp.sum(vector_sum * vector_sum))
    factor = jnp.minimum(jnp.float32(1.0), lax.rsqrt(count_sum) / grad_norm)

    flat_piece = lambda piece: piece.reshape(-1, piece.shape[-1])
    dec_rows_sum, dec_fc2_sum, dec_qkv_sum, proj_sum = [
        flat_piece(piece) for piece in dec_spread.result + late_spread.result
    ]
    halves = [flat_piece(piece) for piece in enc_spread.result]
    other = [links.swap(half, core) for half in halves]

    def sided(mine, yours):
        return jnp.where(bit == 0, jnp.concatenate([mine, yours], 1), jnp.concatenate([yours, mine], 1))

    wide_parts = []
    for at, (lo, hi) in enumerate(((0, 3 * D // 2), (3 * D // 2, 2 * D))):
        wide_parts.append(sided(halves[1][:, lo:hi], other[1][:, lo:hi]).astype(jnp.float32) * (1.0 / scales[1]))
    grads = [
        jnp.concatenate(
            wide_parts + [sided(halves[0], other[0]).astype(jnp.float32) * (1.0 / scales[0]), proj_sum], axis=1
        ),
        sided(halves[2], other[2]).astype(jnp.float32) * (1.0 / scales[2]),
        jnp.concatenate([dec_qkv_sum, dec_rows_sum], axis=1),
        dec_fc2_sum,
        lax.dynamic_slice_in_dim(vector_sum, me * masters[4].shape[0], masters[4].shape[0]),
    ]
    new_w, new_m, new_v = [], [], []
    for index in range(5):
        updated = adam_update(masters[index], firsts[index], seconds[index], grads[index] * factor)
        new_w.append(updated[0])
        new_m.append(updated[1])
        new_v.append(updated[2])
    return (loss, grad_norm, *new_w, *new_m, *new_v, *[w.astype(jnp.bfloat16) for w in new_w])


def solution(mesh):
    both, one = ("rep", "shard"), "shard"
    held = (P(one, None), P(one, None), P(one, None), P(one, None), P(one))
    in_specs = (P(both, None, None), P(both, None), P(both, None), P(both)) + held * 3
    out_specs = (P(), P()) + held * 4
    return jax.shard_map(
        functools.partial(local, dict(mesh.shape)),
        mesh=mesh, in_specs=in_specs, out_specs=out_specs, check_vma=False,
    )
```

```python
import functools
import jax
import jax.numpy as jnp
from jax import lax
from jax.experimental import pallas as pl
from jax.experimental.pallas import tpu as pltpu
from jax.sharding import PartitionSpec as P

D = 768
HEADS = 12
FF = 3072
DD = 384
DHEADS = 6
DFF = 1536
PATCH = 1536


beta_one = 0.9
beta_two = 0.95
bias_fix_one = 1.0 - 0.9**10
bias_fix_two = 1.0 - 0.95**10
learn_rate = 0.02
decay_rate = 0.05
adam_eps = 1e-12
norm_eps = 1e-06


def product_of(left, right):
    return jnp.dot(left, right, preferred_element_type=jnp.float32)


def product_tn(left, right):
    return jnp.dot(left.T, right, preferred_element_type=jnp.float32)


f32, bf16 = jnp.float32, jnp.bfloat16
LOG2E = 1.4426950408889634
NT = (((1,), (1,)), ((), ()))
NN = (((1,), (0,)), ((), ()))
TN = (((0,), (0,)), ((), ()))
def dot(a, b, dims): return lax.dot_general(a, b, dims, preferred_element_type=f32)

def cost(micros, moved=0):
    return pl.CostEstimate(flops=int(micros * 1.1e9), transcendentals=0, bytes_accessed=moved)

def fwd_body(scale, q_ref, k_ref, v_ref, o_ref, lse_ref):
    q = q_ref[0]; k = k_ref[0]; v = v_ref[0]
    lane = lax.broadcasted_iota(jnp.int32, (1, 128), 1)
    outs = []
    for h in range(2):
        own = (lane < 64) if h == 0 else (lane >= 64)
        qh = jnp.where(own, q, jnp.zeros_like(q))
        s = dot(k, qh, NT)
        peak = jnp.max(s, axis=0, keepdims=True)
        e = jnp.exp2((s - peak) * (scale * LOG2E))
        tot = jnp.sum(e, axis=0, keepdims=True)
        p = (e * (1.0 / tot)).astype(bf16)
        outs.append(dot(p, v, TN))
        lse_ref[0, 0, h:h+1, :] = peak * (scale * LOG2E) + jnp.log2(tot)
    o_ref[0] = jnp.where(lane < 64, outs[0], outs[1]).astype(bf16)

def attn_fwd(qkv, heads, rows, bq):
    clips, keys, w3 = qkv.shape
    pairs = heads // 2
    nb = rows // bq
    body = functools.partial(fwd_body, 64 ** -0.5)
    return pl.pallas_call(
        body, grid=(clips, pairs, nb),
        in_specs=[pl.BlockSpec((1, bq, 128), lambda c, p, i: (c, i, p)),
                  pl.BlockSpec((1, keys, 128), lambda c, p, i: (c, 0, pairs + p)),
                  pl.BlockSpec((1, keys, 128), lambda c, p, i: (c, 0, 2 * pairs + p))],
        out_specs=[pl.BlockSpec((1, bq, 128), lambda c, p, i: (c, i, p)),
                   pl.BlockSpec((1, 1, 2, bq), lambda c, p, i: (c * pairs + p, i, 0, 0))],
        out_shape=[jax.ShapeDtypeStruct((clips, rows, w3 // 3), bf16),
                   jax.ShapeDtypeStruct((clips * pairs, nb, 2, bq), f32)],
        compiler_params=pltpu.CompilerParams(vmem_limit_bytes=60 << 20), name="dec_attend_forward", cost_estimate=cost(65),
    )(qkv, qkv, qkv)

def bwd_body(scale, nb, mode, q_ref, k_ref, v_ref, do_ref, lse_ref, dq_ref, dk_ref, dv_ref, dk_acc, dv_acc, kt_ref):
    i = pl.program_id(2)
    q = q_ref[0]; k = k_ref[0]; v = v_ref[0]; do = do_ref[0]
    lane = lax.broadcasted_iota(jnp.int32, (1, 128), 1)
    if mode == 1:
        @pl.when(i == 0)
        def _(): kt_ref[...] = k.T
    dk = dv = None
    dqs = []
    for h in range(2):
        own = (lane < 64) if h == 0 else (lane >= 64)
        qh = jnp.where(own, q, jnp.zeros_like(q))
        doh = jnp.where(own, do, jnp.zeros_like(do))
        s = dot(k, qh, NT)
        dp = dot(v, doh, NT)
        p = jnp.exp2(s * (scale * LOG2E) - lse_ref[0, 0, h:h+1, :])
        pd = p * dp
        delta = jnp.sum(pd, axis=0, keepdims=True)
        ds = (p * (dp - delta)).astype(bf16)
        a = dot(p.astype(bf16), doh, NN)
        b = dot(ds, qh, NN)
        dv = a if dv is None else dv + a
        dk = b if dk is None else dk + b
        if mode == 0:
            dqs.append(dot(ds, k, TN))
        else:
            dqs.append(dot(kt_ref[h*64:(h+1)*64, :], ds, NN))
    if mode == 0:
        dq = jnp.where(lane < 64, dqs[0], dqs[1])
    else:
        dq = jnp.concatenate(dqs, axis=0).T
    bq = q.shape[0]
    dq_ref[0, pl.ds(pl.multiple_of(i * bq, bq), bq), :] = (dq * scale).astype(bf16)
    @pl.when(i == nb - 1)
    def _():
        keys = k.shape[0]
        if nb * bq < keys:
            dq_ref[0, nb * bq:keys, :] = jnp.zeros((keys - nb * bq, 128), bf16)
    @pl.when(i == 0)
    def _():
        dk_acc[...] = dk; dv_acc[...] = dv
    @pl.when(i > 0)
    def _():
        dk_acc[...] += dk; dv_acc[...] += dv
    @pl.when(i == nb - 1)
    def _():
        dk_ref[0] = (dk_acc[...] * scale).astype(bf16)
        dv_ref[0] = dv_acc[...].astype(bf16)

def attn_bwd(qkv, do, lse, heads, rows, bq, clip, pair):
    clips, keys, w3 = qkv.shape
    pairs = heads // 2
    nb = rows // bq
    return pl.pallas_call(
        functools.partial(bwd_body, 64 ** -0.5, nb, 0), grid=(1, 1, nb),
        in_specs=[pl.BlockSpec((1, bq, 128), lambda c, p, i: (clip, i, pair)),
                  pl.BlockSpec((1, keys, 128), lambda c, p, i: (clip, 0, pairs + pair)),
                  pl.BlockSpec((1, keys, 128), lambda c, p, i: (clip, 0, 2 * pairs + pair)),
                  pl.BlockSpec((1, bq, 128), lambda c, p, i: (clip, i, pair)),
                  pl.BlockSpec((1, 1, 2, bq), lambda c, p, i: (clip * pairs + pair, i, 0, 0))],
        out_specs=[pl.BlockSpec((1, keys, 128), lambda c, p, i: (0, 0, 0))] * 3,
        out_shape=[jax.ShapeDtypeStruct((1, keys, 128), bf16)] * 3,
        scratch_shapes=[pltpu.VMEM((keys, 128), f32), pltpu.VMEM((keys, 128), f32), pltpu.VMEM((128, keys), bf16)],
        compiler_params=pltpu.CompilerParams(vmem_limit_bytes=60 << 20), name=f"dec_attend_backward_{clip}_{pair}",
        cost_estimate=cost(17),
    )(qkv, qkv, qkv, do, lse)
DEC_VEC = 6 * D + FF + D + DD

def ln(x):
    c = x - jnp.mean(x, axis=1, keepdims=True)
    inv = lax.rsqrt(jnp.mean(c * c, axis=1, keepdims=True) + norm_eps)
    return c * inv, inv

def ln_back(up, scaled, inv, gain):
    w = up * gain
    return inv * (w - jnp.mean(w, axis=1, keepdims=True) - scaled * jnp.mean(w * scaled, axis=1, keepdims=True))

def col(x): return jnp.sum(x, axis=0, keepdims=True)

def gelu_parts(x):
    cdf = 0.5 * (1.0 + lax.erf(x * 0.7071067811865476))
    return x * cdf, cdf + x * jnp.exp(-0.5 * x * x) * 0.3989422804014327

def post_body(nb, rows, keys, cnt_ref, inv_ref, h_ref, o_ref, t_ref, wout_ref, wup_ref, wdown_ref, whead_ref,
              v_ref, dmid_ref, do_ref, grow_ref, gdown_ref, s384_ref, s1536_ref, loss_ref, gdown_acc):
    c = pl.program_id(0); i = pl.program_id(1)
    first = jnp.logical_and(c == 0, i == 0)
    @pl.when(first)
    def _():
        for r in (grow_ref, gdown_acc, s384_ref, s1536_ref, loss_ref):
            r[...] = jnp.zeros_like(r)
    R = rows
    h = h_ref[0]; o = o_ref[0]
    w, ff = h.shape[1], wup_ref.shape[1]
    gain2, bias2, gainf, biasf = (v_ref[:, DEC_VEC + j * DD:DEC_VEC + (j + 1) * DD] for j in range(2, 6))
    bup = v_ref[:, DEC_VEC + 6 * DD:DEC_VEC + 6 * DD + DFF]
    bdown = v_ref[:, DEC_VEC + 6 * DD + DFF:DEC_VEC + 7 * DD + DFF]
    bhead = v_ref[:, DEC_VEC + 7 * DD + DFF:]
    h1 = h + dot(o, wout_ref[...], NN)
    sc2, inv2 = ln(h1)
    m = (sc2 * gain2 + bias2).astype(bf16)
    inner = dot(m, wup_ref[...], NN) + bup
    act, slope = gelu_parts(inner)
    act = act.astype(bf16)
    out = h1 + (dot(act, wdown_ref[...], NN) + bdown)
    scf, invf = ln(out)
    fin = (scf * gainf + biasf).astype(bf16)
    pred = dot(fin, whead_ref[...], NN) + bhead
    t = t_ref[0].astype(f32)
    tc = t - jnp.mean(t, axis=1, keepdims=True)
    err = pred - tc * lax.rsqrt(jnp.mean(tc * tc, axis=1, keepdims=True) + norm_eps)
    row = lax.broadcasted_iota(jnp.int32, (R, 1), 0) + i * R
    live = (row < cnt_ref[c]).astype(f32)
    rl = jnp.mean(err * err, axis=1, keepdims=True) * live
    loss_ref[...] += jnp.sum(rl).reshape(1, 1)
    pg32 = err * (live * inv_ref[0])
    pg = pg32.astype(bf16)
    grow_ref[:, w + ff:] += dot(fin, pg, TN)
    dfin = dot(pg, whead_ref[...], NT)
    s1536_ref[1:2, :] += col(pg.astype(f32))
    s384_ref[2:3, :] += col(dfin * scf)
    s384_ref[3:4, :] += col(dfin)
    dout = ln_back(dfin, scf, invf, gainf)
    dl = dout.astype(bf16)
    gdown_acc[...] += dot(dl, act, TN)
    s384_ref[4:5, :] += col(dl.astype(f32))
    din = (dot(dl, wdown_ref[...], NT) * slope).astype(bf16)
    grow_ref[:, w:w + ff] += dot(m, din, TN)
    s1536_ref[0:1, :] += col(din.astype(f32))
    dm = dot(din, wup_ref[...], NT)
    s384_ref[0:1, :] += col(dm * sc2)
    s384_ref[1:2, :] += col(dm)
    dmid = dout + ln_back(dm, sc2, inv2, gain2)
    bl = dmid.astype(bf16)
    grow_ref[:, :w] += dot(o, bl, TN)
    do_ref[0] = dot(bl, wout_ref[...], NT).astype(bf16)
    dmid_ref[0, pl.ds(pl.multiple_of(i * R, R), R), :] = dmid
    @pl.when(i == nb - 1)
    def _():
        dmid_ref[0, nb * R:keys, :] = jnp.zeros((keys - nb * R, dmid.shape[1]), f32)
    @pl.when(jnp.logical_and(c == pl.num_programs(0) - 1, i == nb - 1))
    def _():
        gdown_ref[...] = gdown_acc[...].T

def dec_post(counts, inv, h, o, t, wout, wup, wdown, whead, vec, R):
    clips, keys, w = h.shape
    rows = o.shape[1]; nb = rows // R
    ff, px = wup.shape[1], whead.shape[1]
    full = lambda a: pl.BlockSpec(a.shape, lambda c, i: (0,) * len(a.shape))
    sm = pl.BlockSpec(memory_space=pltpu.SMEM)
    outs = [jax.ShapeDtypeStruct((clips, keys, w), f32), jax.ShapeDtypeStruct((clips, rows, w), bf16),
            jax.ShapeDtypeStruct((w, w + ff + px), f32), jax.ShapeDtypeStruct((ff, w), f32), jax.ShapeDtypeStruct((8, w), f32), jax.ShapeDtypeStruct((8, ff), f32),
            jax.ShapeDtypeStruct((1, 1), f32)]
    blk = lambda n: pl.BlockSpec((1, R, n), lambda c, i: (c, i, 0))
    return pl.pallas_call(
        functools.partial(post_body, nb, R, keys), grid=(clips, nb),
        in_specs=[sm, sm, blk(w), blk(w), blk(px), full(wout), full(wup), full(wdown), full(whead), full(vec)],
        out_specs=[pl.BlockSpec((1, keys, w), lambda c, i: (c, 0, 0)), blk(w)] + [full(x) for x in outs[2:]],
        out_shape=outs, compiler_params=pltpu.CompilerParams(vmem_limit_bytes=62 << 20), name="dec_post",
        scratch_shapes=[pltpu.VMEM((w, ff), f32)], cost_estimate=cost(67),
    )(counts, inv, h, o, t, wout, wup, wdown, whead, vec)

def qkv_body(h_ref, w_ref, v_ref, o_ref):
    s, _ = ln(h_ref[0])
    a = (s * v_ref[:, DEC_VEC:DEC_VEC + DD] + v_ref[:, DEC_VEC + DD:DEC_VEC + 2 * DD]).astype(bf16)
    o_ref[0] = dot(a, w_ref[...], NN).astype(bf16)

def dec_qkv(h, w, v, R):
    clips, keys, d = h.shape
    full = lambda a: pl.BlockSpec(a.shape, lambda c, i: (0,) * len(a.shape))
    return pl.pallas_call(qkv_body, grid=(clips, keys // R),
        in_specs=[pl.BlockSpec((1, R, d), lambda c, i: (c, i, 0)), full(w), full(v)],
        out_specs=pl.BlockSpec((1, R, w.shape[1]), lambda c, i: (c, i, 0)),
        out_shape=jax.ShapeDtypeStruct((clips, keys, w.shape[1]), bf16),
        compiler_params=pltpu.CompilerParams(vmem_limit_bytes=60 << 20), name="dec_qkv", cost_estimate=cost(9))(h, w, v)

def qkvb_body(R, masked, h_ref, dmid_ref, w_ref, v_ref, gi_ref, si_ref, *refs):
    parts, (dh_ref, g_ref, s_ref) = refs[:9], refs[9:]
    i = pl.program_id(0)
    @pl.when(i == 0)
    def _():
        g_ref[...] = gi_ref[...]; s_ref[...] = si_ref[...]
    d = h_ref.shape[2]
    s, inv = ln(h_ref[0])
    gain = v_ref[:, DEC_VEC:DEC_VEC + DD]
    a = (s * gain + v_ref[:, DEC_VEC + DD:DEC_VEC + 2 * DD]).astype(bf16)
    da = None
    for j in range(3):
        x = jnp.concatenate([parts[3 * p + j][0] for p in range(3)], axis=1)
        g_ref[:, j * d:(j + 1) * d] += dot(a, x, TN)
        y = dot(x, w_ref[:, j * d:(j + 1) * d], NT)
        da = y if da is None else da + y
    s_ref[0:1, :] += col(da * s)
    s_ref[1:2, :] += col(da)
    dh = dmid_ref[0] + ln_back(da, s, inv, gain)
    row = lax.broadcasted_iota(jnp.int32, (R, 1), 0) + i * R
    s_ref[2:3, :] += col(jnp.where(row < masked, dh, 0.0))
    dh_ref[0] = dh.astype(bf16)

def dec_qkv_back(h, parts, dmid, w, v, masked, R, clip, before):
    clips, keys, d = h.shape
    full = lambda a: pl.BlockSpec(a.shape, lambda i: (0,) * len(a.shape))
    blk = pl.BlockSpec((1, R, d), lambda i: (clip, i, 0))
    part = pl.BlockSpec((1, R, 128), lambda i: (0, i, 0))
    outs = [jax.ShapeDtypeStruct((1, keys, d), bf16), jax.ShapeDtypeStruct((d, 3 * d), f32), jax.ShapeDtypeStruct((8, d), f32)]
    return pl.pallas_call(functools.partial(qkvb_body, R, masked), grid=(keys // R,),
        in_specs=[blk, blk, full(w), full(v), full(outs[1]), full(outs[2])] + [part] * 9,
        out_specs=[pl.BlockSpec((1, R, d), lambda i: (0, i, 0)), full(outs[1]), full(outs[2])], out_shape=outs,
        compiler_params=pltpu.CompilerParams(vmem_limit_bytes=60 << 20), name=f"dec_qkv_back_{clip}",
        cost_estimate=cost(10))(h, dmid, w, v, *before, *parts)

def pick_body(idx_ref, x_ref, *refs):
    n = x_ref.shape[1]
    hot = (idx_ref[0] == lax.broadcasted_iota(jnp.int32, (1, n), 1)).astype(f32).astype(bf16)
    refs[-1][0] = dot(hot, x_ref[0], NN).astype(bf16)

def pick_rows(x, idx, R, clip, name, into=None):
    clips, n, w = x.shape
    m = idx.shape[1]
    more = [] if into is None else [into]
    return pl.pallas_call(pick_body, grid=(m // R,),
        in_specs=[pl.BlockSpec((1, R, 1), lambda i: (clip, i, 0)), pl.BlockSpec((1, n, w), lambda i: (clip, 0, 0))]
        + [pl.BlockSpec(memory_space=pl.ANY)] * len(more),
        out_specs=pl.BlockSpec((1, R, w), lambda i: (clip, i, 0)),
        out_shape=jax.ShapeDtypeStruct((clips, m, w), bf16), cost_estimate=cost(m / 140),
        input_output_aliases={2: 0} if more else {},
        compiler_params=pltpu.CompilerParams(vmem_limit_bytes=60 << 20), name=f"{name}_{clip}")(idx[:, :, None], x, *more)

QKV, OUT, UP, PROJ = slice(0, 3 * D), slice(3 * D, 4 * D), slice(4 * D, 4 * D + FF), slice(4 * D + FF, 4 * D + FF + DD)

def enc_vec(v_ref, at):
    starts = [0, D, 2 * D, 3 * D, 4 * D, 5 * D, 6 * D, 6 * D + FF]
    return v_ref[:, starts[at]:starts[at] + (FF if at == 6 else D)]

def most(x):
    x = x.astype(f32)
    return jnp.max(jnp.sum(x * x, axis=0, keepdims=True))

def enc_scores(qkv_ref, rows, p, h, seen):
    lane = lax.broadcasted_iota(jnp.int32, (1, 128), 1)
    own = (lane < 64) if h == 0 else (lane >= 64)
    q = qkv_ref[rows, p * 128:(p + 1) * 128]
    k = qkv_ref[rows, D + p * 128:D + (p + 1) * 128]
    v = qkv_ref[rows, 2 * D + p * 128:2 * D + (p + 1) * 128]
    qh = jnp.where(own, q, jnp.zeros_like(q))
    s = dot(qh, k, NT)
    s = jnp.where(lax.broadcasted_iota(jnp.int32, (1, s.shape[1]), 1) < seen, s, -3e38)
    peak = jnp.max(s, axis=1, keepdims=True)
    e = jnp.exp2((s - peak) * (0.125 * LOG2E))
    return q, k, v, qh, own, e * (1.0 / jnp.sum(e, axis=1, keepdims=True))

def fetches(at_ref, sources, whole, sems):
    rows = sources[0].shape[0]
    copies = [(sources[0], at_ref[0] * rows)]
    for far in range((len(sources) - 1) // 2):
        for side in range(2):
            start = at_ref[2 + far] * rows + (at_ref[1] if side == 0 else 1 - at_ref[1]) * (rows // 2)
            copies.append((sources[1 + 2 * far + side], start))
    return [
        pltpu.make_async_copy(source, whole.at[pl.ds(pl.multiple_of(start, 16), source.shape[0])], sems.at[k])
        for k, (source, start) in enumerate(copies)
    ]

def enc_fwd_body(clips, seen, count, at_ref, x_ref, pos_ref, v_ref, *refs):
    row_sources, col_sources = refs[:count], refs[count:2 * count]
    (h_ref, qkv_ref, h1_ref, inner_ref, enc_ref, proj_ref, tall_ref, pair_ref, m_ref, lat_ref, most_ref,
     wr_ref, wc_ref, row_sems, col_sems) = refs[2 * count:]
    col_copies = fetches(at_ref, col_sources, wc_ref, col_sems)
    row_copies = fetches(at_ref, row_sources, wr_ref, row_sems)
    for copy in col_copies + row_copies: copy.start()
    for copy in col_copies: copy.wait()
    enc_fwd_math(clips, seen, row_copies, x_ref, pos_ref, wr_ref, wc_ref, v_ref, h_ref, qkv_ref, h1_ref, inner_ref,
                 enc_ref, proj_ref, tall_ref, pair_ref, m_ref, lat_ref, most_ref)

def enc_fwd_math(clips, seen, row_copies, x_ref, pos_ref, wr_ref, wc_ref, v_ref,
                 h_ref, qkv_ref, h1_ref, inner_ref, enc_ref, proj_ref, tall_ref, pair_ref, m_ref, lat_ref, most_ref):
    x = x_ref[...]
    h = dot(x, wc_ref[:PATCH], NN) + pos_ref[...]
    h_ref[...] = h
    s1, _ = ln(h)
    a = (s1 * enc_vec(v_ref, 0) + enc_vec(v_ref, 1)).astype(bf16)
    pair_ref[0] = a
    for copy in row_copies: copy.wait()
    qkv_ref[...] = dot(a, wr_ref[:, QKV], NN).astype(bf16)
    n = h.shape[0] // clips
    for c in range(clips):
        rows = slice(c * n, (c + 1) * n)
        for p in range(HEADS // 2):
            outs = []
            for hd in range(2):
                q, k, v, qh, own, prob = enc_scores(qkv_ref, rows, p, hd, seen)
                outs.append(dot(prob.astype(bf16), v, NN))
            lane = lax.broadcasted_iota(jnp.int32, (1, 128), 1)
            pair_ref[1, rows, p * 128:(p + 1) * 128] = jnp.where(lane < 64, outs[0], outs[1]).astype(bf16)
    o = pair_ref[1]
    h1 = h + dot(o, wr_ref[:, OUT], NN)
    h1_ref[...] = h1
    s2, _ = ln(h1)
    m = (s2 * enc_vec(v_ref, 2) + enc_vec(v_ref, 3)).astype(bf16)
    m_ref[...] = m
    inner = dot(m, wr_ref[:, UP], NN) + enc_vec(v_ref, 6)
    inner_ref[...] = inner
    act = gelu_parts(inner)[0].astype(bf16)
    out = h1 + (dot(act, wc_ref[PATCH:], NN) + enc_vec(v_ref, 7))
    enc_ref[...] = out
    sf, _ = ln(out)
    lat = (sf * enc_vec(v_ref, 4) + enc_vec(v_ref, 5)).astype(bf16)
    lat_ref[...] = lat
    proj_ref[...] = dot(lat, wr_ref[:, PROJ], NN)
    tall_ref[:, :PATCH] = x
    tall_ref[:, PATCH:] = act
    for at, y in enumerate((x, act, a, o, m)):
        most_ref[at:at + 1, :] = jnp.broadcast_to(most(y).reshape(1, 1), (1, 128))

def whole(shape): return pl.BlockSpec(shape, lambda: (0,) * len(shape))

def weight_scratch(row_sources, col_sources, shard):
    scratch = [pltpu.VMEM((shard * s[0].shape[0], s[0].shape[1]), bf16) for s in (row_sources, col_sources)]
    return scratch + [pltpu.SemaphoreType.DMA((len(row_sources),))] * 2

def enc_fwd(at, x, pos, vec, row_sources, col_sources, clips, seen, shard):
    n = x.shape[0]
    shapes = [((n, D), f32), ((n, 3 * D), bf16), ((n, D), f32), ((n, FF), f32), ((n, D), f32), ((n, DD), f32),
              ((n, PATCH + FF), bf16), ((2, n, D), bf16), ((n, D), bf16), ((n, D), bf16), ((8, 128), f32)]
    count = len(row_sources)
    return pl.pallas_call(functools.partial(enc_fwd_body, clips, seen, count),
        in_specs=[pl.BlockSpec(memory_space=pltpu.SMEM)] + [whole(a.shape) for a in (x, pos, vec)]
        + [pl.BlockSpec(memory_space=pl.ANY)] * (2 * count),
        out_specs=[whole(s) for s, _ in shapes], out_shape=[jax.ShapeDtypeStruct(s, d) for s, d in shapes],
        scratch_shapes=weight_scratch(row_sources, col_sources, shard),
        compiler_params=pltpu.CompilerParams(vmem_limit_bytes=62 << 20), name="enc_forward", cost_estimate=cost(19),
    )(at, x, pos, vec, *row_sources, *col_sources)

def enc_bwd_body(clips, seen, count, at_ref, dp_ref, h_ref, qkv_ref, h1_ref, inner_ref, enc_ref, v_ref, *refs):
    row_sources, col_sources = refs[:count], refs[count:2 * count]
    (gdown_ref, gup_ref, gwide_ref, gin_ref, s_ref, sup_ref, most_ref, wr_ref, wc_ref, row_sems, col_sems) = refs[2 * count:]
    row_copies = fetches(at_ref, row_sources, wr_ref, row_sems)
    col_copies = fetches(at_ref, col_sources, wc_ref, col_sems)
    for copy in row_copies + col_copies: copy.start()
    for copy in row_copies: copy.wait()
    sf, invf = ln(enc_ref[...])
    up = dot(dp_ref[...], wr_ref[:, PROJ], NT)
    s_ref[4:5, :] = col(up * sf); s_ref[5:6, :] = col(up)
    dout = ln_back(up, sf, invf, enc_vec(v_ref, 4))
    dl = dout.astype(bf16)
    gdown_ref[...] = dl
    s_ref[6:7, :] = col(dl.astype(f32))
    for copy in col_copies: copy.wait()
    din = (dot(dl, wc_ref[PATCH:], NT) * gelu_parts(inner_ref[...])[1]).astype(bf16)
    gup_ref[...] = din
    sup_ref[...] = col(din.astype(f32))
    dm = dot(din, wr_ref[:, UP], NT)
    s2, inv2 = ln(h1_ref[...])
    s_ref[2:3, :] = col(dm * s2); s_ref[3:4, :] = col(dm)
    dmid = dout + ln_back(dm, s2, inv2, enc_vec(v_ref, 2))
    bl = dmid.astype(bf16)
    gwide_ref[:, 3 * D:] = bl
    do = dot(bl, wr_ref[:, OUT], NT).astype(bf16)
    n = do.shape[0] // clips
    for c in range(clips):
        rows = slice(c * n, (c + 1) * n)
        for p in range(HEADS // 2):
            dop = do[rows, p * 128:(p + 1) * 128]
            dqs, dk, dv = [], None, None
            for hd in range(2):
                q, k, v, qh, own, prob = enc_scores(qkv_ref, rows, p, hd, seen)
                doh = jnp.where(own, dop, jnp.zeros_like(dop))
                dpr = dot(doh, v, NT)
                ds = (prob * (dpr - jnp.sum(dpr * prob, axis=1, keepdims=True))).astype(bf16)
                dqs.append(dot(ds, k, NN))
                x, y = dot(ds, qh, TN), dot(prob.astype(bf16), doh, TN)
                dk = x if dk is None else dk + x
                dv = y if dv is None else dv + y
            lane = lax.broadcasted_iota(jnp.int32, (1, 128), 1)
            dq = jnp.where(lane < 64, dqs[0], dqs[1])
            gwide_ref[rows, p * 128:(p + 1) * 128] = (dq * 0.125).astype(bf16)
            gwide_ref[rows, D + p * 128:D + (p + 1) * 128] = (dk * 0.125).astype(bf16)
            gwide_ref[rows, 2 * D + p * 128:2 * D + (p + 1) * 128] = dv.astype(bf16)
    da = dot(gwide_ref[:, :3 * D], wr_ref[:, QKV], NT)
    s1, inv1 = ln(h_ref[...])
    s_ref[0:1, :] = col(da * s1); s_ref[1:2, :] = col(da)
    s_ref[7:8, :] = jnp.zeros_like(s_ref[7:8, :])
    gin = (dmid + ln_back(da, s1, inv1, enc_vec(v_ref, 0))).astype(bf16)
    gin_ref[...] = gin
    for at, y in enumerate((gin, dl, gwide_ref[:, :3 * D], bl, din)):
        most_ref[at:at + 1, :] = jnp.broadcast_to(most(y).reshape(1, 1), (1, 128))

def enc_bwd(at, dp, h, qkv, h1, inner, enc, vec, row_sources, col_sources, clips, seen, shard):
    n = h.shape[0]
    shapes = [((n, D), bf16), ((n, FF), bf16), ((n, 4 * D), bf16), ((n, D), bf16), ((8, D), f32), ((1, FF), f32), ((8, 128), f32)]
    ins = (dp, h, qkv, h1, inner, enc, vec)
    count = len(row_sources)
    return pl.pallas_call(functools.partial(enc_bwd_body, clips, seen, count),
        in_specs=[pl.BlockSpec(memory_space=pltpu.SMEM)] + [whole(a.shape) for a in ins]
        + [pl.BlockSpec(memory_space=pl.ANY)] * (2 * count),
        out_specs=[whole(s) for s, _ in shapes], out_shape=[jax.ShapeDtypeStruct(s, d) for s, d in shapes],
        scratch_shapes=weight_scratch(row_sources, col_sources, shard),
        compiler_params=pltpu.CompilerParams(vmem_limit_bytes=62 << 20), name="enc_backward", cost_estimate=cost(27),
    )(at, *ins, *row_sources, *col_sources)

def pair_body(al_ref, bl_ref, ar_ref, br_ref, o_ref):
    o_ref[...] = dot(al_ref[0], ar_ref[0], TN) + dot(bl_ref[0], br_ref[0], TN)

def pair_product(lefts, rights, rows, cols, bm, bn, left_at, right_at, name):
    n = lefts[0].shape[1]
    ls = pl.BlockSpec((1, n, bm), lambda i, j: left_at(i, j))
    rs = pl.BlockSpec((1, n, bn), lambda i, j: right_at(i, j))
    return pl.pallas_call(pair_body, grid=(rows // bm, cols // bn), in_specs=[ls, ls, rs, rs],
        out_specs=pl.BlockSpec((bm, bn), lambda i, j: (i, j)), out_shape=jax.ShapeDtypeStruct((rows, cols), f32),
        compiler_params=pltpu.CompilerParams(vmem_limit_bytes=60 << 20), name=name,
        cost_estimate=cost(8),
    )(lefts[0], lefts[1], rights[0], rights[1])
def dec_parts(dec_low_rows, dec_low_fc2):
    mats = (
        dec_low_rows[:, : 3 * DD],
        dec_low_rows[:, 3 * DD : 4 * DD],
        dec_low_rows[:, 4 * DD : 4 * DD + DFF],
        dec_low_fc2,
    )
    return (mats, dec_low_rows[:, 4 * DD + DFF :])


def adam_update(master, moment_one, moment_two, gradient):
    new_one = beta_one * moment_one + (1.0 - beta_one) * gradient
    new_two = beta_two * moment_two + (1.0 - beta_two) * gradient * gradient
    stepped = new_one / bias_fix_one / (jnp.sqrt(new_two / bias_fix_two) + adam_eps)
    return (master - learn_rate * (stepped + decay_rate * master), new_one, new_two)


BLOCK = 720


def sinusoid_at(places, feat_width):
    column = jnp.arange(feat_width)
    expo = (2 * (column // 2)).astype(jnp.float32) / feat_width
    angles = places.astype(jnp.float32)[..., None] / jnp.power(jnp.float32(10000.0), expo)
    turns = jnp.round(angles * 0.6366197723675814)
    r = ((angles - turns * 1.5703125) - turns * 4.837512969970703125e-4) - turns * 7.54978995489188216e-8
    z = r * r
    sine = ((-1.9515295891e-4 * z + 8.3321608736e-3) * z - 1.6666654611e-1) * z * r + r
    cosine = ((2.443315711809948e-5 * z - 1.388731625493765e-3) * z + 4.166664568298827e-2) * z * z - 0.5 * z + 1.0
    quarter = turns.astype(jnp.int32) + column % 2
    value = jnp.where(quarter % 2 == 0, sine, cosine)
    return jnp.where(quarter % 4 < 2, value, -value)


def bit_of(name, hop):
    return (lax.axis_index(name) // hop) % 2


def swap(value, name, size, hop):
    return lax.ppermute(value, name, [(i, i ^ hop) for i in range(size)])


def total_everywhere(value, sizes, combine=jnp.add):
    for name, size in sizes:
        hop = 1
        while hop < size:
            value = combine(value, swap(value, name, size, hop))
            hop *= 2
    return value


def keep_and_send(value, dim, bit):
    half = value.shape[dim] // 2
    kept = lax.dynamic_slice_in_dim(value, bit * half, half, dim)
    sent = lax.dynamic_slice_in_dim(value, (1 - bit) * half, half, dim)
    return kept, sent


def join(mine, other, dim, bit):
    return jnp.where(
        bit == 0, jnp.concatenate([mine, other], axis=dim), jnp.concatenate([other, mine], axis=dim)
    )


def split_view(value, shard, ways):
    rows = value.shape[0] // shard
    return value.reshape((shard,) + (2,) * ways + (rows >> ways, value.shape[1]))


class Links:
    def __init__(self, rep, shard):
        self.rep, self.shard = rep, shard
        self.ways = min(3, rep.bit_length() - 1)
        self.inner = [("rep", 1 << k) for k in range(self.ways)]
        self.outer = [("rep", 1 << k) for k in range(self.ways, rep.bit_length() - 1)]
        self.owners = [("shard", 1 << k) for k in reversed(range(shard.bit_length() - 1))]
        self.sizes = (("rep", rep), ("shard", shard))

    def size(self, name):
        return self.rep if name == "rep" else self.shard

    def swap(self, value, hop):
        return swap(value, hop[0], self.size(hop[0]), hop[1])

    def dim(self, hop, core):
        return 0 if hop[0] == "shard" else hop[1].bit_length() - (not core)

    def reduce(self, parts, scales, turns, core):
        parts = list(parts)
        first = self.inner[:1] if core else []
        rest = self.inner[1:] + self.owners[:1]
        orders = []
        for turn in turns:
            turn = turn % len(rest)
            orders.append(first + rest[turn:] + rest[:turn] + self.owners[1:])
        for step in range(len(orders[0])):
            held, moving = [], []
            for part, scale, order in zip(parts, scales, orders):
                hop = order[step]
                kept, sent = keep_and_send(part, self.dim(hop, core), bit_of(*hop))
                if scale is not None:
                    sent = (sent * scale).astype(jnp.float16)
                held.append(kept)
                moving.append(self.swap(sent, hop))
            moving = yield moving
            for at, (kept, came) in enumerate(zip(held, moving)):
                if scales[at] is not None:
                    came = came.astype(jnp.float32) * (1.0 / scales[at])
                parts[at] = kept + came
        for hop in self.outer:
            mine = [
                part if scale is None else lax.optimization_barrier((part * scale).astype(jnp.float16))
                for part, scale in zip(parts, scales)
            ]
            other = yield [self.swap(part, hop) for part in mine]
            for at, scale in enumerate(scales):
                if scale is None:
                    parts[at] = mine[at] + other[at]
                else:
                    both = mine[at].astype(jnp.float32) + other[at].astype(jnp.float32)
                    parts[at] = both * (1.0 / scale)
        return parts

    def spread(self, pieces, turns, core, across=None):
        pieces = list(pieces)
        rest = self.inner[1:]
        orders = []
        for turn in turns:
            turn = turn % len(rest) if rest else 0
            orders.append(rest[turn:] + rest[:turn] + (self.inner[:1] if (core if across is None else across) else []))
        for step in range(len(orders[0])):
            moving = yield [self.swap(piece, order[step]) for piece, order in zip(pieces, orders)]
            pieces = [
                join(piece, came, self.dim(order[step], core), bit_of(*order[step]))
                for piece, came, order in zip(pieces, moving, orders)
            ]
        return pieces

    def own_block(self, view):
        for hop in self.inner:
            view, _ = keep_and_send(view, self.dim(hop, True), bit_of(*hop))
        return view


class Steps:
    def __init__(self, generator):
        self.generator, self.flight, self.result = generator, None, None
        self.step()

    def step(self):
        if self.result is None:
            try:
                self.flight = self.generator.send(self.flight)
            except StopIteration as end:
                self.flight, self.result = None, end.value


def arrive(steps, value=()):
    steps = [each for each in steps if each.result is None]
    value, flights = lax.optimization_barrier((value, [each.flight for each in steps]))
    for each, flight in zip(steps, flights):
        each.flight = flight
        each.step()
    return value


def complete(*steps):
    while any(each.result is None for each in steps):
        arrive(steps)
    return [each.result for each in steps]


def one_hop(links, values, hop):
    return (yield [links.swap(value, hop) for value in values])


def over_all(links, value, combine, hops):
    for hop in hops:
        if isinstance(hop[0], tuple):
            near, far = hop
            both = (near[0], near[1] ^ far[1])
            came = yield [links.swap(value, each) for each in (near, far, both)]
            value = combine(combine(value, came[0]), combine(came[1], came[2]))
        else:
            other = yield links.swap(value, hop)
            value = combine(value, other)
    return value


def paired(hops):
    return [tuple(hops[:2])] + hops[2:] if len(hops) > 1 else hops


def from_owners(links, owned, fars):
    size = links.shard
    return (
        yield [
            [lax.ppermute(own, "shard", [(i, (i + far) % size) for i in range(size)]) for own in owned] for far in fars
        ]
    )


def assembled(own, parts, me):
    parts = [part.reshape(own.shape) for part in parts]
    if len(parts) == 1:
        return join(own, parts[0], 0, me)
    whole = jnp.zeros((len(parts) + 1,) + own.shape, own.dtype)
    for far, part in enumerate([own] + parts):
        whole = lax.dynamic_update_slice_in_dim(whole, part[None], (me - far) % (len(parts) + 1), 0)
    return whole.reshape((-1,) + own.shape[1:])


def half_of(value, bit):
    size = value.shape[-1] // 2
    return lax.dynamic_slice_in_dim(value, bit * size, size, value.ndim - 1)


def local(mesh_shape, clips, visible_idx, masked_idx, loss_counts, *state):
    masters, firsts, seconds = state[:5], state[5:10], state[10:]
    seq_count, tube_count, _ = clips.shape
    seen_count = visible_idx.shape[1]
    hidden_count = masked_idx.shape[1]
    query_rows = -(-hidden_count // BLOCK) * BLOCK
    seen_rows = -(-seen_count // 16) * 16
    rep, shard = mesh_shape["rep"], mesh_shape["shard"]
    links = Links(rep, shard)
    me = lax.axis_index("shard")

    views = [split_view(master, 1, links.ways) for master in masters[:4]]
    blocks = [links.own_block(view).astype(jnp.bfloat16) for view in views]
    vec_own = masters[4].astype(jnp.bfloat16).reshape(1, -1)
    fars = range(1, shard)
    first = Steps(from_owners(links, blocks[:2] + [vec_own], fars))
    core, inner, outer, owners = links.inner[:1], links.inner[1:], links.outer, links.owners
    counts = jnp.sum(loss_counts).astype(jnp.float32).reshape(1)
    counts = Steps(over_all(links, counts, jnp.add, core + inner[:1] + owners + inner[1:] + outer))

    seen_idx = jnp.pad(visible_idx, ((0, 0), (0, seen_rows - seen_count)), constant_values=-1)
    hidden_idx = jnp.pad(masked_idx, ((0, 0), (0, query_rows - hidden_count)), constant_values=-1)
    seen_pixels = None
    for clip in range(seq_count):
        seen_pixels = pick_rows(clips, seen_idx, seen_rows, clip, "pick_seen", seen_pixels)
    seen_pixels = arrive([counts], seen_pixels)
    lows = [master.astype(jnp.bfloat16) for master in masters[:4]]
    place_seen = jnp.pad(sinusoid_at(visible_idx, D), ((0, 0), (0, seen_rows - seen_count), (0, 0)))
    place_seen, seen_pixels, lows, hidden_idx = arrive(
        [counts, first], (place_seen, seen_pixels, lows, hidden_idx)
    )
    enc_came = [block for came in first.result for block in came[:2]]
    vec_parts = [came[2] for came in first.result]
    share = Steps(links.spread(enc_came, (0, 1) * len(fars), True, False))
    vec = assembled(vec_own, vec_parts, me).reshape(1, -1).astype(jnp.float32)
    token = vec[:, DEC_VEC - DD : DEC_VEC]

    pixels = pick_rows(clips, hidden_idx, BLOCK, 0, "pick_hidden")
    pixels, hidden_idx, dec_blocks, order = arrive(
        [share], (pixels, hidden_idx, blocks[2:], (masked_idx, visible_idx))
    )
    second = Steps(from_owners(links, dec_blocks, fars))
    for clip in range(1, seq_count):
        pixels = pick_rows(clips, hidden_idx, BLOCK, clip, "pick_hidden", pixels)
    pixels, order = arrive([share, second], (pixels, order))
    near = share.result
    far_core = Steps(one_hop(links, near, core[0]))
    dec_came = [block for came in second.result for block in came]
    dec_share = Steps(links.spread(dec_came, (0, 1) * len(fars), True, True))
    place = jnp.concatenate([sinusoid_at(order[0], DD) + token, sinusoid_at(order[1], DD)], axis=1)
    place, place_seen, near = arrive([far_core, dec_share], (place, place_seen, near))
    flat = lambda whole: whole.reshape(-1, whole.shape[-1])
    halves = [(flat(mine), flat(other)) for mine, other in zip(near, far_core.result)]
    sources = [
        [lows[at]] + [half for pair_of in halves[at::2] for half in pair_of] for at in (0, 1)
    ]
    at = jnp.stack([me, bit_of(*core[0])] + [(me - far) % shard for far in fars]).astype(jnp.int32)
    (enc_h, enc_qkv, enc_mid, enc_inner, encoded, projected, tall, pair, normed_two, latent, left_most) = enc_fwd(
        at, seen_pixels.reshape(-1, PATCH), place_seen.reshape(-1, D), vec, *sources, seq_count, seen_count, shard
    )
    projected, tall = arrive([counts, dec_share], (projected, tall))
    core = core[0]
    complete(dec_share)
    left_swap = Steps(one_hop(links, (tall, pair, normed_two), core))
    dec_low_rows, u_down = [
        flat(assembled(lows[2 + k], dec_share.result[k::2], me)) for k in (0, 1)
    ]
    (u_qkv, u_out, u_up, _), w_head = dec_parts(dec_low_rows, u_down)

    projected = projected.reshape(seq_count, seen_rows, DD)[:, :seen_count]
    hidden = place.at[:, hidden_count:].add(projected)
    qkv = arrive([counts], dec_qkv(hidden, u_qkv, vec, tube_count // 2))
    mixed, log_sums = attn_fwd(qkv, DHEADS, query_rows, BLOCK)
    log_sums = arrive([counts, left_swap], log_sums)
    count_sum = complete(counts)[0][0]
    far_lefts = left_swap.result
    (middle_grad, mixed_grad, grad_row_part, grad_dec_fc2, narrow_grads, wide_grads, loss_part) = dec_post(
        loss_counts, (2.0 / (PATCH * count_sum)).reshape(1), hidden, mixed, pixels,
        u_out, u_up, u_down, w_head, vec, BLOCK,
    )
    view = functools.partial(split_view, shard=shard, ways=links.ways)
    dec_flight = Steps(links.reduce([view(grad_row_part), view(grad_dec_fc2)], (None, None), (0, 1), True))
    input_grads, before = [], [jnp.zeros((DD, 3 * DD), jnp.float32), jnp.zeros((8, DD), jnp.float32)]
    parts = [[], []]
    for clip in range(seq_count):
        for pair_at in range(DHEADS // 2):
            parts[clip] += attn_bwd(qkv, mixed_grad, log_sums, DHEADS, query_rows, BLOCK, clip, pair_at)
            log_sums = arrive([dec_flight], log_sums)
        back = dec_qkv_back(
            hidden, parts[clip], middle_grad, u_qkv, vec, hidden_count, tube_count // 2, clip, before
        )
        input_grads.append(back[0])
        before = back[1:]
    grad_qkv, one_grads = before
    dec_sums = complete(dec_flight)[0]

    proj_grad = jnp.concatenate([grad[:, hidden_count:] for grad in input_grads], axis=0)
    proj_grad = jnp.pad(proj_grad, ((0, 0), (0, seen_rows - seen_count), (0, 0))).reshape(-1, DD)
    grad_proj = product_tn(latent, proj_grad)
    late = Steps(links.reduce([view(grad_qkv), view(grad_proj)], (None, None), (0, 1), True))
    proj_grad = arrive([late], proj_grad)
    dec_spread = Steps(links.spread(dec_sums, (0, 1), True))
    grad_down, grad_up, grad_wide, grad_in, enc_sums, up_sums, right_most = enc_bwd(
        at, proj_grad, enc_h, enc_qkv, enc_mid, enc_inner, encoded, vec, *sources, seq_count, seen_count, shard
    )
    grad_vectors = jnp.concatenate(
        [enc_sums[at] for at in range(6)] + [up_sums[0], enc_sums[6], one_grads[2], one_grads[0], one_grads[1]]
        + [narrow_grads[0], narrow_grads[1], narrow_grads[2], narrow_grads[3], wide_grads[0], narrow_grads[4], wide_grads[1]]
    )

    bit = bit_of(*core)
    grad_up, grad_wide, grad_in, grad_down, right_most, grad_vectors = arrive(
        [late, dec_spread], (grad_up, grad_wide, grad_in, grad_down, right_most, grad_vectors)
    )
    shape_right = lambda b: (
        half_of(grad_up, b)[None],
        jnp.concatenate([half_of(grad_wide[:, : 3 * D], b), half_of(grad_wide[:, 3 * D :], b)], axis=1)[None],
        jnp.stack([half_of(grad_in, b), half_of(grad_down, b)]),
    )
    right_swap = Steps(one_hop(links, shape_right(1 - bit), core))
    rights = arrive([right_swap], shape_right(bit))
    norms = jnp.sqrt(left_most[:5, 0] * right_most[:5, 0])
    bounds = jnp.stack([norms[4], jnp.maximum(norms[2], norms[3]), jnp.maximum(norms[0], norms[1])])
    size = grad_vectors.shape[0]
    is_sum = lax.broadcasted_iota(jnp.int32, (1, size + 128), 1) < size + 1
    message = jnp.concatenate([grad_vectors, loss_part[0], bounds, jnp.zeros(124, jnp.float32)]).reshape(1, -1)
    hops = [core] + inner[:1] + owners + paired(inner[1:] + outer)
    vector_flight = Steps(over_all(links, message, lambda x, y: jnp.where(is_sum, x + y, jnp.maximum(x, y)), hops))
    rights = arrive([vector_flight], rights)
    far_rights = right_swap.result
    wide_cols, tall_rows = 2 * D, PATCH + FF
    zero = lambda i, j: (0, 0, i)
    hops = [vector_flight, late, dec_spread]
    sum_up = pair_product(
        (normed_two[None], far_lefts[2][None]), (rights[0], far_rights[0]), D, wide_cols, D, D // 2,
        zero, lambda i, j: (0, 0, j), "grad_up",
    )
    sum_up, rights = arrive(hops, (sum_up, rights))
    sum_wide = pair_product(
        (pair, far_lefts[1]), (rights[1], far_rights[1]), D, wide_cols, D, D // 2,
        lambda i, j: (j // 3, 0, i), lambda i, j: (0, 0, j), "grad_wide",
    )
    sum_wide, rights = arrive(hops, (sum_wide, rights))
    sum_tall = pair_product(
        (tall[None], far_lefts[0][None]), (rights[2], far_rights[2]), tall_rows, D // 2, D, D // 2,
        zero, lambda i, j: (jnp.minimum(i // 2, 1), 0, j), "grad_tall",
    )
    sum_up, sum_wide, sum_tall = arrive(hops, (sum_up, sum_wide, sum_tall))
    totals = complete(*hops)[0]
    vector_sum, loss_sum = totals[0, :size], totals[0, size]
    bounds = totals[0, size + 1 : size + 4] * (2.0 * rep * shard)
    scales = list(jnp.exp2(jnp.floor(15.0 - jnp.log2(jnp.maximum(bounds, 1e-30)))))
    slim = functools.partial(split_view, shard=shard, ways=links.ways - 1)
    enc_flight = Steps(links.reduce([slim(sum_up), slim(sum_wide), slim(sum_tall)], scales, (0, 1, 2), False))
    late_sums = late.result
    late_spread = Steps(links.spread(late_sums, (0, 1), True))
    while enc_flight.result is None:
        arrive([enc_flight, late_spread])
    complete(late_spread)
    enc_parts_sum = enc_flight.result

    lowered = [(part * scale).astype(jnp.float16) for part, scale in zip(enc_parts_sum, scales)]
    enc_spread = Steps(links.spread(lowered, (0, 0, 1), False))
    squares = jnp.float32(0.0)
    for part in enc_parts_sum + dec_sums + late_sums:
        squares = squares + jnp.sum(part * part)
    norm = Steps(over_all(links, squares.reshape(1), jnp.add, [core] + owners + paired(inner)))
    for _ in owners:
        arrive([norm])
    arrive([norm, enc_spread])
    everyone = complete(norm)[0]
    loss = loss_sum / count_sum
    grad_norm = jnp.sqrt(everyone[0] + jnp.sum(vector_sum * vector_sum))
    factor = jnp.minimum(jnp.float32(1.0), lax.rsqrt(count_sum) / grad_norm)

    flat_piece = lambda piece: piece.reshape(-1, piece.shape[-1])
    dec_rows_sum, dec_fc2_sum, dec_qkv_sum, proj_sum = [
        flat_piece(piece) for piece in dec_spread.result + late_spread.result
    ]
    own_vectors = lax.dynamic_slice_in_dim(vector_sum, me * masters[4].shape[0], masters[4].shape[0])
    updates = {}
    for index, gradient in (
        (2, jnp.concatenate([dec_qkv_sum, dec_rows_sum], axis=1)), (3, dec_fc2_sum), (4, own_vectors),
    ):
        updates[index] = adam_update(masters[index], firsts[index], seconds[index], gradient * factor)
    updates = arrive([enc_spread], updates)
    halves = [flat_piece(piece) for piece in complete(enc_spread)[0]]
    other = [links.swap(half, core) for half in halves]

    def sided(mine, yours):
        return jnp.where(bit == 0, jnp.concatenate([mine, yours], 1), jnp.concatenate([yours, mine], 1))

    wide_parts = []
    for at, (lo, hi) in enumerate(((0, 3 * D // 2), (3 * D // 2, 2 * D))):
        wide_parts.append(sided(halves[1][:, lo:hi], other[1][:, lo:hi]).astype(jnp.float32) * (1.0 / scales[1]))
    grads = [
        jnp.concatenate(
            wide_parts + [sided(halves[0], other[0]).astype(jnp.float32) * (1.0 / scales[0]), proj_sum], axis=1
        ),
        sided(halves[2], other[2]).astype(jnp.float32) * (1.0 / scales[2]),
    ]
    for index in (0, 1):
        updates[index] = adam_update(masters[index], firsts[index], seconds[index], grads[index] * factor)
    new_w, new_m, new_v = [[updates[index][kind] for index in range(5)] for kind in range(3)]
    return (loss, grad_norm, *new_w, *new_m, *new_v, *[w.astype(jnp.bfloat16) for w in new_w])


def solution(mesh):
    both, one = ("rep", "shard"), "shard"
    held = (P(one, None), P(one, None), P(one, None), P(one, None), P(one))
    in_specs = (P(both, None, None), P(both, None), P(both, None), P(both)) + held * 3
    out_specs = (P(), P()) + held * 4
    return jax.shard_map(
        functools.partial(local, dict(mesh.shape)),
        mesh=mesh, in_specs=in_specs, out_specs=out_specs, check_vma=False,
    )
```

```python
import functools
import jax
import jax.numpy as jnp
from jax import lax
from jax.experimental import pallas as pl
from jax.experimental.pallas import tpu as pltpu
from jax.sharding import PartitionSpec as P

D = 768
HEADS = 12
FF = 3072
DD = 384
DHEADS = 6
DFF = 1536
PATCH = 1536


beta_one = 0.9
beta_two = 0.95
bias_fix_one = 1.0 - 0.9**10
bias_fix_two = 1.0 - 0.95**10
learn_rate = 0.02
decay_rate = 0.05
adam_eps = 1e-12
norm_eps = 1e-06


def product_of(left, right):
    return jnp.dot(left, right, preferred_element_type=jnp.float32)


def product_tn(left, right):
    return jnp.dot(left.T, right, preferred_element_type=jnp.float32)


f32, bf16 = jnp.float32, jnp.bfloat16
LOG2E = 1.4426950408889634
NT = (((1,), (1,)), ((), ()))
NN = (((1,), (0,)), ((), ()))
TN = (((0,), (0,)), ((), ()))
def dot(a, b, dims): return lax.dot_general(a, b, dims, preferred_element_type=f32)

def cost(micros, moved=0):
    return pl.CostEstimate(flops=int(micros * 1.1e9), transcendentals=0, bytes_accessed=moved)

def fwd_body(scale, q_ref, k_ref, v_ref, o_ref, lse_ref):
    q = q_ref[0]; k = k_ref[0]; v = v_ref[0]
    lane = lax.broadcasted_iota(jnp.int32, (1, 128), 1)
    outs = []
    for h in range(2):
        own = (lane < 64) if h == 0 else (lane >= 64)
        qh = jnp.where(own, q, jnp.zeros_like(q))
        s = dot(k, qh, NT)
        peak = jnp.max(s, axis=0, keepdims=True)
        e = jnp.exp2((s - peak) * (scale * LOG2E))
        tot = jnp.sum(e, axis=0, keepdims=True)
        p = (e * (1.0 / tot)).astype(bf16)
        outs.append(dot(p, v, TN))
        lse_ref[0, 0, h:h+1, :] = peak * (scale * LOG2E) + jnp.log2(tot)
    o_ref[0] = jnp.where(lane < 64, outs[0], outs[1]).astype(bf16)

def attn_fwd(qkv, heads, rows, bq):
    clips, keys, w3 = qkv.shape
    pairs = heads // 2
    nb = rows // bq
    body = functools.partial(fwd_body, 64 ** -0.5)
    return pl.pallas_call(
        body, grid=(clips, pairs, nb),
        in_specs=[pl.BlockSpec((1, bq, 128), lambda c, p, i: (c, i, p)),
                  pl.BlockSpec((1, keys, 128), lambda c, p, i: (c, 0, pairs + p)),
                  pl.BlockSpec((1, keys, 128), lambda c, p, i: (c, 0, 2 * pairs + p))],
        out_specs=[pl.BlockSpec((1, bq, 128), lambda c, p, i: (c, i, p)),
                   pl.BlockSpec((1, 1, 2, bq), lambda c, p, i: (c * pairs + p, i, 0, 0))],
        out_shape=[jax.ShapeDtypeStruct((clips, rows, w3 // 3), bf16),
                   jax.ShapeDtypeStruct((clips * pairs, nb, 2, bq), f32)],
        compiler_params=pltpu.CompilerParams(vmem_limit_bytes=60 << 20), name="dec_attend_forward", cost_estimate=cost(65),
    )(qkv, qkv, qkv)

def bwd_body(scale, nb, mode, q_ref, k_ref, v_ref, do_ref, lse_ref, dq_ref, dk_ref, dv_ref, dk_acc, dv_acc, kt_ref):
    i = pl.program_id(2)
    q = q_ref[0]; k = k_ref[0]; v = v_ref[0]; do = do_ref[0]
    lane = lax.broadcasted_iota(jnp.int32, (1, 128), 1)
    if mode == 1:
        @pl.when(i == 0)
        def _(): kt_ref[...] = k.T
    dk = dv = None
    dqs = []
    for h in range(2):
        own = (lane < 64) if h == 0 else (lane >= 64)
        qh = jnp.where(own, q, jnp.zeros_like(q))
        doh = jnp.where(own, do, jnp.zeros_like(do))
        s = dot(k, qh, NT)
        dp = dot(v, doh, NT)
        p = jnp.exp2(s * (scale * LOG2E) - lse_ref[0, 0, h:h+1, :])
        pd = p * dp
        delta = jnp.sum(pd, axis=0, keepdims=True)
        ds = (p * (dp - delta)).astype(bf16)
        a = dot(p.astype(bf16), doh, NN)
        b = dot(ds, qh, NN)
        dv = a if dv is None else dv + a
        dk = b if dk is None else dk + b
        if mode == 0:
            dqs.append(dot(ds, k, TN))
        else:
            dqs.append(dot(kt_ref[h*64:(h+1)*64, :], ds, NN))
    if mode == 0:
        dq = jnp.where(lane < 64, dqs[0], dqs[1])
    else:
        dq = jnp.concatenate(dqs, axis=0).T
    bq = q.shape[0]
    dq_ref[0, pl.ds(pl.multiple_of(i * bq, bq), bq), :] = (dq * scale).astype(bf16)
    @pl.when(i == nb - 1)
    def _():
        keys = k.shape[0]
        if nb * bq < keys:
            dq_ref[0, nb * bq:keys, :] = jnp.zeros((keys - nb * bq, 128), bf16)
    @pl.when(i == 0)
    def _():
        dk_acc[...] = dk; dv_acc[...] = dv
    @pl.when(i > 0)
    def _():
        dk_acc[...] += dk; dv_acc[...] += dv
    @pl.when(i == nb - 1)
    def _():
        dk_ref[0] = (dk_acc[...] * scale).astype(bf16)
        dv_ref[0] = dv_acc[...].astype(bf16)

def attn_bwd(qkv, do, lse, heads, rows, bq, clip, pair):
    clips, keys, w3 = qkv.shape
    pairs = heads // 2
    nb = rows // bq
    return pl.pallas_call(
        functools.partial(bwd_body, 64 ** -0.5, nb, 0), grid=(1, 1, nb),
        in_specs=[pl.BlockSpec((1, bq, 128), lambda c, p, i: (clip, i, pair)),
                  pl.BlockSpec((1, keys, 128), lambda c, p, i: (clip, 0, pairs + pair)),
                  pl.BlockSpec((1, keys, 128), lambda c, p, i: (clip, 0, 2 * pairs + pair)),
                  pl.BlockSpec((1, bq, 128), lambda c, p, i: (clip, i, pair)),
                  pl.BlockSpec((1, 1, 2, bq), lambda c, p, i: (clip * pairs + pair, i, 0, 0))],
        out_specs=[pl.BlockSpec((1, keys, 128), lambda c, p, i: (0, 0, 0))] * 3,
        out_shape=[jax.ShapeDtypeStruct((1, keys, 128), bf16)] * 3,
        scratch_shapes=[pltpu.VMEM((keys, 128), f32), pltpu.VMEM((keys, 128), f32), pltpu.VMEM((128, keys), bf16)],
        compiler_params=pltpu.CompilerParams(vmem_limit_bytes=60 << 20), name=f"dec_attend_backward_{clip}_{pair}",
        cost_estimate=cost(17),
    )(qkv, qkv, qkv, do, lse)
DEC_VEC = 6 * D + FF + D + DD

def ln(x):
    c = x - jnp.mean(x, axis=1, keepdims=True)
    inv = lax.rsqrt(jnp.mean(c * c, axis=1, keepdims=True) + norm_eps)
    return c * inv, inv

def ln_back(up, scaled, inv, gain):
    w = up * gain
    return inv * (w - jnp.mean(w, axis=1, keepdims=True) - scaled * jnp.mean(w * scaled, axis=1, keepdims=True))

def col(x): return jnp.sum(x, axis=0, keepdims=True)

def gelu_parts(x):
    cdf = 0.5 * (1.0 + lax.erf(x * 0.7071067811865476))
    return x * cdf, cdf + x * jnp.exp(-0.5 * x * x) * 0.3989422804014327

def post_body(nb, rows, keys, cnt_ref, inv_ref, h_ref, o_ref, t_ref, wout_ref, wup_ref, wdown_ref, whead_ref,
              v_ref, dmid_ref, do_ref, grow_ref, gdown_ref, s384_ref, s1536_ref, loss_ref, gdown_acc):
    c = pl.program_id(0); i = pl.program_id(1)
    first = jnp.logical_and(c == 0, i == 0)
    @pl.when(first)
    def _():
        for r in (grow_ref, gdown_acc, s384_ref, s1536_ref, loss_ref):
            r[...] = jnp.zeros_like(r)
    R = rows
    h = h_ref[0]; o = o_ref[0]
    w, ff = h.shape[1], wup_ref.shape[1]
    gain2, bias2, gainf, biasf = (v_ref[:, DEC_VEC + j * DD:DEC_VEC + (j + 1) * DD] for j in range(2, 6))
    bup = v_ref[:, DEC_VEC + 6 * DD:DEC_VEC + 6 * DD + DFF]
    bdown = v_ref[:, DEC_VEC + 6 * DD + DFF:DEC_VEC + 7 * DD + DFF]
    bhead = v_ref[:, DEC_VEC + 7 * DD + DFF:]
    h1 = h + dot(o, wout_ref[...], NN)
    sc2, inv2 = ln(h1)
    m = (sc2 * gain2 + bias2).astype(bf16)
    inner = dot(m, wup_ref[...], NN) + bup
    act, slope = gelu_parts(inner)
    act = act.astype(bf16)
    out = h1 + (dot(act, wdown_ref[...], NN) + bdown)
    scf, invf = ln(out)
    fin = (scf * gainf + biasf).astype(bf16)
    pred = dot(fin, whead_ref[...], NN) + bhead
    t = t_ref[0].astype(f32)
    tc = t - jnp.mean(t, axis=1, keepdims=True)
    err = pred - tc * lax.rsqrt(jnp.mean(tc * tc, axis=1, keepdims=True) + norm_eps)
    row = lax.broadcasted_iota(jnp.int32, (R, 1), 0) + i * R
    live = (row < cnt_ref[c]).astype(f32)
    rl = jnp.mean(err * err, axis=1, keepdims=True) * live
    loss_ref[...] += jnp.sum(rl).reshape(1, 1)
    pg32 = err * (live * inv_ref[0])
    pg = pg32.astype(bf16)
    grow_ref[:, w + ff:] += dot(fin, pg, TN)
    dfin = dot(pg, whead_ref[...], NT)
    s1536_ref[1:2, :] += col(pg.astype(f32))
    s384_ref[2:3, :] += col(dfin * scf)
    s384_ref[3:4, :] += col(dfin)
    dout = ln_back(dfin, scf, invf, gainf)
    dl = dout.astype(bf16)
    gdown_acc[...] += dot(dl, act, TN)
    s384_ref[4:5, :] += col(dl.astype(f32))
    din = (dot(dl, wdown_ref[...], NT) * slope).astype(bf16)
    grow_ref[:, w:w + ff] += dot(m, din, TN)
    s1536_ref[0:1, :] += col(din.astype(f32))
    dm = dot(din, wup_ref[...], NT)
    s384_ref[0:1, :] += col(dm * sc2)
    s384_ref[1:2, :] += col(dm)
    dmid = dout + ln_back(dm, sc2, inv2, gain2)
    bl = dmid.astype(bf16)
    grow_ref[:, :w] += dot(o, bl, TN)
    do_ref[0] = dot(bl, wout_ref[...], NT).astype(bf16)
    dmid_ref[0, pl.ds(pl.multiple_of(i * R, R), R), :] = dmid
    @pl.when(i == nb - 1)
    def _():
        dmid_ref[0, nb * R:keys, :] = jnp.zeros((keys - nb * R, dmid.shape[1]), f32)
    @pl.when(jnp.logical_and(c == pl.num_programs(0) - 1, i == nb - 1))
    def _():
        gdown_ref[...] = gdown_acc[...].T

def dec_post(counts, inv, h, o, t, wout, wup, wdown, whead, vec, R):
    clips, keys, w = h.shape
    rows = o.shape[1]; nb = rows // R
    ff, px = wup.shape[1], whead.shape[1]
    full = lambda a: pl.BlockSpec(a.shape, lambda c, i: (0,) * len(a.shape))
    sm = pl.BlockSpec(memory_space=pltpu.SMEM)
    outs = [jax.ShapeDtypeStruct((clips, keys, w), f32), jax.ShapeDtypeStruct((clips, rows, w), bf16),
            jax.ShapeDtypeStruct((w, w + ff + px), f32), jax.ShapeDtypeStruct((ff, w), f32), jax.ShapeDtypeStruct((8, w), f32), jax.ShapeDtypeStruct((8, ff), f32),
            jax.ShapeDtypeStruct((1, 1), f32)]
    blk = lambda n: pl.BlockSpec((1, R, n), lambda c, i: (c, i, 0))
    return pl.pallas_call(
        functools.partial(post_body, nb, R, keys), grid=(clips, nb),
        in_specs=[sm, sm, blk(w), blk(w), blk(px), full(wout), full(wup), full(wdown), full(whead), full(vec)],
        out_specs=[pl.BlockSpec((1, keys, w), lambda c, i: (c, 0, 0)), blk(w)] + [full(x) for x in outs[2:]],
        out_shape=outs, compiler_params=pltpu.CompilerParams(vmem_limit_bytes=62 << 20), name="dec_post",
        scratch_shapes=[pltpu.VMEM((w, ff), f32)], cost_estimate=cost(67),
    )(counts, inv, h, o, t, wout, wup, wdown, whead, vec)

def qkv_body(h_ref, w_ref, v_ref, o_ref):
    s, _ = ln(h_ref[0])
    a = (s * v_ref[:, DEC_VEC:DEC_VEC + DD] + v_ref[:, DEC_VEC + DD:DEC_VEC + 2 * DD]).astype(bf16)
    o_ref[0] = dot(a, w_ref[...], NN).astype(bf16)

def dec_qkv(h, w, v, R):
    clips, keys, d = h.shape
    full = lambda a: pl.BlockSpec(a.shape, lambda c, i: (0,) * len(a.shape))
    return pl.pallas_call(qkv_body, grid=(clips, keys // R),
        in_specs=[pl.BlockSpec((1, R, d), lambda c, i: (c, i, 0)), full(w), full(v)],
        out_specs=pl.BlockSpec((1, R, w.shape[1]), lambda c, i: (c, i, 0)),
        out_shape=jax.ShapeDtypeStruct((clips, keys, w.shape[1]), bf16),
        compiler_params=pltpu.CompilerParams(vmem_limit_bytes=60 << 20), name="dec_qkv", cost_estimate=cost(9))(h, w, v)

def qkvb_body(R, masked, h_ref, dmid_ref, w_ref, v_ref, gi_ref, si_ref, *refs):
    parts, (dh_ref, g_ref, s_ref) = refs[:9], refs[9:]
    i = pl.program_id(0)
    @pl.when(i == 0)
    def _():
        g_ref[...] = gi_ref[...]; s_ref[...] = si_ref[...]
    d = h_ref.shape[2]
    s, inv = ln(h_ref[0])
    gain = v_ref[:, DEC_VEC:DEC_VEC + DD]
    a = (s * gain + v_ref[:, DEC_VEC + DD:DEC_VEC + 2 * DD]).astype(bf16)
    da = None
    for j in range(3):
        x = jnp.concatenate([parts[3 * p + j][0] for p in range(3)], axis=1)
        g_ref[:, j * d:(j + 1) * d] += dot(a, x, TN)
        y = dot(x, w_ref[:, j * d:(j + 1) * d], NT)
        da = y if da is None else da + y
    s_ref[0:1, :] += col(da * s)
    s_ref[1:2, :] += col(da)
    dh = dmid_ref[0] + ln_back(da, s, inv, gain)
    row = lax.broadcasted_iota(jnp.int32, (R, 1), 0) + i * R
    s_ref[2:3, :] += col(jnp.where(row < masked, dh, 0.0))
    dh_ref[0] = dh.astype(bf16)

def dec_qkv_back(h, parts, dmid, w, v, masked, R, clip, before):
    clips, keys, d = h.shape
    full = lambda a: pl.BlockSpec(a.shape, lambda i: (0,) * len(a.shape))
    blk = pl.BlockSpec((1, R, d), lambda i: (clip, i, 0))
    part = pl.BlockSpec((1, R, 128), lambda i: (0, i, 0))
    outs = [jax.ShapeDtypeStruct((1, keys, d), bf16), jax.ShapeDtypeStruct((d, 3 * d), f32), jax.ShapeDtypeStruct((8, d), f32)]
    return pl.pallas_call(functools.partial(qkvb_body, R, masked), grid=(keys // R,),
        in_specs=[blk, blk, full(w), full(v), full(outs[1]), full(outs[2])] + [part] * 9,
        out_specs=[pl.BlockSpec((1, R, d), lambda i: (0, i, 0)), full(outs[1]), full(outs[2])], out_shape=outs,
        compiler_params=pltpu.CompilerParams(vmem_limit_bytes=60 << 20), name=f"dec_qkv_back_{clip}",
        cost_estimate=cost(10))(h, dmid, w, v, *before, *parts)

def pick_body(idx_ref, x_ref, *refs):
    n = x_ref.shape[1]
    hot = (idx_ref[0] == lax.broadcasted_iota(jnp.int32, (1, n), 1)).astype(f32).astype(bf16)
    refs[-1][0] = dot(hot, x_ref[0], NN).astype(bf16)

def pick_rows(x, idx, R, clip, name, into=None):
    clips, n, w = x.shape
    m = idx.shape[1]
    more = [] if into is None else [into]
    return pl.pallas_call(pick_body, grid=(m // R,),
        in_specs=[pl.BlockSpec((1, R, 1), lambda i: (clip, i, 0)), pl.BlockSpec((1, n, w), lambda i: (clip, 0, 0))]
        + [pl.BlockSpec(memory_space=pl.ANY)] * len(more),
        out_specs=pl.BlockSpec((1, R, w), lambda i: (clip, i, 0)),
        out_shape=jax.ShapeDtypeStruct((clips, m, w), bf16), cost_estimate=cost(m / 140),
        input_output_aliases={2: 0} if more else {},
        compiler_params=pltpu.CompilerParams(vmem_limit_bytes=60 << 20), name=f"{name}_{clip}")(idx[:, :, None], x, *more)

QKV, OUT, UP, PROJ = slice(0, 3 * D), slice(3 * D, 4 * D), slice(4 * D, 4 * D + FF), slice(4 * D + FF, 4 * D + FF + DD)

def enc_vec(v_ref, at):
    starts = [0, D, 2 * D, 3 * D, 4 * D, 5 * D, 6 * D, 6 * D + FF]
    return v_ref[:, starts[at]:starts[at] + (FF if at == 6 else D)]

def most(x):
    x = x.astype(f32)
    return jnp.max(jnp.sum(x * x, axis=0, keepdims=True))

def enc_scores(qkv_ref, rows, p, h, seen):
    lane = lax.broadcasted_iota(jnp.int32, (1, 128), 1)
    own = (lane < 64) if h == 0 else (lane >= 64)
    q = qkv_ref[rows, p * 128:(p + 1) * 128]
    k = qkv_ref[rows, D + p * 128:D + (p + 1) * 128]
    v = qkv_ref[rows, 2 * D + p * 128:2 * D + (p + 1) * 128]
    qh = jnp.where(own, q, jnp.zeros_like(q))
    s = dot(qh, k, NT)
    s = jnp.where(lax.broadcasted_iota(jnp.int32, (1, s.shape[1]), 1) < seen, s, -3e38)
    peak = jnp.max(s, axis=1, keepdims=True)
    e = jnp.exp2((s - peak) * (0.125 * LOG2E))
    return q, k, v, qh, own, e * (1.0 / jnp.sum(e, axis=1, keepdims=True))

def fetches(at_ref, sources, whole, sems):
    rows = sources[0].shape[0]
    copies = [(sources[0], at_ref[0] * rows)]
    for far in range((len(sources) - 1) // 2):
        for side in range(2):
            start = at_ref[2 + far] * rows + (at_ref[1] if side == 0 else 1 - at_ref[1]) * (rows // 2)
            copies.append((sources[1 + 2 * far + side], start))
    return [
        pltpu.make_async_copy(source, whole.at[pl.ds(pl.multiple_of(start, 16), source.shape[0])], sems.at[k])
        for k, (source, start) in enumerate(copies)
    ]

def enc_fwd_body(clips, seen, count, at_ref, x_ref, pos_ref, v_ref, *refs):
    row_sources, col_sources = refs[:count], refs[count:2 * count]
    (h_ref, qkv_ref, h1_ref, inner_ref, enc_ref, proj_ref, tall_ref, pair_ref, m_ref, lat_ref, most_ref,
     wr_ref, wc_ref, row_sems, col_sems) = refs[2 * count:]
    col_copies = fetches(at_ref, col_sources, wc_ref, col_sems)
    row_copies = fetches(at_ref, row_sources, wr_ref, row_sems)
    for copy in col_copies + row_copies: copy.start()
    for copy in col_copies: copy.wait()
    enc_fwd_math(clips, seen, row_copies, x_ref, pos_ref, wr_ref, wc_ref, v_ref, h_ref, qkv_ref, h1_ref, inner_ref,
                 enc_ref, proj_ref, tall_ref, pair_ref, m_ref, lat_ref, most_ref)

def enc_fwd_math(clips, seen, row_copies, x_ref, pos_ref, wr_ref, wc_ref, v_ref,
                 h_ref, qkv_ref, h1_ref, inner_ref, enc_ref, proj_ref, tall_ref, pair_ref, m_ref, lat_ref, most_ref):
    x = x_ref[...]
    h = dot(x, wc_ref[:PATCH], NN) + pos_ref[...]
    h_ref[...] = h
    s1, _ = ln(h)
    a = (s1 * enc_vec(v_ref, 0) + enc_vec(v_ref, 1)).astype(bf16)
    pair_ref[0] = a
    for copy in row_copies: copy.wait()
    qkv_ref[...] = dot(a, wr_ref[:, QKV], NN).astype(bf16)
    n = h.shape[0] // clips
    for c in range(clips):
        rows = slice(c * n, (c + 1) * n)
        for p in range(HEADS // 2):
            outs = []
            for hd in range(2):
                q, k, v, qh, own, prob = enc_scores(qkv_ref, rows, p, hd, seen)
                outs.append(dot(prob.astype(bf16), v, NN))
            lane = lax.broadcasted_iota(jnp.int32, (1, 128), 1)
            pair_ref[1, rows, p * 128:(p + 1) * 128] = jnp.where(lane < 64, outs[0], outs[1]).astype(bf16)
    o = pair_ref[1]
    h1 = h + dot(o, wr_ref[:, OUT], NN)
    h1_ref[...] = h1
    s2, _ = ln(h1)
    m = (s2 * enc_vec(v_ref, 2) + enc_vec(v_ref, 3)).astype(bf16)
    m_ref[...] = m
    inner = dot(m, wr_ref[:, UP], NN) + enc_vec(v_ref, 6)
    inner_ref[...] = inner
    act = gelu_parts(inner)[0].astype(bf16)
    out = h1 + (dot(act, wc_ref[PATCH:], NN) + enc_vec(v_ref, 7))
    enc_ref[...] = out
    sf, _ = ln(out)
    lat = (sf * enc_vec(v_ref, 4) + enc_vec(v_ref, 5)).astype(bf16)
    lat_ref[...] = lat
    proj_ref[...] = dot(lat, wr_ref[:, PROJ], NN)
    tall_ref[:, :PATCH] = x
    tall_ref[:, PATCH:] = act
    for at, y in enumerate((x, act, a, o, m)):
        most_ref[at:at + 1, :] = jnp.broadcast_to(most(y).reshape(1, 1), (1, 128))

def whole(shape): return pl.BlockSpec(shape, lambda: (0,) * len(shape))

def weight_scratch(row_sources, col_sources, shard):
    scratch = [pltpu.VMEM((shard * s[0].shape[0], s[0].shape[1]), bf16) for s in (row_sources, col_sources)]
    return scratch + [pltpu.SemaphoreType.DMA((len(row_sources),))] * 2

def enc_fwd(at, x, pos, vec, row_sources, col_sources, clips, seen, shard):
    n = x.shape[0]
    shapes = [((n, D), f32), ((n, 3 * D), bf16), ((n, D), f32), ((n, FF), f32), ((n, D), f32), ((n, DD), f32),
              ((n, PATCH + FF), bf16), ((2, n, D), bf16), ((n, D), bf16), ((n, D), bf16), ((8, 128), f32)]
    count = len(row_sources)
    return pl.pallas_call(functools.partial(enc_fwd_body, clips, seen, count),
        in_specs=[pl.BlockSpec(memory_space=pltpu.SMEM)] + [whole(a.shape) for a in (x, pos, vec)]
        + [pl.BlockSpec(memory_space=pl.ANY)] * (2 * count),
        out_specs=[whole(s) for s, _ in shapes], out_shape=[jax.ShapeDtypeStruct(s, d) for s, d in shapes],
        scratch_shapes=weight_scratch(row_sources, col_sources, shard),
        compiler_params=pltpu.CompilerParams(vmem_limit_bytes=62 << 20), name="enc_forward", cost_estimate=cost(19),
    )(at, x, pos, vec, *row_sources, *col_sources)

def enc_bwd_body(clips, seen, count, at_ref, dp_ref, h_ref, qkv_ref, h1_ref, inner_ref, enc_ref, v_ref, *refs):
    row_sources, col_sources = refs[:count], refs[count:2 * count]
    (gdown_ref, gup_ref, gwide_ref, gin_ref, s_ref, sup_ref, most_ref, wr_ref, wc_ref, row_sems, col_sems) = refs[2 * count:]
    row_copies = fetches(at_ref, row_sources, wr_ref, row_sems)
    col_copies = fetches(at_ref, col_sources, wc_ref, col_sems)
    for copy in row_copies + col_copies: copy.start()
    for copy in row_copies: copy.wait()
    sf, invf = ln(enc_ref[...])
    up = dot(dp_ref[...], wr_ref[:, PROJ], NT)
    s_ref[4:5, :] = col(up * sf); s_ref[5:6, :] = col(up)
    dout = ln_back(up, sf, invf, enc_vec(v_ref, 4))
    dl = dout.astype(bf16)
    gdown_ref[...] = dl
    s_ref[6:7, :] = col(dl.astype(f32))
    for copy in col_copies: copy.wait()
    din = (dot(dl, wc_ref[PATCH:], NT) * gelu_parts(inner_ref[...])[1]).astype(bf16)
    gup_ref[...] = din
    sup_ref[...] = col(din.astype(f32))
    dm = dot(din, wr_ref[:, UP], NT)
    s2, inv2 = ln(h1_ref[...])
    s_ref[2:3, :] = col(dm * s2); s_ref[3:4, :] = col(dm)
    dmid = dout + ln_back(dm, s2, inv2, enc_vec(v_ref, 2))
    bl = dmid.astype(bf16)
    gwide_ref[:, 3 * D:] = bl
    do = dot(bl, wr_ref[:, OUT], NT).astype(bf16)
    n = do.shape[0] // clips
    for c in range(clips):
        rows = slice(c * n, (c + 1) * n)
        for p in range(HEADS // 2):
            dop = do[rows, p * 128:(p + 1) * 128]
            dqs, dk, dv = [], None, None
            for hd in range(2):
                q, k, v, qh, own, prob = enc_scores(qkv_ref, rows, p, hd, seen)
                doh = jnp.where(own, dop, jnp.zeros_like(dop))
                dpr = dot(doh, v, NT)
                ds = (prob * (dpr - jnp.sum(dpr * prob, axis=1, keepdims=True))).astype(bf16)
                dqs.append(dot(ds, k, NN))
                x, y = dot(ds, qh, TN), dot(prob.astype(bf16), doh, TN)
                dk = x if dk is None else dk + x
                dv = y if dv is None else dv + y
            lane = lax.broadcasted_iota(jnp.int32, (1, 128), 1)
            dq = jnp.where(lane < 64, dqs[0], dqs[1])
            gwide_ref[rows, p * 128:(p + 1) * 128] = (dq * 0.125).astype(bf16)
            gwide_ref[rows, D + p * 128:D + (p + 1) * 128] = (dk * 0.125).astype(bf16)
            gwide_ref[rows, 2 * D + p * 128:2 * D + (p + 1) * 128] = dv.astype(bf16)
    da = dot(gwide_ref[:, :3 * D], wr_ref[:, QKV], NT)
    s1, inv1 = ln(h_ref[...])
    s_ref[0:1, :] = col(da * s1); s_ref[1:2, :] = col(da)
    s_ref[7:8, :] = jnp.zeros_like(s_ref[7:8, :])
    gin = (dmid + ln_back(da, s1, inv1, enc_vec(v_ref, 0))).astype(bf16)
    gin_ref[...] = gin
    for at, y in enumerate((gin, dl, gwide_ref[:, :3 * D], bl, din)):
        most_ref[at:at + 1, :] = jnp.broadcast_to(most(y).reshape(1, 1), (1, 128))

def enc_bwd(at, dp, h, qkv, h1, inner, enc, vec, row_sources, col_sources, clips, seen, shard):
    n = h.shape[0]
    shapes = [((n, D), bf16), ((n, FF), bf16), ((n, 4 * D), bf16), ((n, D), bf16), ((8, D), f32), ((1, FF), f32), ((8, 128), f32)]
    ins = (dp, h, qkv, h1, inner, enc, vec)
    count = len(row_sources)
    return pl.pallas_call(functools.partial(enc_bwd_body, clips, seen, count),
        in_specs=[pl.BlockSpec(memory_space=pltpu.SMEM)] + [whole(a.shape) for a in ins]
        + [pl.BlockSpec(memory_space=pl.ANY)] * (2 * count),
        out_specs=[whole(s) for s, _ in shapes], out_shape=[jax.ShapeDtypeStruct(s, d) for s, d in shapes],
        scratch_shapes=weight_scratch(row_sources, col_sources, shard),
        compiler_params=pltpu.CompilerParams(vmem_limit_bytes=62 << 20), name="enc_backward", cost_estimate=cost(27),
    )(at, *ins, *row_sources, *col_sources)

def pair_body(al_ref, bl_ref, ar_ref, br_ref, o_ref):
    o_ref[...] = dot(al_ref[0], ar_ref[0], TN) + dot(bl_ref[0], br_ref[0], TN)

def pair_product(lefts, rights, rows, cols, bm, bn, left_at, right_at, name):
    n = lefts[0].shape[1]
    ls = pl.BlockSpec((1, n, bm), lambda i, j: left_at(i, j))
    rs = pl.BlockSpec((1, n, bn), lambda i, j: right_at(i, j))
    return pl.pallas_call(pair_body, grid=(rows // bm, cols // bn), in_specs=[ls, ls, rs, rs],
        out_specs=pl.BlockSpec((bm, bn), lambda i, j: (i, j)), out_shape=jax.ShapeDtypeStruct((rows, cols), f32),
        compiler_params=pltpu.CompilerParams(vmem_limit_bytes=60 << 20), name=name,
        cost_estimate=cost(8),
    )(lefts[0], lefts[1], rights[0], rights[1])
def dec_parts(dec_low_rows, dec_low_fc2):
    mats = (
        dec_low_rows[:, : 3 * DD],
        dec_low_rows[:, 3 * DD : 4 * DD],
        dec_low_rows[:, 4 * DD : 4 * DD + DFF],
        dec_low_fc2,
    )
    return (mats, dec_low_rows[:, 4 * DD + DFF :])


def adam_update(master, moment_one, moment_two, gradient):
    new_one = beta_one * moment_one + (1.0 - beta_one) * gradient
    new_two = beta_two * moment_two + (1.0 - beta_two) * gradient * gradient
    stepped = new_one / bias_fix_one / (jnp.sqrt(new_two / bias_fix_two) + adam_eps)
    return (master - learn_rate * (stepped + decay_rate * master), new_one, new_two)


BLOCK = 720


def sinusoid_at(places, feat_width):
    column = jnp.arange(feat_width)
    expo = (2 * (column // 2)).astype(jnp.float32) / feat_width
    angles = places.astype(jnp.float32)[..., None] / jnp.power(jnp.float32(10000.0), expo)
    turns = jnp.round(angles * 0.6366197723675814)
    r = ((angles - turns * 1.5703125) - turns * 4.837512969970703125e-4) - turns * 7.54978995489188216e-8
    z = r * r
    sine = ((-1.9515295891e-4 * z + 8.3321608736e-3) * z - 1.6666654611e-1) * z * r + r
    cosine = ((2.443315711809948e-5 * z - 1.388731625493765e-3) * z + 4.166664568298827e-2) * z * z - 0.5 * z + 1.0
    quarter = turns.astype(jnp.int32) + column % 2
    value = jnp.where(quarter % 2 == 0, sine, cosine)
    return jnp.where(quarter % 4 < 2, value, -value)


def bit_of(name, hop):
    return (lax.axis_index(name) // hop) % 2


def swap(value, name, size, hop):
    return lax.ppermute(value, name, [(i, i ^ hop) for i in range(size)])


def total_everywhere(value, sizes, combine=jnp.add):
    for name, size in sizes:
        hop = 1
        while hop < size:
            value = combine(value, swap(value, name, size, hop))
            hop *= 2
    return value


def keep_and_send(value, dim, bit):
    half = value.shape[dim] // 2
    kept = lax.dynamic_slice_in_dim(value, bit * half, half, dim)
    sent = lax.dynamic_slice_in_dim(value, (1 - bit) * half, half, dim)
    return kept, sent


def join(mine, other, dim, bit):
    return jnp.where(
        bit == 0, jnp.concatenate([mine, other], axis=dim), jnp.concatenate([other, mine], axis=dim)
    )


def split_view(value, shard, ways):
    rows = value.shape[0] // shard
    return value.reshape((shard,) + (2,) * ways + (rows >> ways, value.shape[1]))


class Links:
    def __init__(self, rep, shard):
        self.rep, self.shard = rep, shard
        self.ways = min(3, rep.bit_length() - 1)
        self.inner = [("rep", 1 << k) for k in range(self.ways)]
        self.outer = [("rep", 1 << k) for k in range(self.ways, rep.bit_length() - 1)]
        self.owners = [("shard", 1 << k) for k in reversed(range(shard.bit_length() - 1))]
        self.sizes = (("rep", rep), ("shard", shard))

    def size(self, name):
        return self.rep if name == "rep" else self.shard

    def swap(self, value, hop):
        return swap(value, hop[0], self.size(hop[0]), hop[1])

    def dim(self, hop, core):
        return 0 if hop[0] == "shard" else hop[1].bit_length() - (not core)

    def reduce(self, parts, scales, turns, core):
        parts = list(parts)
        first = self.inner[:1] if core else []
        rest = self.inner[1:] + self.owners[:1]
        orders = []
        for turn in turns:
            turn = turn % len(rest)
            orders.append(first + rest[turn:] + rest[:turn] + self.owners[1:])
        for step in range(len(orders[0])):
            held, moving = [], []
            for part, scale, order in zip(parts, scales, orders):
                hop = order[step]
                kept, sent = keep_and_send(part, self.dim(hop, core), bit_of(*hop))
                if scale is not None:
                    sent = (sent * scale).astype(jnp.float16)
                held.append(kept)
                moving.append(self.swap(sent, hop))
            moving = yield moving
            for at, (kept, came) in enumerate(zip(held, moving)):
                if scales[at] is not None:
                    came = came.astype(jnp.float32) * (1.0 / scales[at])
                parts[at] = kept + came
        for hop in self.outer:
            mine = [
                part if scale is None else lax.optimization_barrier((part * scale).astype(jnp.float16))
                for part, scale in zip(parts, scales)
            ]
            other = yield [self.swap(part, hop) for part in mine]
            for at, scale in enumerate(scales):
                if scale is None:
                    parts[at] = mine[at] + other[at]
                else:
                    both = mine[at].astype(jnp.float32) + other[at].astype(jnp.float32)
                    parts[at] = both * (1.0 / scale)
        return parts

    def spread(self, pieces, turns, core, across=None):
        pieces = list(pieces)
        rest = self.inner[1:]
        orders = []
        for turn in turns:
            turn = turn % len(rest) if rest else 0
            orders.append(rest[turn:] + rest[:turn] + (self.inner[:1] if (core if across is None else across) else []))
        for step in range(len(orders[0])):
            moving = yield [self.swap(piece, order[step]) for piece, order in zip(pieces, orders)]
            pieces = [
                join(piece, came, self.dim(order[step], core), bit_of(*order[step]))
                for piece, came, order in zip(pieces, moving, orders)
            ]
        return pieces

    def own_block(self, view):
        for hop in self.inner:
            view, _ = keep_and_send(view, self.dim(hop, True), bit_of(*hop))
        return view


class Steps:
    def __init__(self, generator):
        self.generator, self.flight, self.result = generator, None, None
        self.step()

    def step(self):
        if self.result is None:
            try:
                self.flight = self.generator.send(self.flight)
            except StopIteration as end:
                self.flight, self.result = None, end.value


def arrive(steps, value=()):
    steps = [each for each in steps if each.result is None]
    value, flights = lax.optimization_barrier((value, [each.flight for each in steps]))
    for each, flight in zip(steps, flights):
        each.flight = flight
        each.step()
    return value


def complete(*steps):
    while any(each.result is None for each in steps):
        arrive(steps)
    return [each.result for each in steps]


def one_hop(links, values, hop):
    return (yield [links.swap(value, hop) for value in values])


def over_all(links, value, combine, hops):
    for hop in hops:
        if isinstance(hop[0], tuple):
            near, far = hop
            both = (near[0], near[1] ^ far[1])
            came = yield [links.swap(value, each) for each in (near, far, both)]
            value = combine(combine(value, came[0]), combine(came[1], came[2]))
        else:
            other = yield links.swap(value, hop)
            value = combine(value, other)
    return value


def over_and_back(links, parts, turns):
    blocks = yield from links.reduce(parts, (None,) * len(parts), turns, True)
    rows = yield from links.spread(blocks, turns, True)
    return blocks, rows


def paired(hops):
    return [tuple(hops[:2])] + hops[2:] if len(hops) > 1 else hops


def from_owners(links, owned, fars):
    size = links.shard
    return (
        yield [
            [lax.ppermute(own, "shard", [(i, (i + far) % size) for i in range(size)]) for own in owned] for far in fars
        ]
    )


def assembled(own, parts, me):
    parts = [part.reshape(own.shape) for part in parts]
    if len(parts) == 1:
        return join(own, parts[0], 0, me)
    whole = jnp.zeros((len(parts) + 1,) + own.shape, own.dtype)
    for far, part in enumerate([own] + parts):
        whole = lax.dynamic_update_slice_in_dim(whole, part[None], (me - far) % (len(parts) + 1), 0)
    return whole.reshape((-1,) + own.shape[1:])


def half_of(value, bit):
    size = value.shape[-1] // 2
    return lax.dynamic_slice_in_dim(value, bit * size, size, value.ndim - 1)


def local(mesh_shape, clips, visible_idx, masked_idx, loss_counts, *state):
    masters, firsts, seconds = state[:5], state[5:10], state[10:]
    seq_count, tube_count, _ = clips.shape
    seen_count = visible_idx.shape[1]
    hidden_count = masked_idx.shape[1]
    query_rows = -(-hidden_count // BLOCK) * BLOCK
    seen_rows = -(-seen_count // 16) * 16
    rep, shard = mesh_shape["rep"], mesh_shape["shard"]
    links = Links(rep, shard)
    me = lax.axis_index("shard")

    views = [split_view(master, 1, links.ways) for master in masters[:4]]
    blocks = [links.own_block(view).astype(jnp.bfloat16) for view in views]
    vec_own = masters[4].astype(jnp.bfloat16).reshape(1, -1)
    fars = range(1, shard)
    first = Steps(from_owners(links, blocks[:2] + [vec_own], fars))
    core, inner, outer, owners = links.inner[:1], links.inner[1:], links.outer, links.owners
    counts = jnp.sum(loss_counts).astype(jnp.float32).reshape(1)
    counts = Steps(over_all(links, counts, jnp.add, core + inner[:1] + owners + inner[1:] + outer))

    seen_idx = jnp.pad(visible_idx, ((0, 0), (0, seen_rows - seen_count)), constant_values=-1)
    hidden_idx = jnp.pad(masked_idx, ((0, 0), (0, query_rows - hidden_count)), constant_values=-1)
    seen_pixels = None
    for clip in range(seq_count):
        seen_pixels = pick_rows(clips, seen_idx, seen_rows, clip, "pick_seen", seen_pixels)
    seen_pixels = arrive([counts], seen_pixels)
    lows = [master.astype(jnp.bfloat16) for master in masters[:4]]
    place_seen = jnp.pad(sinusoid_at(visible_idx, D), ((0, 0), (0, seen_rows - seen_count), (0, 0)))
    place_seen, seen_pixels, lows, hidden_idx = arrive(
        [counts, first], (place_seen, seen_pixels, lows, hidden_idx)
    )
    enc_came = [block for came in first.result for block in came[:2]]
    vec_parts = [came[2] for came in first.result]
    share = Steps(links.spread(enc_came, (0, 1) * len(fars), True, False))
    vec = assembled(vec_own, vec_parts, me).reshape(1, -1).astype(jnp.float32)
    token = vec[:, DEC_VEC - DD : DEC_VEC]

    pixels = pick_rows(clips, hidden_idx, BLOCK, 0, "pick_hidden")
    pixels, hidden_idx, dec_blocks, order = arrive(
        [share], (pixels, hidden_idx, blocks[2:], (masked_idx, visible_idx))
    )
    second = Steps(from_owners(links, dec_blocks, fars))
    for clip in range(1, seq_count):
        pixels = pick_rows(clips, hidden_idx, BLOCK, clip, "pick_hidden", pixels)
    pixels, order = arrive([share, second], (pixels, order))
    near = share.result
    far_core = Steps(one_hop(links, near, core[0]))
    dec_came = [block for came in second.result for block in came]
    dec_share = Steps(links.spread(dec_came, (0, 1) * len(fars), True, True))
    place = jnp.concatenate([sinusoid_at(order[0], DD) + token, sinusoid_at(order[1], DD)], axis=1)
    place, place_seen, near = arrive([far_core, dec_share], (place, place_seen, near))
    flat = lambda whole: whole.reshape(-1, whole.shape[-1])
    halves = [(flat(mine), flat(other)) for mine, other in zip(near, far_core.result)]
    sources = [
        [lows[at]] + [half for pair_of in halves[at::2] for half in pair_of] for at in (0, 1)
    ]
    at = jnp.stack([me, bit_of(*core[0])] + [(me - far) % shard for far in fars]).astype(jnp.int32)
    (enc_h, enc_qkv, enc_mid, enc_inner, encoded, projected, tall, pair, normed_two, latent, left_most) = enc_fwd(
        at, seen_pixels.reshape(-1, PATCH), place_seen.reshape(-1, D), vec, *sources, seq_count, seen_count, shard
    )
    projected, tall = arrive([counts, dec_share], (projected, tall))
    core = core[0]
    complete(dec_share)
    left_swap = Steps(one_hop(links, (tall, pair, normed_two), core))
    dec_low_rows, u_down = [
        flat(assembled(lows[2 + k], dec_share.result[k::2], me)) for k in (0, 1)
    ]
    (u_qkv, u_out, u_up, _), w_head = dec_parts(dec_low_rows, u_down)

    projected = projected.reshape(seq_count, seen_rows, DD)[:, :seen_count]
    hidden = place.at[:, hidden_count:].add(projected)
    qkv = arrive([counts], dec_qkv(hidden, u_qkv, vec, tube_count // 2))
    mixed, log_sums = attn_fwd(qkv, DHEADS, query_rows, BLOCK)
    log_sums = arrive([counts, left_swap], log_sums)
    count_sum = complete(counts)[0][0]
    far_lefts = left_swap.result
    (middle_grad, mixed_grad, grad_row_part, grad_dec_fc2, narrow_grads, wide_grads, loss_part) = dec_post(
        loss_counts, (2.0 / (PATCH * count_sum)).reshape(1), hidden, mixed, pixels,
        u_out, u_up, u_down, w_head, vec, BLOCK,
    )
    view = functools.partial(split_view, shard=shard, ways=links.ways)
    dec_flight = Steps(over_and_back(links, [view(grad_row_part), view(grad_dec_fc2)], (0, 1)))
    input_grads, before = [], [jnp.zeros((DD, 3 * DD), jnp.float32), jnp.zeros((8, DD), jnp.float32)]
    parts = [[], []]
    for clip in range(seq_count):
        for pair_at in range(DHEADS // 2):
            parts[clip] += attn_bwd(qkv, mixed_grad, log_sums, DHEADS, query_rows, BLOCK, clip, pair_at)
            log_sums = arrive([dec_flight], log_sums)
        back = dec_qkv_back(
            hidden, parts[clip], middle_grad, u_qkv, vec, hidden_count, tube_count // 2, clip, before
        )
        input_grads.append(back[0])
        before = back[1:]
    grad_qkv, one_grads = before
    proj_grad = jnp.concatenate([grad[:, hidden_count:] for grad in input_grads], axis=0)
    proj_grad = jnp.pad(proj_grad, ((0, 0), (0, seen_rows - seen_count), (0, 0))).reshape(-1, DD)
    grad_proj = product_tn(latent, proj_grad)
    late = Steps(over_and_back(links, [view(grad_qkv), view(grad_proj)], (0, 1)))
    grad_down, grad_up, grad_wide, grad_in, enc_sums, up_sums, right_most = enc_bwd(
        at, proj_grad, enc_h, enc_qkv, enc_mid, enc_inner, encoded, vec, *sources, seq_count, seen_count, shard
    )
    grad_vectors = jnp.concatenate(
        [enc_sums[at] for at in range(6)] + [up_sums[0], enc_sums[6], one_grads[2], one_grads[0], one_grads[1]]
        + [narrow_grads[0], narrow_grads[1], narrow_grads[2], narrow_grads[3], wide_grads[0], narrow_grads[4], wide_grads[1]]
    )

    bit = bit_of(*core)
    shape_right = lambda b: (
        half_of(grad_up, b)[None],
        jnp.concatenate([half_of(grad_wide[:, : 3 * D], b), half_of(grad_wide[:, 3 * D :], b)], axis=1)[None],
        jnp.stack([half_of(grad_in, b), half_of(grad_down, b)]),
    )
    right_swap = Steps(one_hop(links, shape_right(1 - bit), core))
    rights = arrive([right_swap], shape_right(bit))
    norms = jnp.sqrt(left_most[:5, 0] * right_most[:5, 0])
    bounds = jnp.stack([norms[4], jnp.maximum(norms[2], norms[3]), jnp.maximum(norms[0], norms[1])])
    size = grad_vectors.shape[0]
    is_sum = lax.broadcasted_iota(jnp.int32, (1, size + 128), 1) < size + 1
    message = jnp.concatenate([grad_vectors, loss_part[0], bounds, jnp.zeros(124, jnp.float32)]).reshape(1, -1)
    hops = [core] + inner[:1] + owners + paired(inner[1:] + outer)
    vector_flight = Steps(over_all(links, message, lambda x, y: jnp.where(is_sum, x + y, jnp.maximum(x, y)), hops))
    rights = arrive([vector_flight], rights)
    far_rights = right_swap.result
    wide_cols, tall_rows = 2 * D, PATCH + FF
    zero = lambda i, j: (0, 0, i)
    hops = [vector_flight, late, dec_flight]
    sum_up = pair_product(
        (normed_two[None], far_lefts[2][None]), (rights[0], far_rights[0]), D, wide_cols, D, D // 2,
        zero, lambda i, j: (0, 0, j), "grad_up",
    )
    sum_up, rights = arrive(hops, (sum_up, rights))
    sum_wide = pair_product(
        (pair, far_lefts[1]), (rights[1], far_rights[1]), D, wide_cols, D, D // 2,
        lambda i, j: (j // 3, 0, i), lambda i, j: (0, 0, j), "grad_wide",
    )
    sum_wide, rights = arrive(hops, (sum_wide, rights))
    sum_tall = pair_product(
        (tall[None], far_lefts[0][None]), (rights[2], far_rights[2]), tall_rows, D // 2, D, D // 2,
        zero, lambda i, j: (jnp.minimum(i // 2, 1), 0, j), "grad_tall",
    )
    sum_up, sum_wide, sum_tall = arrive(hops, (sum_up, sum_wide, sum_tall))
    totals = complete(vector_flight)[0]
    vector_sum, loss_sum = totals[0, :size], totals[0, size]
    bounds = totals[0, size + 1 : size + 4] * (2.0 * rep * shard)
    scales = list(jnp.exp2(jnp.floor(15.0 - jnp.log2(jnp.maximum(bounds, 1e-30)))))
    slim = functools.partial(split_view, shard=shard, ways=links.ways - 1)
    enc_flight = Steps(links.reduce([slim(sum_up), slim(sum_wide), slim(sum_tall)], scales, (0, 1, 2), False))
    while enc_flight.result is None:
        arrive([enc_flight, late, dec_flight])
    (late_sums, late_rows), (dec_sums, dec_rows_all) = complete(late, dec_flight)
    enc_parts_sum = enc_flight.result

    lowered = [(part * scale).astype(jnp.float16) for part, scale in zip(enc_parts_sum, scales)]
    enc_spread = Steps(links.spread(lowered, (0, 0, 1), False))
    squares = jnp.float32(0.0)
    for part in enc_parts_sum + dec_sums + late_sums:
        squares = squares + jnp.sum(part * part)
    norm = Steps(over_all(links, squares.reshape(1), jnp.add, [core] + owners + paired(inner)))
    for _ in owners:
        arrive([norm])
    arrive([norm, enc_spread])
    everyone = complete(norm)[0]
    loss = loss_sum / count_sum
    grad_norm = jnp.sqrt(everyone[0] + jnp.sum(vector_sum * vector_sum))
    factor = jnp.minimum(jnp.float32(1.0), lax.rsqrt(count_sum) / grad_norm)

    flat_piece = lambda piece: piece.reshape(-1, piece.shape[-1])
    dec_rows_sum, dec_fc2_sum, dec_qkv_sum, proj_sum = [
        flat_piece(piece) for piece in dec_rows_all + late_rows
    ]
    own_vectors = lax.dynamic_slice_in_dim(vector_sum, me * masters[4].shape[0], masters[4].shape[0])
    def update(index, gradient):
        updated = adam_update(masters[index], firsts[index], seconds[index], gradient * factor)
        return (*updated, updated[0].astype(jnp.bfloat16))

    updates = {}
    for index, gradient in (
        (2, jnp.concatenate([dec_qkv_sum, dec_rows_sum], axis=1)), (3, dec_fc2_sum), (4, own_vectors),
    ):
        updates[index] = update(index, gradient)
    updates = arrive([enc_spread], updates)
    near16 = [flat_piece(piece) for piece in complete(enc_spread)[0]]
    tall_swap = Steps(one_hop(links, near16[2:], core))
    wide_swap = Steps(one_hop(links, near16[:2], core))

    def sided(mine, yours, k):
        both = jnp.where(bit == 0, jnp.concatenate([mine, yours], 1), jnp.concatenate([yours, mine], 1))
        return both.astype(jnp.float32) * (1.0 / scales[k])

    near16 = arrive([tall_swap], near16)
    updates[1] = update(1, sided(near16[2], tall_swap.result[0], 2))
    near16, updates[1] = arrive([wide_swap], (near16, updates[1]))
    far_up, far_wide = wide_swap.result
    cut = 3 * D // 2
    updates[0] = update(0, jnp.concatenate([
        sided(near16[1][:, :cut], far_wide[:, :cut], 1), sided(near16[1][:, cut:], far_wide[:, cut:], 1),
        sided(near16[0], far_up, 0), proj_sum,
    ], axis=1))
    new_w, new_m, new_v, lows = [[updates[index][kind] for index in range(5)] for kind in range(4)]
    return (loss, grad_norm, *new_w, *new_m, *new_v, *lows)


def solution(mesh):
    both, one = ("rep", "shard"), "shard"
    held = (P(one, None), P(one, None), P(one, None), P(one, None), P(one))
    in_specs = (P(both, None, None), P(both, None), P(both, None), P(both)) + held * 3
    out_specs = (P(), P()) + held * 4
    return jax.shard_map(
        functools.partial(local, dict(mesh.shape)),
        mesh=mesh, in_specs=in_specs, out_specs=out_specs, check_vma=False,
    )
```

```python
import functools
import jax
import jax.numpy as jnp
from jax import lax
from jax.experimental import pallas as pl
from jax.experimental.pallas import tpu as pltpu
from jax.sharding import PartitionSpec as P

D = 768
HEADS = 12
FF = 3072
DD = 384
DHEADS = 6
DFF = 1536
PATCH = 1536


beta_one = 0.9
beta_two = 0.95
bias_fix_one = 1.0 - 0.9**10
bias_fix_two = 1.0 - 0.95**10
learn_rate = 0.02
decay_rate = 0.05
adam_eps = 1e-12
norm_eps = 1e-06


def product_of(left, right):
    return jnp.dot(left, right, preferred_element_type=jnp.float32)


def product_tn(left, right):
    return jnp.dot(left.T, right, preferred_element_type=jnp.float32)


f32, bf16 = jnp.float32, jnp.bfloat16
LOG2E = 1.4426950408889634
NT = (((1,), (1,)), ((), ()))
NN = (((1,), (0,)), ((), ()))
TN = (((0,), (0,)), ((), ()))
def dot(a, b, dims): return lax.dot_general(a, b, dims, preferred_element_type=f32)

def cost(micros, moved=0):
    return pl.CostEstimate(flops=int(micros * 1.1e9), transcendentals=0, bytes_accessed=moved)

def fwd_body(scale, q_ref, k_ref, v_ref, o_ref, lse_ref):
    q = q_ref[0]; k = k_ref[0]; v = v_ref[0]
    lane = lax.broadcasted_iota(jnp.int32, (1, 128), 1)
    outs = []
    for h in range(2):
        own = (lane < 64) if h == 0 else (lane >= 64)
        qh = jnp.where(own, q, jnp.zeros_like(q))
        s = dot(k, qh, NT)
        peak = jnp.max(s, axis=0, keepdims=True)
        e = jnp.exp2((s - peak) * (scale * LOG2E))
        tot = jnp.sum(e, axis=0, keepdims=True)
        p = (e * (1.0 / tot)).astype(bf16)
        outs.append(dot(p, v, TN))
        lse_ref[0, 0, h:h+1, :] = peak * (scale * LOG2E) + jnp.log2(tot)
    o_ref[0] = jnp.where(lane < 64, outs[0], outs[1]).astype(bf16)

def attn_fwd(qkv, heads, rows, bq):
    clips, keys, w3 = qkv.shape
    pairs = heads // 2
    nb = rows // bq
    body = functools.partial(fwd_body, 64 ** -0.5)
    return pl.pallas_call(
        body, grid=(clips, pairs, nb),
        in_specs=[pl.BlockSpec((1, bq, 128), lambda c, p, i: (c, i, p)),
                  pl.BlockSpec((1, keys, 128), lambda c, p, i: (c, 0, pairs + p)),
                  pl.BlockSpec((1, keys, 128), lambda c, p, i: (c, 0, 2 * pairs + p))],
        out_specs=[pl.BlockSpec((1, bq, 128), lambda c, p, i: (c, i, p)),
                   pl.BlockSpec((1, 1, 2, bq), lambda c, p, i: (c * pairs + p, i, 0, 0))],
        out_shape=[jax.ShapeDtypeStruct((clips, rows, w3 // 3), bf16),
                   jax.ShapeDtypeStruct((clips * pairs, nb, 2, bq), f32)],
        compiler_params=pltpu.CompilerParams(vmem_limit_bytes=60 << 20), name="dec_attend_forward", cost_estimate=cost(65),
    )(qkv, qkv, qkv)

def bwd_body(scale, nb, mode, q_ref, k_ref, v_ref, do_ref, lse_ref, dq_ref, dk_ref, dv_ref, dk_acc, dv_acc, kt_ref):
    i = pl.program_id(2)
    q = q_ref[0]; k = k_ref[0]; v = v_ref[0]; do = do_ref[0]
    lane = lax.broadcasted_iota(jnp.int32, (1, 128), 1)
    if mode == 1:
        @pl.when(i == 0)
        def _(): kt_ref[...] = k.T
    dk = dv = None
    dqs = []
    for h in range(2):
        own = (lane < 64) if h == 0 else (lane >= 64)
        qh = jnp.where(own, q, jnp.zeros_like(q))
        doh = jnp.where(own, do, jnp.zeros_like(do))
        s = dot(k, qh, NT)
        dp = dot(v, doh, NT)
        p = jnp.exp2(s * (scale * LOG2E) - lse_ref[0, 0, h:h+1, :])
        pd = p * dp
        delta = jnp.sum(pd, axis=0, keepdims=True)
        ds = (p * (dp - delta)).astype(bf16)
        a = dot(p.astype(bf16), doh, NN)
        b = dot(ds, qh, NN)
        dv = a if dv is None else dv + a
        dk = b if dk is None else dk + b
        if mode == 0:
            dqs.append(dot(ds, k, TN))
        else:
            dqs.append(dot(kt_ref[h*64:(h+1)*64, :], ds, NN))
    if mode == 0:
        dq = jnp.where(lane < 64, dqs[0], dqs[1])
    else:
        dq = jnp.concatenate(dqs, axis=0).T
    bq = q.shape[0]
    dq_ref[0, pl.ds(pl.multiple_of(i * bq, bq), bq), :] = (dq * scale).astype(bf16)
    @pl.when(i == nb - 1)
    def _():
        keys = k.shape[0]
        if nb * bq < keys:
            dq_ref[0, nb * bq:keys, :] = jnp.zeros((keys - nb * bq, 128), bf16)
    @pl.when(i == 0)
    def _():
        dk_acc[...] = dk; dv_acc[...] = dv
    @pl.when(i > 0)
    def _():
        dk_acc[...] += dk; dv_acc[...] += dv
    @pl.when(i == nb - 1)
    def _():
        dk_ref[0] = (dk_acc[...] * scale).astype(bf16)
        dv_ref[0] = dv_acc[...].astype(bf16)

def attn_bwd(qkv, do, lse, heads, rows, bq, clip, pair):
    clips, keys, w3 = qkv.shape
    pairs = heads // 2
    nb = rows // bq
    return pl.pallas_call(
        functools.partial(bwd_body, 64 ** -0.5, nb, 0), grid=(1, 1, nb),
        in_specs=[pl.BlockSpec((1, bq, 128), lambda c, p, i: (clip, i, pair)),
                  pl.BlockSpec((1, keys, 128), lambda c, p, i: (clip, 0, pairs + pair)),
                  pl.BlockSpec((1, keys, 128), lambda c, p, i: (clip, 0, 2 * pairs + pair)),
                  pl.BlockSpec((1, bq, 128), lambda c, p, i: (clip, i, pair)),
                  pl.BlockSpec((1, 1, 2, bq), lambda c, p, i: (clip * pairs + pair, i, 0, 0))],
        out_specs=[pl.BlockSpec((1, keys, 128), lambda c, p, i: (0, 0, 0))] * 3,
        out_shape=[jax.ShapeDtypeStruct((1, keys, 128), bf16)] * 3,
        scratch_shapes=[pltpu.VMEM((keys, 128), f32), pltpu.VMEM((keys, 128), f32), pltpu.VMEM((128, keys), bf16)],
        compiler_params=pltpu.CompilerParams(vmem_limit_bytes=60 << 20), name=f"dec_attend_backward_{clip}_{pair}",
        cost_estimate=cost(17),
    )(qkv, qkv, qkv, do, lse)
DEC_VEC = 6 * D + FF + D + DD

def ln(x):
    c = x - jnp.mean(x, axis=1, keepdims=True)
    inv = lax.rsqrt(jnp.mean(c * c, axis=1, keepdims=True) + norm_eps)
    return c * inv, inv

def ln_back(up, scaled, inv, gain):
    w = up * gain
    return inv * (w - jnp.mean(w, axis=1, keepdims=True) - scaled * jnp.mean(w * scaled, axis=1, keepdims=True))

def col(x): return jnp.sum(x, axis=0, keepdims=True)

def gelu_parts(x):
    cdf = 0.5 * (1.0 + lax.erf(x * 0.7071067811865476))
    return x * cdf, cdf + x * jnp.exp(-0.5 * x * x) * 0.3989422804014327

def post_body(nb, rows, keys, cnt_ref, inv_ref, h_ref, o_ref, t_ref, wout_ref, wup_ref, wdown_ref, whead_ref,
              v_ref, dmid_ref, do_ref, grow_ref, gdown_ref, s384_ref, s1536_ref, loss_ref, gdown_acc):
    c = pl.program_id(0); i = pl.program_id(1)
    first = jnp.logical_and(c == 0, i == 0)
    @pl.when(first)
    def _():
        for r in (grow_ref, gdown_acc, s384_ref, s1536_ref, loss_ref):
            r[...] = jnp.zeros_like(r)
    R = rows
    h = h_ref[0]; o = o_ref[0]
    w, ff = h.shape[1], wup_ref.shape[1]
    gain2, bias2, gainf, biasf = (v_ref[:, DEC_VEC + j * DD:DEC_VEC + (j + 1) * DD] for j in range(2, 6))
    bup = v_ref[:, DEC_VEC + 6 * DD:DEC_VEC + 6 * DD + DFF]
    bdown = v_ref[:, DEC_VEC + 6 * DD + DFF:DEC_VEC + 7 * DD + DFF]
    bhead = v_ref[:, DEC_VEC + 7 * DD + DFF:]
    h1 = h + dot(o, wout_ref[...], NN)
    sc2, inv2 = ln(h1)
    m = (sc2 * gain2 + bias2).astype(bf16)
    inner = dot(m, wup_ref[...], NN) + bup
    act, slope = gelu_parts(inner)
    act = act.astype(bf16)
    out = h1 + (dot(act, wdown_ref[...], NN) + bdown)
    scf, invf = ln(out)
    fin = (scf * gainf + biasf).astype(bf16)
    pred = dot(fin, whead_ref[...], NN) + bhead
    t = t_ref[0].astype(f32)
    tc = t - jnp.mean(t, axis=1, keepdims=True)
    err = pred - tc * lax.rsqrt(jnp.mean(tc * tc, axis=1, keepdims=True) + norm_eps)
    row = lax.broadcasted_iota(jnp.int32, (R, 1), 0) + i * R
    live = (row < cnt_ref[c]).astype(f32)
    rl = jnp.mean(err * err, axis=1, keepdims=True) * live
    loss_ref[...] += jnp.sum(rl).reshape(1, 1)
    pg32 = err * (live * inv_ref[0])
    pg = pg32.astype(bf16)
    grow_ref[:, w + ff:] += dot(fin, pg, TN)
    dfin = dot(pg, whead_ref[...], NT)
    s1536_ref[1:2, :] += col(pg.astype(f32))
    s384_ref[2:3, :] += col(dfin * scf)
    s384_ref[3:4, :] += col(dfin)
    dout = ln_back(dfin, scf, invf, gainf)
    dl = dout.astype(bf16)
    gdown_acc[...] += dot(dl, act, TN)
    s384_ref[4:5, :] += col(dl.astype(f32))
    din = (dot(dl, wdown_ref[...], NT) * slope).astype(bf16)
    grow_ref[:, w:w + ff] += dot(m, din, TN)
    s1536_ref[0:1, :] += col(din.astype(f32))
    dm = dot(din, wup_ref[...], NT)
    s384_ref[0:1, :] += col(dm * sc2)
    s384_ref[1:2, :] += col(dm)
    dmid = dout + ln_back(dm, sc2, inv2, gain2)
    bl = dmid.astype(bf16)
    grow_ref[:, :w] += dot(o, bl, TN)
    do_ref[0] = dot(bl, wout_ref[...], NT).astype(bf16)
    dmid_ref[0, pl.ds(pl.multiple_of(i * R, R), R), :] = dmid
    @pl.when(i == nb - 1)
    def _():
        dmid_ref[0, nb * R:keys, :] = jnp.zeros((keys - nb * R, dmid.shape[1]), f32)
    @pl.when(jnp.logical_and(c == pl.num_programs(0) - 1, i == nb - 1))
    def _():
        gdown_ref[...] = gdown_acc[...].T

def dec_post(counts, inv, h, o, t, wout, wup, wdown, whead, vec, R):
    clips, keys, w = h.shape
    rows = o.shape[1]; nb = rows // R
    ff, px = wup.shape[1], whead.shape[1]
    full = lambda a: pl.BlockSpec(a.shape, lambda c, i: (0,) * len(a.shape))
    sm = pl.BlockSpec(memory_space=pltpu.SMEM)
    outs = [jax.ShapeDtypeStruct((clips, keys, w), f32), jax.ShapeDtypeStruct((clips, rows, w), bf16),
            jax.ShapeDtypeStruct((w, w + ff + px), f32), jax.ShapeDtypeStruct((ff, w), f32), jax.ShapeDtypeStruct((8, w), f32), jax.ShapeDtypeStruct((8, ff), f32),
            jax.ShapeDtypeStruct((1, 1), f32)]
    blk = lambda n: pl.BlockSpec((1, R, n), lambda c, i: (c, i, 0))
    return pl.pallas_call(
        functools.partial(post_body, nb, R, keys), grid=(clips, nb),
        in_specs=[sm, sm, blk(w), blk(w), blk(px), full(wout), full(wup), full(wdown), full(whead), full(vec)],
        out_specs=[pl.BlockSpec((1, keys, w), lambda c, i: (c, 0, 0)), blk(w)] + [full(x) for x in outs[2:]],
        out_shape=outs, compiler_params=pltpu.CompilerParams(vmem_limit_bytes=62 << 20), name="dec_post",
        scratch_shapes=[pltpu.VMEM((w, ff), f32)], cost_estimate=cost(67),
    )(counts, inv, h, o, t, wout, wup, wdown, whead, vec)

def qkv_body(h_ref, w_ref, v_ref, o_ref):
    s, _ = ln(h_ref[0])
    a = (s * v_ref[:, DEC_VEC:DEC_VEC + DD] + v_ref[:, DEC_VEC + DD:DEC_VEC + 2 * DD]).astype(bf16)
    o_ref[0] = dot(a, w_ref[...], NN).astype(bf16)

def dec_qkv(h, w, v, R):
    clips, keys, d = h.shape
    full = lambda a: pl.BlockSpec(a.shape, lambda c, i: (0,) * len(a.shape))
    return pl.pallas_call(qkv_body, grid=(clips, keys // R),
        in_specs=[pl.BlockSpec((1, R, d), lambda c, i: (c, i, 0)), full(w), full(v)],
        out_specs=pl.BlockSpec((1, R, w.shape[1]), lambda c, i: (c, i, 0)),
        out_shape=jax.ShapeDtypeStruct((clips, keys, w.shape[1]), bf16),
        compiler_params=pltpu.CompilerParams(vmem_limit_bytes=60 << 20), name="dec_qkv", cost_estimate=cost(9))(h, w, v)

def qkvb_body(R, masked, h_ref, dmid_ref, w_ref, v_ref, gi_ref, si_ref, *refs):
    parts, (dh_ref, g_ref, s_ref) = refs[:9], refs[9:]
    i = pl.program_id(0)
    @pl.when(i == 0)
    def _():
        g_ref[...] = gi_ref[...]; s_ref[...] = si_ref[...]
    d = h_ref.shape[2]
    s, inv = ln(h_ref[0])
    gain = v_ref[:, DEC_VEC:DEC_VEC + DD]
    a = (s * gain + v_ref[:, DEC_VEC + DD:DEC_VEC + 2 * DD]).astype(bf16)
    da = None
    for j in range(3):
        x = jnp.concatenate([parts[3 * p + j][0] for p in range(3)], axis=1)
        g_ref[:, j * d:(j + 1) * d] += dot(a, x, TN)
        y = dot(x, w_ref[:, j * d:(j + 1) * d], NT)
        da = y if da is None else da + y
    s_ref[0:1, :] += col(da * s)
    s_ref[1:2, :] += col(da)
    dh = dmid_ref[0] + ln_back(da, s, inv, gain)
    row = lax.broadcasted_iota(jnp.int32, (R, 1), 0) + i * R
    s_ref[2:3, :] += col(jnp.where(row < masked, dh, 0.0))
    dh_ref[0] = dh.astype(bf16)

def dec_qkv_back(h, parts, dmid, w, v, masked, R, clip, before):
    clips, keys, d = h.shape
    full = lambda a: pl.BlockSpec(a.shape, lambda i: (0,) * len(a.shape))
    blk = pl.BlockSpec((1, R, d), lambda i: (clip, i, 0))
    part = pl.BlockSpec((1, R, 128), lambda i: (0, i, 0))
    outs = [jax.ShapeDtypeStruct((1, keys, d), bf16), jax.ShapeDtypeStruct((d, 3 * d), f32), jax.ShapeDtypeStruct((8, d), f32)]
    return pl.pallas_call(functools.partial(qkvb_body, R, masked), grid=(keys // R,),
        in_specs=[blk, blk, full(w), full(v), full(outs[1]), full(outs[2])] + [part] * 9,
        out_specs=[pl.BlockSpec((1, R, d), lambda i: (0, i, 0)), full(outs[1]), full(outs[2])], out_shape=outs,
        compiler_params=pltpu.CompilerParams(vmem_limit_bytes=60 << 20), name=f"dec_qkv_back_{clip}",
        cost_estimate=cost(10))(h, dmid, w, v, *before, *parts)

def pick_body(idx_ref, x_ref, *refs):
    n = x_ref.shape[1]
    hot = (idx_ref[0] == lax.broadcasted_iota(jnp.int32, (1, n), 1)).astype(f32).astype(bf16)
    refs[-1][0] = dot(hot, x_ref[0], NN).astype(bf16)

def pick_rows(x, idx, R, clip, name, into=None):
    clips, n, w = x.shape
    m = idx.shape[1]
    more = [] if into is None else [into]
    return pl.pallas_call(pick_body, grid=(m // R,),
        in_specs=[pl.BlockSpec((1, R, 1), lambda i: (clip, i, 0)), pl.BlockSpec((1, n, w), lambda i: (clip, 0, 0))]
        + [pl.BlockSpec(memory_space=pl.ANY)] * len(more),
        out_specs=pl.BlockSpec((1, R, w), lambda i: (clip, i, 0)),
        out_shape=jax.ShapeDtypeStruct((clips, m, w), bf16), cost_estimate=cost(m / 140),
        input_output_aliases={2: 0} if more else {},
        compiler_params=pltpu.CompilerParams(vmem_limit_bytes=60 << 20), name=f"{name}_{clip}")(idx[:, :, None], x, *more)

QKV, OUT, UP, PROJ = slice(0, 3 * D), slice(3 * D, 4 * D), slice(4 * D, 4 * D + FF), slice(4 * D + FF, 4 * D + FF + DD)

def enc_vec(v_ref, at):
    starts = [0, D, 2 * D, 3 * D, 4 * D, 5 * D, 6 * D, 6 * D + FF]
    return v_ref[:, starts[at]:starts[at] + (FF if at == 6 else D)]

def most(x):
    x = x.astype(f32)
    return jnp.max(jnp.sum(x * x, axis=0, keepdims=True))

def enc_scores(qkv_ref, rows, p, h, seen):
    lane = lax.broadcasted_iota(jnp.int32, (1, 128), 1)
    own = (lane < 64) if h == 0 else (lane >= 64)
    q = qkv_ref[rows, p * 128:(p + 1) * 128]
    k = qkv_ref[rows, D + p * 128:D + (p + 1) * 128]
    v = qkv_ref[rows, 2 * D + p * 128:2 * D + (p + 1) * 128]
    qh = jnp.where(own, q, jnp.zeros_like(q))
    s = dot(qh, k, NT)
    s = jnp.where(lax.broadcasted_iota(jnp.int32, (1, s.shape[1]), 1) < seen, s, -3e38)
    peak = jnp.max(s, axis=1, keepdims=True)
    e = jnp.exp2((s - peak) * (0.125 * LOG2E))
    return q, k, v, qh, own, e * (1.0 / jnp.sum(e, axis=1, keepdims=True))

def fetches(at_ref, sources, whole, sems):
    rows = sources[0].shape[0]
    copies = [(sources[0], at_ref[0] * rows)]
    for far in range((len(sources) - 1) // 2):
        for side in range(2):
            start = at_ref[2 + far] * rows + (at_ref[1] if side == 0 else 1 - at_ref[1]) * (rows // 2)
            copies.append((sources[1 + 2 * far + side], start))
    return [
        pltpu.make_async_copy(source, whole.at[pl.ds(pl.multiple_of(start, 16), source.shape[0])], sems.at[k])
        for k, (source, start) in enumerate(copies)
    ]

def enc_fwd_body(clips, seen, count, at_ref, x_ref, pos_ref, v_ref, *refs):
    row_sources, col_sources = refs[:count], refs[count:2 * count]
    (h_ref, qkv_ref, h1_ref, inner_ref, enc_ref, proj_ref, tall_ref, pair_ref, m_ref, lat_ref, most_ref,
     wr_ref, wc_ref, row_sems, col_sems) = refs[2 * count:]
    col_copies = fetches(at_ref, col_sources, wc_ref, col_sems)
    row_copies = fetches(at_ref, row_sources, wr_ref, row_sems)
    for copy in col_copies + row_copies: copy.start()
    for copy in col_copies: copy.wait()
    enc_fwd_math(clips, seen, row_copies, x_ref, pos_ref, wr_ref, wc_ref, v_ref, h_ref, qkv_ref, h1_ref, inner_ref,
                 enc_ref, proj_ref, tall_ref, pair_ref, m_ref, lat_ref, most_ref)

def enc_fwd_math(clips, seen, row_copies, x_ref, pos_ref, wr_ref, wc_ref, v_ref,
                 h_ref, qkv_ref, h1_ref, inner_ref, enc_ref, proj_ref, tall_ref, pair_ref, m_ref, lat_ref, most_ref):
    x = x_ref[...]
    h = dot(x, wc_ref[:PATCH], NN) + pos_ref[...]
    h_ref[...] = h
    s1, _ = ln(h)
    a = (s1 * enc_vec(v_ref, 0) + enc_vec(v_ref, 1)).astype(bf16)
    pair_ref[0] = a
    for copy in row_copies: copy.wait()
    qkv_ref[...] = dot(a, wr_ref[:, QKV], NN).astype(bf16)
    n = h.shape[0] // clips
    for c in range(clips):
        rows = slice(c * n, (c + 1) * n)
        for p in range(HEADS // 2):
            outs = []
            for hd in range(2):
                q, k, v, qh, own, prob = enc_scores(qkv_ref, rows, p, hd, seen)
                outs.append(dot(prob.astype(bf16), v, NN))
            lane = lax.broadcasted_iota(jnp.int32, (1, 128), 1)
            pair_ref[1, rows, p * 128:(p + 1) * 128] = jnp.where(lane < 64, outs[0], outs[1]).astype(bf16)
    o = pair_ref[1]
    h1 = h + dot(o, wr_ref[:, OUT], NN)
    h1_ref[...] = h1
    s2, _ = ln(h1)
    m = (s2 * enc_vec(v_ref, 2) + enc_vec(v_ref, 3)).astype(bf16)
    m_ref[...] = m
    inner = dot(m, wr_ref[:, UP], NN) + enc_vec(v_ref, 6)
    inner_ref[...] = inner
    act = gelu_parts(inner)[0].astype(bf16)
    out = h1 + (dot(act, wc_ref[PATCH:], NN) + enc_vec(v_ref, 7))
    enc_ref[...] = out
    sf, _ = ln(out)
    lat = (sf * enc_vec(v_ref, 4) + enc_vec(v_ref, 5)).astype(bf16)
    lat_ref[...] = lat
    proj_ref[...] = dot(lat, wr_ref[:, PROJ], NN)
    tall_ref[:, :PATCH] = x
    tall_ref[:, PATCH:] = act
    for at, y in enumerate((x, act, a, o, m)):
        most_ref[at:at + 1, :] = jnp.broadcast_to(most(y).reshape(1, 1), (1, 128))

def whole(shape): return pl.BlockSpec(shape, lambda: (0,) * len(shape))

def weight_scratch(row_sources, col_sources, shard):
    scratch = [pltpu.VMEM((shard * s[0].shape[0], s[0].shape[1]), bf16) for s in (row_sources, col_sources)]
    return scratch + [pltpu.SemaphoreType.DMA((len(row_sources),))] * 2

def enc_fwd(at, x, pos, vec, row_sources, col_sources, clips, seen, shard):
    n = x.shape[0]
    shapes = [((n, D), f32), ((n, 3 * D), bf16), ((n, D), f32), ((n, FF), f32), ((n, D), f32), ((n, DD), f32),
              ((n, PATCH + FF), bf16), ((2, n, D), bf16), ((n, D), bf16), ((n, D), bf16), ((8, 128), f32)]
    count = len(row_sources)
    return pl.pallas_call(functools.partial(enc_fwd_body, clips, seen, count),
        in_specs=[pl.BlockSpec(memory_space=pltpu.SMEM)] + [whole(a.shape) for a in (x, pos, vec)]
        + [pl.BlockSpec(memory_space=pl.ANY)] * (2 * count),
        out_specs=[whole(s) for s, _ in shapes], out_shape=[jax.ShapeDtypeStruct(s, d) for s, d in shapes],
        scratch_shapes=weight_scratch(row_sources, col_sources, shard),
        compiler_params=pltpu.CompilerParams(vmem_limit_bytes=62 << 20), name="enc_forward", cost_estimate=cost(19),
    )(at, x, pos, vec, *row_sources, *col_sources)

def enc_bwd_body(clips, seen, count, at_ref, dp_ref, h_ref, qkv_ref, h1_ref, inner_ref, enc_ref, v_ref, *refs):
    row_sources, col_sources = refs[:count], refs[count:2 * count]
    (gdown_ref, gup_ref, gwide_ref, gin_ref, s_ref, sup_ref, most_ref, wr_ref, wc_ref, row_sems, col_sems) = refs[2 * count:]
    row_copies = fetches(at_ref, row_sources, wr_ref, row_sems)
    col_copies = fetches(at_ref, col_sources, wc_ref, col_sems)
    for copy in row_copies + col_copies: copy.start()
    for copy in row_copies: copy.wait()
    sf, invf = ln(enc_ref[...])
    up = dot(dp_ref[...], wr_ref[:, PROJ], NT)
    s_ref[4:5, :] = col(up * sf); s_ref[5:6, :] = col(up)
    dout = ln_back(up, sf, invf, enc_vec(v_ref, 4))
    dl = dout.astype(bf16)
    gdown_ref[...] = dl
    s_ref[6:7, :] = col(dl.astype(f32))
    for copy in col_copies: copy.wait()
    din = (dot(dl, wc_ref[PATCH:], NT) * gelu_parts(inner_ref[...])[1]).astype(bf16)
    gup_ref[...] = din
    sup_ref[...] = col(din.astype(f32))
    dm = dot(din, wr_ref[:, UP], NT)
    s2, inv2 = ln(h1_ref[...])
    s_ref[2:3, :] = col(dm * s2); s_ref[3:4, :] = col(dm)
    dmid = dout + ln_back(dm, s2, inv2, enc_vec(v_ref, 2))
    bl = dmid.astype(bf16)
    gwide_ref[:, 3 * D:] = bl
    do = dot(bl, wr_ref[:, OUT], NT).astype(bf16)
    n = do.shape[0] // clips
    for c in range(clips):
        rows = slice(c * n, (c + 1) * n)
        for p in range(HEADS // 2):
            dop = do[rows, p * 128:(p + 1) * 128]
            dqs, dk, dv = [], None, None
            for hd in range(2):
                q, k, v, qh, own, prob = enc_scores(qkv_ref, rows, p, hd, seen)
                doh = jnp.where(own, dop, jnp.zeros_like(dop))
                dpr = dot(doh, v, NT)
                ds = (prob * (dpr - jnp.sum(dpr * prob, axis=1, keepdims=True))).astype(bf16)
                dqs.append(dot(ds, k, NN))
                x, y = dot(ds, qh, TN), dot(prob.astype(bf16), doh, TN)
                dk = x if dk is None else dk + x
                dv = y if dv is None else dv + y
            lane = lax.broadcasted_iota(jnp.int32, (1, 128), 1)
            dq = jnp.where(lane < 64, dqs[0], dqs[1])
            gwide_ref[rows, p * 128:(p + 1) * 128] = (dq * 0.125).astype(bf16)
            gwide_ref[rows, D + p * 128:D + (p + 1) * 128] = (dk * 0.125).astype(bf16)
            gwide_ref[rows, 2 * D + p * 128:2 * D + (p + 1) * 128] = dv.astype(bf16)
    da = dot(gwide_ref[:, :3 * D], wr_ref[:, QKV], NT)
    s1, inv1 = ln(h_ref[...])
    s_ref[0:1, :] = col(da * s1); s_ref[1:2, :] = col(da)
    s_ref[7:8, :] = jnp.zeros_like(s_ref[7:8, :])
    gin = (dmid + ln_back(da, s1, inv1, enc_vec(v_ref, 0))).astype(bf16)
    gin_ref[...] = gin
    for at, y in enumerate((gin, dl, gwide_ref[:, :3 * D], bl, din)):
        most_ref[at:at + 1, :] = jnp.broadcast_to(most(y).reshape(1, 1), (1, 128))

def enc_bwd(at, dp, h, qkv, h1, inner, enc, vec, row_sources, col_sources, clips, seen, shard):
    n = h.shape[0]
    shapes = [((n, D), bf16), ((n, FF), bf16), ((n, 4 * D), bf16), ((n, D), bf16), ((8, D), f32), ((1, FF), f32), ((8, 128), f32)]
    ins = (dp, h, qkv, h1, inner, enc, vec)
    count = len(row_sources)
    return pl.pallas_call(functools.partial(enc_bwd_body, clips, seen, count),
        in_specs=[pl.BlockSpec(memory_space=pltpu.SMEM)] + [whole(a.shape) for a in ins]
        + [pl.BlockSpec(memory_space=pl.ANY)] * (2 * count),
        out_specs=[whole(s) for s, _ in shapes], out_shape=[jax.ShapeDtypeStruct(s, d) for s, d in shapes],
        scratch_shapes=weight_scratch(row_sources, col_sources, shard),
        compiler_params=pltpu.CompilerParams(vmem_limit_bytes=62 << 20), name="enc_backward", cost_estimate=cost(27),
    )(at, *ins, *row_sources, *col_sources)

def pair_body(al_ref, bl_ref, ar_ref, br_ref, o_ref):
    o_ref[...] = dot(al_ref[0], ar_ref[0], TN) + dot(bl_ref[0], br_ref[0], TN)

def pair_product(lefts, rights, rows, cols, bm, bn, left_at, right_at, name):
    n = lefts[0].shape[1]
    ls = pl.BlockSpec((1, n, bm), lambda i, j: left_at(i, j))
    rs = pl.BlockSpec((1, n, bn), lambda i, j: right_at(i, j))
    return pl.pallas_call(pair_body, grid=(rows // bm, cols // bn), in_specs=[ls, ls, rs, rs],
        out_specs=pl.BlockSpec((bm, bn), lambda i, j: (i, j)), out_shape=jax.ShapeDtypeStruct((rows, cols), f32),
        compiler_params=pltpu.CompilerParams(vmem_limit_bytes=60 << 20), name=name,
        cost_estimate=cost(8),
    )(lefts[0], lefts[1], rights[0], rights[1])
def dec_parts(dec_low_rows, dec_low_fc2):
    mats = (
        dec_low_rows[:, : 3 * DD],
        dec_low_rows[:, 3 * DD : 4 * DD],
        dec_low_rows[:, 4 * DD : 4 * DD + DFF],
        dec_low_fc2,
    )
    return (mats, dec_low_rows[:, 4 * DD + DFF :])


def adam_update(master, moment_one, moment_two, gradient):
    new_one = beta_one * moment_one + (1.0 - beta_one) * gradient
    new_two = beta_two * moment_two + (1.0 - beta_two) * gradient * gradient
    stepped = new_one / bias_fix_one / (jnp.sqrt(new_two / bias_fix_two) + adam_eps)
    return (master - learn_rate * (stepped + decay_rate * master), new_one, new_two)


BLOCK = 720


def sinusoid_at(places, feat_width):
    column = jnp.arange(feat_width)
    expo = (2 * (column // 2)).astype(jnp.float32) / feat_width
    angles = places.astype(jnp.float32)[..., None] / jnp.power(jnp.float32(10000.0), expo)
    turns = jnp.round(angles * 0.6366197723675814)
    r = ((angles - turns * 1.5703125) - turns * 4.837512969970703125e-4) - turns * 7.54978995489188216e-8
    z = r * r
    sine = ((-1.9515295891e-4 * z + 8.3321608736e-3) * z - 1.6666654611e-1) * z * r + r
    cosine = ((2.443315711809948e-5 * z - 1.388731625493765e-3) * z + 4.166664568298827e-2) * z * z - 0.5 * z + 1.0
    quarter = turns.astype(jnp.int32) + column % 2
    value = jnp.where(quarter % 2 == 0, sine, cosine)
    return jnp.where(quarter % 4 < 2, value, -value)


def bit_of(name, hop):
    return (lax.axis_index(name) // hop) % 2


def swap(value, name, size, hop):
    return lax.ppermute(value, name, [(i, i ^ hop) for i in range(size)])


def total_everywhere(value, sizes, combine=jnp.add):
    for name, size in sizes:
        hop = 1
        while hop < size:
            value = combine(value, swap(value, name, size, hop))
            hop *= 2
    return value


def keep_and_send(value, dim, bit):
    half = value.shape[dim] // 2
    kept = lax.dynamic_slice_in_dim(value, bit * half, half, dim)
    sent = lax.dynamic_slice_in_dim(value, (1 - bit) * half, half, dim)
    return kept, sent


def join(mine, other, dim, bit):
    return jnp.where(
        bit == 0, jnp.concatenate([mine, other], axis=dim), jnp.concatenate([other, mine], axis=dim)
    )


def split_view(value, shard, ways):
    rows = value.shape[0] // shard
    return value.reshape((shard,) + (2,) * ways + (rows >> ways, value.shape[1]))


class Links:
    def __init__(self, rep, shard):
        self.rep, self.shard = rep, shard
        self.ways = min(3, rep.bit_length() - 1)
        self.inner = [("rep", 1 << k) for k in range(self.ways)]
        self.outer = [("rep", 1 << k) for k in range(self.ways, rep.bit_length() - 1)]
        self.owners = [("shard", 1 << k) for k in reversed(range(shard.bit_length() - 1))]
        self.sizes = (("rep", rep), ("shard", shard))

    def size(self, name):
        return self.rep if name == "rep" else self.shard

    def swap(self, value, hop):
        return swap(value, hop[0], self.size(hop[0]), hop[1])

    def dim(self, hop, core):
        return 0 if hop[0] == "shard" else hop[1].bit_length() - (not core)

    def reduce(self, parts, scales, turns, core):
        parts = list(parts)
        first = self.inner[:1] if core else []
        rest = self.inner[1:] + self.owners[:1]
        orders = []
        for turn in turns:
            turn = turn % len(rest)
            orders.append(first + rest[turn:] + rest[:turn] + self.owners[1:])
        for step in range(len(orders[0])):
            held, moving = [], []
            for part, scale, order in zip(parts, scales, orders):
                hop = order[step]
                kept, sent = keep_and_send(part, self.dim(hop, core), bit_of(*hop))
                if scale is not None:
                    sent = (sent * scale).astype(jnp.float16)
                held.append(kept)
                moving.append(self.swap(sent, hop))
            moving = yield moving
            for at, (kept, came) in enumerate(zip(held, moving)):
                if scales[at] is not None:
                    came = came.astype(jnp.float32) * (1.0 / scales[at])
                parts[at] = kept + came
        for hop in self.outer:
            mine = [
                part if scale is None else lax.optimization_barrier((part * scale).astype(jnp.float16))
                for part, scale in zip(parts, scales)
            ]
            other = yield [self.swap(part, hop) for part in mine]
            for at, scale in enumerate(scales):
                if scale is None:
                    parts[at] = mine[at] + other[at]
                else:
                    both = mine[at].astype(jnp.float32) + other[at].astype(jnp.float32)
                    parts[at] = both * (1.0 / scale)
        return parts

    def spread(self, pieces, turns, core, across=None):
        pieces = list(pieces)
        rest = self.inner[1:]
        orders = []
        for turn in turns:
            turn = turn % len(rest) if rest else 0
            orders.append(rest[turn:] + rest[:turn] + (self.inner[:1] if (core if across is None else across) else []))
        for step in range(len(orders[0])):
            moving = yield [self.swap(piece, order[step]) for piece, order in zip(pieces, orders)]
            pieces = [
                join(piece, came, self.dim(order[step], core), bit_of(*order[step]))
                for piece, came, order in zip(pieces, moving, orders)
            ]
        return pieces

    def own_block(self, view):
        for hop in self.inner:
            view, _ = keep_and_send(view, self.dim(hop, True), bit_of(*hop))
        return view


class Steps:
    def __init__(self, generator):
        self.generator, self.flight, self.result = generator, None, None
        self.step()

    def step(self):
        if self.result is None:
            try:
                self.flight = self.generator.send(self.flight)
            except StopIteration as end:
                self.flight, self.result = None, end.value


def arrive(steps, value=()):
    steps = [each for each in steps if each.result is None]
    value, flights = lax.optimization_barrier((value, [each.flight for each in steps]))
    for each, flight in zip(steps, flights):
        each.flight = flight
        each.step()
    return value


def complete(*steps):
    while any(each.result is None for each in steps):
        arrive(steps)
    return [each.result for each in steps]


def one_hop(links, values, hop):
    return (yield [links.swap(value, hop) for value in values])


def over_all(links, value, combine, hops):
    for hop in hops:
        if isinstance(hop[0], tuple):
            near, far = hop
            both = (near[0], near[1] ^ far[1])
            came = yield [links.swap(value, each) for each in (near, far, both)]
            value = combine(combine(value, came[0]), combine(came[1], came[2]))
        else:
            other = yield links.swap(value, hop)
            value = combine(value, other)
    return value


def over_and_back(links, parts, turns):
    blocks = yield from links.reduce(parts, (None,) * len(parts), turns, True)
    rows = yield from links.spread(blocks, turns, True)
    return blocks, rows


def paired(hops):
    return [tuple(hops[:2])] + hops[2:] if len(hops) > 1 else hops


def from_owners(links, owned, fars):
    size = links.shard
    return (
        yield [
            [lax.ppermute(own, "shard", [(i, (i + far) % size) for i in range(size)]) for own in owned] for far in fars
        ]
    )


def assembled(own, parts, me):
    parts = [part.reshape(own.shape) for part in parts]
    if len(parts) == 1:
        return join(own, parts[0], 0, me)
    whole = jnp.zeros((len(parts) + 1,) + own.shape, own.dtype)
    for far, part in enumerate([own] + parts):
        whole = lax.dynamic_update_slice_in_dim(whole, part[None], (me - far) % (len(parts) + 1), 0)
    return whole.reshape((-1,) + own.shape[1:])


def half_of(value, bit):
    size = value.shape[-1] // 2
    return lax.dynamic_slice_in_dim(value, bit * size, size, value.ndim - 1)


def local(mesh_shape, clips, visible_idx, masked_idx, loss_counts, *state):
    masters, firsts, seconds = state[:5], state[5:10], state[10:]
    seq_count, tube_count, _ = clips.shape
    seen_count = visible_idx.shape[1]
    hidden_count = masked_idx.shape[1]
    query_rows = -(-hidden_count // BLOCK) * BLOCK
    seen_rows = -(-seen_count // 16) * 16
    rep, shard = mesh_shape["rep"], mesh_shape["shard"]
    links = Links(rep, shard)
    me = lax.axis_index("shard")

    views = [split_view(master, 1, links.ways) for master in masters[:4]]
    blocks = [links.own_block(view).astype(jnp.bfloat16) for view in views]
    vec_own = masters[4].astype(jnp.bfloat16).reshape(1, -1)
    fars = range(1, shard)
    first = Steps(from_owners(links, blocks[:2] + [vec_own], fars))
    core, inner, outer, owners = links.inner[:1], links.inner[1:], links.outer, links.owners
    counts = jnp.sum(loss_counts).astype(jnp.float32).reshape(1)
    counts = Steps(over_all(links, counts, jnp.add, core + inner[:1] + owners + inner[1:] + outer))

    seen_idx = jnp.pad(visible_idx, ((0, 0), (0, seen_rows - seen_count)), constant_values=-1)
    hidden_idx = jnp.pad(masked_idx, ((0, 0), (0, query_rows - hidden_count)), constant_values=-1)
    seen_pixels = None
    for clip in range(seq_count):
        seen_pixels = pick_rows(clips, seen_idx, seen_rows, clip, "pick_seen", seen_pixels)
    seen_pixels = arrive([counts], seen_pixels)
    lows = [master.astype(jnp.bfloat16) for master in masters[:4]]
    place_seen = jnp.pad(sinusoid_at(visible_idx, D), ((0, 0), (0, seen_rows - seen_count), (0, 0)))
    place_seen, seen_pixels, lows, hidden_idx = arrive(
        [counts, first], (place_seen, seen_pixels, lows, hidden_idx)
    )
    enc_came = [block for came in first.result for block in came[:2]]
    vec_parts = [came[2] for came in first.result]
    share = Steps(links.spread(enc_came, (0, 1) * len(fars), True, False))
    vec = assembled(vec_own, vec_parts, me).reshape(1, -1).astype(jnp.float32)
    token = vec[:, DEC_VEC - DD : DEC_VEC]

    pixels = pick_rows(clips, hidden_idx, BLOCK, 0, "pick_hidden")
    pixels, hidden_idx, dec_blocks, order = arrive(
        [share], (pixels, hidden_idx, blocks[2:], (masked_idx, visible_idx))
    )
    second = Steps(from_owners(links, dec_blocks, fars))
    for clip in range(1, seq_count):
        pixels = pick_rows(clips, hidden_idx, BLOCK, clip, "pick_hidden", pixels)
    pixels, order = arrive([share, second], (pixels, order))
    near = share.result
    far_core = Steps(one_hop(links, near, core[0]))
    dec_came = [block for came in second.result for block in came]
    dec_share = Steps(links.spread(dec_came, (0, 1) * len(fars), True, True))
    place = jnp.concatenate([sinusoid_at(order[0], DD) + token, sinusoid_at(order[1], DD)], axis=1)
    place, place_seen, near = arrive([far_core, dec_share], (place, place_seen, near))
    flat = lambda whole: whole.reshape(-1, whole.shape[-1])
    halves = [(flat(mine), flat(other)) for mine, other in zip(near, far_core.result)]
    sources = [
        [lows[at]] + [half for pair_of in halves[at::2] for half in pair_of] for at in (0, 1)
    ]
    at = jnp.stack([me, bit_of(*core[0])] + [(me - far) % shard for far in fars]).astype(jnp.int32)
    (enc_h, enc_qkv, enc_mid, enc_inner, encoded, projected, tall, pair, normed_two, latent, left_most) = enc_fwd(
        at, seen_pixels.reshape(-1, PATCH), place_seen.reshape(-1, D), vec, *sources, seq_count, seen_count, shard
    )
    projected, tall = arrive([counts, dec_share], (projected, tall))
    core = core[0]
    complete(dec_share)
    left_swap = Steps(one_hop(links, (tall, pair, normed_two), core))
    dec_low_rows, u_down = [
        flat(assembled(lows[2 + k], dec_share.result[k::2], me)) for k in (0, 1)
    ]
    (u_qkv, u_out, u_up, _), w_head = dec_parts(dec_low_rows, u_down)

    projected = projected.reshape(seq_count, seen_rows, DD)[:, :seen_count]
    hidden = place.at[:, hidden_count:].add(projected)
    qkv = arrive([counts], dec_qkv(hidden, u_qkv, vec, tube_count // 2))
    mixed, log_sums = attn_fwd(qkv, DHEADS, query_rows, BLOCK)
    log_sums = arrive([counts, left_swap], log_sums)
    count_sum = complete(counts)[0][0]
    far_lefts = left_swap.result
    (middle_grad, mixed_grad, grad_row_part, grad_dec_fc2, narrow_grads, wide_grads, loss_part) = dec_post(
        loss_counts, (2.0 / (PATCH * count_sum)).reshape(1), hidden, mixed, pixels,
        u_out, u_up, u_down, w_head, vec, BLOCK,
    )
    view = functools.partial(split_view, shard=shard, ways=links.ways)
    dec_flight = Steps(over_and_back(links, [view(grad_row_part), view(grad_dec_fc2)], (0, 1)))
    input_grads, before = [], [jnp.zeros((DD, 3 * DD), jnp.float32), jnp.zeros((8, DD), jnp.float32)]
    parts = [[], []]
    for clip in range(seq_count):
        for pair_at in range(DHEADS // 2):
            parts[clip] += attn_bwd(qkv, mixed_grad, log_sums, DHEADS, query_rows, BLOCK, clip, pair_at)
            log_sums = arrive([dec_flight], log_sums)
        back = dec_qkv_back(
            hidden, parts[clip], middle_grad, u_qkv, vec, hidden_count, tube_count // 2, clip, before
        )
        input_grads.append(back[0])
        before = back[1:]
    grad_qkv, one_grads = before
    proj_grad = jnp.concatenate([grad[:, hidden_count:] for grad in input_grads], axis=0)
    proj_grad = jnp.pad(proj_grad, ((0, 0), (0, seen_rows - seen_count), (0, 0))).reshape(-1, DD)
    grad_proj = product_tn(latent, proj_grad)
    late = Steps(over_and_back(links, [view(grad_qkv), view(grad_proj)], (0, 1)))
    grad_down, grad_up, grad_wide, grad_in, enc_sums, up_sums, right_most = enc_bwd(
        at, proj_grad, enc_h, enc_qkv, enc_mid, enc_inner, encoded, vec, *sources, seq_count, seen_count, shard
    )
    grad_vectors = jnp.concatenate(
        [enc_sums[at] for at in range(6)] + [up_sums[0], enc_sums[6], one_grads[2], one_grads[0], one_grads[1]]
        + [narrow_grads[0], narrow_grads[1], narrow_grads[2], narrow_grads[3], wide_grads[0], narrow_grads[4], wide_grads[1]]
    )

    bit = bit_of(*core)
    shape_right = lambda b: (
        half_of(grad_up, b)[None],
        jnp.concatenate([half_of(grad_wide[:, : 3 * D], b), half_of(grad_wide[:, 3 * D :], b)], axis=1)[None],
        jnp.stack([half_of(grad_in, b), half_of(grad_down, b)]),
    )
    right_swap = Steps(one_hop(links, shape_right(1 - bit), core))
    rights = arrive([right_swap], shape_right(bit))
    norms = jnp.sqrt(left_most[:5, 0] * right_most[:5, 0])
    bounds = jnp.stack([norms[4], jnp.maximum(norms[2], norms[3]), jnp.maximum(norms[0], norms[1])])
    size = grad_vectors.shape[0]
    is_sum = lax.broadcasted_iota(jnp.int32, (1, size + 128), 1) < size + 1
    message = jnp.concatenate([grad_vectors, loss_part[0], bounds, jnp.zeros(124, jnp.float32)]).reshape(1, -1)
    hops = [core] + inner[:1] + owners + paired(inner[1:] + outer)
    vector_flight = Steps(over_all(links, message, lambda x, y: jnp.where(is_sum, x + y, jnp.maximum(x, y)), hops))
    rights = arrive([vector_flight], rights)
    far_rights = right_swap.result
    wide_cols, tall_rows = 2 * D, PATCH + FF
    zero = lambda i, j: (0, 0, i)
    hops = [vector_flight, late]
    sum_up = pair_product(
        (normed_two[None], far_lefts[2][None]), (rights[0], far_rights[0]), D, wide_cols, D, D // 2,
        zero, lambda i, j: (0, 0, j), "grad_up",
    )
    sum_up, rights = arrive(hops, (sum_up, rights))
    sum_wide = pair_product(
        (pair, far_lefts[1]), (rights[1], far_rights[1]), D, wide_cols, D, D // 2,
        lambda i, j: (j // 3, 0, i), lambda i, j: (0, 0, j), "grad_wide",
    )
    sum_wide, rights = arrive(hops, (sum_wide, rights))
    sum_tall = pair_product(
        (tall[None], far_lefts[0][None]), (rights[2], far_rights[2]), tall_rows, D // 2, D, D // 2,
        zero, lambda i, j: (jnp.minimum(i // 2, 1), 0, j), "grad_tall",
    )
    sum_up, sum_wide, sum_tall = arrive(hops, (sum_up, sum_wide, sum_tall))
    totals = complete(vector_flight)[0]
    vector_sum, loss_sum = totals[0, :size], totals[0, size]
    bounds = totals[0, size + 1 : size + 4] * (2.0 * rep * shard)
    scales = list(jnp.exp2(jnp.floor(15.0 - jnp.log2(jnp.maximum(bounds, 1e-30)))))
    slim = functools.partial(split_view, shard=shard, ways=links.ways - 1)
    enc_flight = Steps(links.reduce([slim(sum_up), slim(sum_wide), slim(sum_tall)], scales, (0, 1, 2), False))
    while enc_flight.result is None:
        arrive([enc_flight, late, dec_flight])
    (late_sums, late_rows), (dec_sums, dec_rows_all) = complete(late, dec_flight)
    enc_parts_sum = enc_flight.result

    lowered = [(part * scale).astype(jnp.float16) for part, scale in zip(enc_parts_sum, scales)]
    enc_spread = Steps(links.spread(lowered, (0, 0, 1), False))
    squares = jnp.float32(0.0)
    for part in enc_parts_sum + dec_sums + late_sums:
        squares = squares + jnp.sum(part * part)
    norm = Steps(over_all(links, squares.reshape(1), jnp.add, [core] + owners + paired(inner)))
    for _ in owners:
        arrive([norm])
    arrive([norm, enc_spread])
    everyone = complete(norm)[0]
    loss = loss_sum / count_sum
    grad_norm = jnp.sqrt(everyone[0] + jnp.sum(vector_sum * vector_sum))
    factor = jnp.minimum(jnp.float32(1.0), lax.rsqrt(count_sum) / grad_norm)

    flat_piece = lambda piece: piece.reshape(-1, piece.shape[-1])
    dec_rows_sum, dec_fc2_sum, dec_qkv_sum, proj_sum = [
        flat_piece(piece) for piece in dec_rows_all + late_rows
    ]
    own_vectors = lax.dynamic_slice_in_dim(vector_sum, me * masters[4].shape[0], masters[4].shape[0])
    def update(index, gradient):
        updated = adam_update(masters[index], firsts[index], seconds[index], gradient * factor)
        return (*updated, updated[0].astype(jnp.bfloat16))

    updates = {}
    for index, gradient in (
        (2, jnp.concatenate([dec_qkv_sum, dec_rows_sum], axis=1)), (3, dec_fc2_sum), (4, own_vectors),
    ):
        updates[index] = update(index, gradient)
    updates = arrive([enc_spread], updates)
    near16 = [flat_piece(piece) for piece in complete(enc_spread)[0]]
    tall_swap = Steps(one_hop(links, near16[2:], core))
    wide_swap = Steps(one_hop(links, near16[:2], core))

    def sided(mine, yours, k):
        both = jnp.where(bit == 0, jnp.concatenate([mine, yours], 1), jnp.concatenate([yours, mine], 1))
        return both.astype(jnp.float32) * (1.0 / scales[k])

    near16 = arrive([tall_swap], near16)
    updates[1] = update(1, sided(near16[2], tall_swap.result[0], 2))
    near16, updates[1] = arrive([wide_swap], (near16, updates[1]))
    far_up, far_wide = wide_swap.result
    cut = 3 * D // 2
    updates[0] = update(0, jnp.concatenate([
        sided(near16[1][:, :cut], far_wide[:, :cut], 1), sided(near16[1][:, cut:], far_wide[:, cut:], 1),
        sided(near16[0], far_up, 0), proj_sum,
    ], axis=1))
    new_w, new_m, new_v, lows = [[updates[index][kind] for index in range(5)] for kind in range(4)]
    return (loss, grad_norm, *new_w, *new_m, *new_v, *lows)


def solution(mesh):
    both, one = ("rep", "shard"), "shard"
    held = (P(one, None), P(one, None), P(one, None), P(one, None), P(one))
    in_specs = (P(both, None, None), P(both, None), P(both, None), P(both)) + held * 3
    out_specs = (P(), P()) + held * 4
    return jax.shard_map(
        functools.partial(local, dict(mesh.shape)),
        mesh=mesh, in_specs=in_specs, out_specs=out_specs, check_vma=False,
    )
```
